32 devices in a mesh: rep: 2 (over x), fsdp: 16 (over z, y, core).
Axes of the slice: x: 2, y: 2, z: 4, core: 2. Of those that a mesh axis runs over, the one named last changes fastest.
Arguments:
- tokens: bfloat16 [4, 1024, 2048], P('rep', 'fsdp'), may hold values from -6 to 6
- segment_ids: int32 [4, 1024], P('rep', 'fsdp'), may hold values from 0 to 1, never falling along the last dimension, each value on 1 to 768 neighbouring positions
- norm_gains: bfloat16 [2048, 2], P('fsdp'), may hold values from 0.5 to 1.5
- attn_weight: bfloat16 [2048, 4608], P('fsdp'), may hold values from -0.79549513 to 0.79549513
- adapter: bfloat16 [2048, 768], P('fsdp'), may hold values from -0.125 to 0.125
- ffn_weight: bfloat16 [16384, 3, 2048], P('fsdp'), may hold values from -0.125 to 0.125
- ffn_adapter: bfloat16 [16384, 256], P('fsdp'), may hold values from -0.046875 to 0.046875
- cotangent: bfloat16 [4, 1024, 2048], P('rep', 'fsdp'), may hold values from -6 to 6
Outputs:
- block_output: bfloat16 [4, 1024, 2048], P('rep', 'fsdp')
- input_grad: bfloat16 [4, 1024, 2048], P('rep', 'fsdp')
- gains_grad: float32 [2048, 2], P('fsdp')
- attn_grad: float32 [2048, 4608], P('fsdp')
- adapter_grad: float32 [2048, 768], P('fsdp')
- ffn_grad: float32 [16384, 3, 2048], P('fsdp')
- ffn_adapter_grad: float32 [16384, 256], P('fsdp')
The draws below stay inside these ranges and needn't reach their ends.
Inputs may be any that keep to these rules, and one draw needn't show every extreme that they name: `segment_ids`: in each sequence the ids never fall and each id of 0 to 1 marks one document of 1 to 768 tokens.
All inputs are finite; a program needn't handle non-finite values.
Results may differ from the reference program's by a relative error of at most 0.019.
Values may be sent and summed in bfloat16 or wider, within the bound.
A program may use at most 448 MiB of HBM per device.

```python
import math
import jax
import jax.numpy as jnp
import numpy as np
from jax import lax

D = 2048
HEADS = 8
HD = 256
FF = 16384
RANK = 256
SEQS = 4
SEQ = 1024
DOCS = 2
DOC_MOST = 768


def draw_attn_weight(key, part):
    columns = 2 * D + 2 * HD
    column_index = jnp.arange(columns)
    factor = jnp.where(column_index < D + 2 * HD, 1.0, 6.0).astype(jnp.float32) * D ** (-0.5)
    base = jnp.clip(jax.random.normal(key, (D, columns), jnp.float32), -6.0, 6.0)
    return (base * factor[None, :]).astype(jnp.bfloat16)


def steps_of(rng, dims, shards, least, largest):
    factor_of = 1.0
    for axis_at, parts in shards:
        heights = jax.random.uniform(jax.random.fold_in(jax.random.fold_in(rng, 6), axis_at), (parts,), jnp.float32, least / len(shards), largest / len(shards))
        factor_of = factor_of * jnp.repeat(jnp.exp(heights), dims[axis_at] // parts).reshape((-1,) + (1,) * (len(dims) - 1 - axis_at))
    return factor_of


def length_profile(count, total, reach, slope):
    loads = [(1 << 20) // math.isqrt(grade ** slope) + 1 for grade in range(2, count + 1)]
    rest, given = total - reach - (count - 1), [1] * (count - 1)
    while rest > 0:
        movable = [i for i in range(count - 1) if given[i] < reach]
        mass, left = sum([loads[i] for i in movable]), rest
        for i in movable:
            addition = min(reach - given[i], max(1, left * loads[i] // mass), rest)
            given[i] = given[i] + addition
            rest = rest - addition
    return np.array([reach] + given)


def uneven_parts(key, amount, total, bound, skew):
    if amount == 2:
        one = jax.random.randint(key, (), max(1, total - bound), min(bound, total - 1) + 1)
        return jnp.stack([one, total - one])
    sizes = jnp.asarray(length_profile(amount, total, bound, skew), jnp.int32)
    twos = (amount - 1) // 2
    giver, sink = sizes[1:1 + 2 * twos:2], sizes[2:2 + 2 * twos:2]
    margin = jnp.minimum(giver - 1, bound - sink)
    moved = jax.random.randint(jax.random.fold_in(key, 1), (twos,), 0, 1 << 20) % (margin + 1)
    sizes = sizes.at[1:1 + 2 * twos:2].set(giver - moved).at[2:2 + 2 * twos:2].set(sink + moved)
    return sizes[jax.random.permutation(jax.random.fold_in(key, 2), amount)]


def noise(key, dims, width, reach, cuts=(), held_as=jnp.bfloat16):
    drawn = width * jax.random.normal(key, dims, jnp.float32)
    if cuts:
        drawn = drawn * steps_of(key, dims, cuts, -0.22, 0.18)
    return jnp.clip(drawn, -reach, reach).astype(held_as)


def setup_inputs(seed: int = 0) -> dict:
    key_of = jax.random.split(jax.random.key(seed), 9)
    return {
        "tokens": noise(key_of[0], (SEQS, SEQ, D), 1.0, 6.0, ((0, 2), (1, 16))),
        "segment_ids": jax.vmap(lambda own: jnp.searchsorted(jnp.cumsum(uneven_parts(own, DOCS, SEQ, DOC_MOST, 2)), jnp.arange(SEQ), side="right"))(jax.random.split(key_of[1], SEQS)).reshape((SEQS, SEQ)).astype(jnp.int32),
        "norm_gains": jnp.clip(1.0 + 0.1 * jax.random.normal(key_of[2], (D, 2), jnp.float32), 0.5, 1.5).astype(jnp.bfloat16),
        "attn_weight": draw_attn_weight(jax.random.fold_in(key_of[8], 71), 0),
        "adapter": noise(key_of[4], (D, 3 * RANK), D ** -0.5, 0.125, ((0, 16),)),
        "ffn_weight": noise(key_of[5], (FF, 3, D), D ** -0.5, 0.125, ((0, 16),)),
        "ffn_adapter": noise(key_of[6], (FF, RANK), FF ** -0.5, 0.046875, ((0, 16),)),
        "cotangent": noise(key_of[7], (SEQS, SEQ, D), 1.0, 6.0, ((0, 2), (1, 16))),
    }


@jax.custom_vjp
def low(v):
    return lax.optimization_barrier(v.astype(jnp.bfloat16)).astype(jnp.float32)

@jax.custom_vjp
def low_back(v):
    return v

def low_keep(v):
    return (low(v), None)

def low_pass(kept, grad):
    return (grad,)

def back_keep(v):
    return (v, None)

def back_low(kept, grad):
    return (low(grad),)
low.defvjp(low_keep, low_pass)
low_back.defvjp(back_keep, back_low)
epsilon = 1e-06

def product(left_op, right_op):
    return jnp.dot(left_op, right_op, precision=lax.Precision.HIGHEST, preferred_element_type=jnp.float32)

def rms_scale(values, gain_col):
    return values * lax.rsqrt(lax.optimization_barrier(jnp.mean(values * values, axis=-1, keepdims=True)) + epsilon) * gain_col

def angles_of(positions):
    inverse_freq = 10000.0 ** (-2.0 * jnp.arange(HD // 2, dtype=jnp.float32) / HD)
    return positions.astype(jnp.float32)[:, None] * inverse_freq[None, :]

def rotate(field_in, angles):
    half_dim = field_in.shape[-1] // 2
    cosine = jnp.cos(angles)
    sine_part = jnp.sin(angles)
    lower_half = field_in[..., :half_dim]
    upper_half = field_in[..., half_dim:]
    return jnp.concatenate([lower_half * cosine - upper_half * sine_part, upper_half * cosine + lower_half * sine_part], axis=-1)

def doc_positions(seg_whole, seg_local, offset):
    before = lax.optimization_barrier(jnp.sum((seg_whole[None, :] < seg_local[:, None]).astype(jnp.int32), axis=1))
    return offset + jnp.arange(seg_local.shape[0], dtype=jnp.int32) - before

def attention(queries, keys_low, values_low, seg_ids):
    seq_len = keys_low.shape[0]
    block_len = math.gcd(seq_len, 512)
    key_index = jnp.arange(seq_len, dtype=jnp.int32)
    score_scale = HD ** (-0.5)

    def one_block(first_row):
        query_rows = lax.dynamic_slice_in_dim(queries, first_row, block_len, 0)
        row_seg = lax.dynamic_slice_in_dim(seg_ids, first_row, block_len, 0)
        row_index = first_row + jnp.arange(block_len, dtype=jnp.int32)
        scores = jnp.einsum('qhd,kd->qhk', query_rows, keys_low, precision=lax.Precision.HIGHEST) * score_scale
        allowed = (row_seg[:, None] == seg_ids[None, :]) & (key_index[None, :] <= row_index[:, None])
        scores = low_back(jnp.where(allowed[:, None, :], scores, -1e+30))
        top_score = lax.optimization_barrier(jnp.max(scores, axis=-1, keepdims=True))
        exp_scores = jnp.exp(scores - top_score)
        weights = low(exp_scores / lax.optimization_barrier(jnp.sum(exp_scores, axis=-1, keepdims=True)))
        return jnp.einsum('qhk,kd->qhd', weights, values_low, precision=lax.Precision.HIGHEST)
    starts = jnp.arange(seq_len // block_len, dtype=jnp.int32) * block_len
    blocks = lax.map(jax.checkpoint(one_block), starts)
    return blocks.reshape(seq_len, queries.shape[1] * queries.shape[2])

def sequence_forward(hidden_in, seg_ids, gain_cols, attn_w, adapt_w, ffn_w, ffn_low):
    q_width = HEADS * HD
    seq_len = hidden_in.shape[0]
    normed = low(rms_scale(hidden_in, gain_cols[:, 0]))
    projected = product(normed, attn_w[:, :q_width + 2 * HD])
    query_low = low(low_back(product(normed, adapt_w[:, :RANK])))
    query_pre = projected[:, :q_width] + product(query_low, adapt_w[:, RANK:2 * RANK].T)
    angles = angles_of(doc_positions(seg_ids, seg_ids, 0))
    queries = low(rotate(low_back(query_pre).reshape(seq_len, HEADS, HD), angles[:, None, :]))
    keys_low = low(rotate(low_back(projected[:, q_width:q_width + HD]), angles))
    values_low = low(low_back(projected[:, q_width + HD:]))
    context = low(low_back(attention(queries, keys_low, values_low, seg_ids)))
    mixed_sum = hidden_in + low_back(product(context, attn_w[:, q_width + 2 * HD:].T))
    normed_two = low(rms_scale(mixed_sum, gain_cols[:, 1]))
    gate_pre = low_back(product(normed_two, ffn_w[:, 0, :].T))
    up_pre = low_back(product(normed_two, ffn_w[:, 1, :].T))
    hidden_act = low(jax.nn.gelu(gate_pre, approximate=True) * up_pre)
    down_low = low(low_back(product(hidden_act, ffn_low)))
    return mixed_sum + product(hidden_act, ffn_w[:, 2, :]) + product(down_low, adapt_w[:, 2 * RANK:].T)

def reference(tokens, segment_ids, norm_gains, attn_weight, adapter, ffn_weight, ffn_adapter, cotangent):

    def forward(hidden_all, gain_cols, attn_w, adapt_w, ffn_w, ffn_low):

        def one_seq(carried, seq_pair):
            return (carried, sequence_forward(seq_pair[0], seq_pair[1], gain_cols, attn_w, adapt_w, ffn_w, ffn_low))
        _, outputs = lax.scan(one_seq, jnp.zeros((), jnp.float32), (hidden_all, segment_ids))
        return outputs
    inputs = (tokens.astype(jnp.float32), norm_gains.astype(jnp.float32), attn_weight.astype(jnp.float32), adapter.astype(jnp.float32), ffn_weight.astype(jnp.float32), ffn_adapter.astype(jnp.float32))
    result, pullback = jax.vjp(forward, *inputs)
    gradients = pullback(cotangent.astype(jnp.float32))
    return (result.astype(jnp.bfloat16), gradients[0].astype(jnp.bfloat16), gradients[1], gradients[2], gradients[3], gradients[4], gradients[5])
```

```python
import jax
import jax.numpy as jnp
from jax import lax
from jax.sharding import PartitionSpec as P

HEADS = 8
HD = 256
RANK = 256
CHUNKS = 4


epsilon = 1e-06


def rms_scale(values, gain_col):
    return (
        values * lax.rsqrt(jnp.mean(values * values, axis=-1, keepdims=True) + epsilon) * gain_col
    )


def angles_of(positions):
    inverse_freq = 10000.0 ** (-2.0 * jnp.arange(HD // 2, dtype=jnp.float32) / HD)
    return positions.astype(jnp.float32)[..., None] * inverse_freq


def rotate(field_in, angles):
    half_dim = field_in.shape[-1] // 2
    cosine = jnp.cos(angles)
    sine_part = jnp.sin(angles)
    lower_half = field_in[..., :half_dim]
    upper_half = field_in[..., half_dim:]
    return jnp.concatenate(
        [
            lower_half * cosine - upper_half * sine_part,
            upper_half * cosine + lower_half * sine_part,
        ],
        axis=-1,
    )


def gelu_tanh(values):
    return jax.nn.gelu(values, approximate=True)


def contract(left_op, right_op, left_dim, right_dim):
    return lax.dot_general(
        left_op,
        right_op,
        (((left_dim,), (right_dim,)), ((), ())),
        preferred_element_type=jnp.float32,
    )


def batched(left_op, right_op, left_dim, right_dim):
    return lax.dot_general(
        left_op,
        right_op,
        (((left_dim,), (right_dim,)), ((0,), (0,))),
        preferred_element_type=jnp.float32,
    )


def low(values):
    return values.astype(jnp.bfloat16)


def gather_rows(values):
    return lax.all_gather(values, "fsdp", axis=values.ndim - 2, tiled=True)


def sum_rows(values):
    return lax.psum_scatter(values, "fsdp", scatter_dimension=1, tiled=True)


def swap_rep(values):
    return lax.ppermute(values, "rep", [(0, 1), (1, 0)])


def local(
    tokens, segment_ids, norm_gains, attn_weight, adapter, ffn_weight, ffn_adapter, cotangent
):
    micro, local_len, model_dim = tokens.shape
    shards = lax.axis_size("fsdp")
    me = lax.axis_index("fsdp")
    seq_len = local_len * shards
    offset = me * local_len
    count = micro * local_len
    every = micro * seq_len
    q_width = HEADS * HD
    kv_end = q_width + 2 * HD
    score_scale = HD ** (-0.5)
    hidden_cols = ffn_weight.shape[0]
    attn_rows = attn_weight.shape[0]

    seg_cols = count // attn_rows
    seg_block = low(segment_ids).reshape(attn_rows, seg_cols)
    spare = jnp.zeros((attn_rows, 128 - 2 - seg_cols), jnp.bfloat16)
    first = gather_rows(
        jnp.concatenate(
            [
                attn_weight[:, :kv_end],
                adapter[:, : 2 * RANK],
                norm_gains,
                seg_block,
                spare,
            ],
            axis=1,
        )
    )
    second = gather_rows(jnp.concatenate([attn_weight[:, kv_end:], adapter[:, 2 * RANK :]], axis=1))
    extra = kv_end + 2 * RANK
    w_proj = first[:, :kv_end]
    a_q = first[:, kv_end : kv_end + RANK]
    bq_t = first[:, kv_end + RANK : extra]
    gain_two = first[:, extra : extra + 2].astype(jnp.float32)
    seg_all = first[:, extra + 2 : extra + 2 + seg_cols].reshape(shards, micro, local_len)
    seg_all = seg_all.transpose(1, 0, 2).reshape(micro, seq_len).astype(jnp.int32)
    w_out = second[:, :q_width]
    bd_t = second[:, q_width:]
    cot_all = gather_rows(cotangent).reshape(every, model_dim)

    hidden_in = tokens.reshape(count, model_dim).astype(jnp.float32)
    key_index = jnp.arange(seq_len, dtype=jnp.int32)
    query_index = offset + jnp.arange(local_len, dtype=jnp.int32)
    before = jnp.sum(
        (seg_all[:, None, :] < segment_ids[:, :, None]).astype(jnp.int32), axis=2
    )
    angles = angles_of(query_index[None, :] - before).reshape(count, HD // 2)
    normed, norm_back_one = jax.vjp(rms_scale, hidden_in, gain_two[:, 0])
    normed_low = low(normed)
    normed_cols = lax.all_to_all(
        normed_low.reshape(micro, local_len, model_dim), "fsdp", 2, 1, tiled=True
    ).reshape(every, attn_rows)
    projected = contract(normed_low, w_proj, 1, 0)
    query_low = low(contract(normed_low, a_q, 1, 0))
    query_pre = projected[:, :q_width] + contract(query_low, bq_t, 1, 1)
    queries = low(rotate(query_pre.reshape(count, HEADS, HD), angles[:, None, :]))
    queries = queries.reshape(micro, local_len * HEADS, HD)
    keys_low = low(rotate(projected[:, q_width : q_width + HD], angles))
    values_low = low(projected[:, q_width + HD :])
    kv_all = gather_rows(
        jnp.concatenate([keys_low, values_low], axis=1).reshape(micro, local_len, 2 * HD)
    )
    keys_all = kv_all[..., :HD]
    values_all = kv_all[..., HD:]
    allowed = (
        (segment_ids[:, :, None] == seg_all[:, None, :])
        & (key_index[None, None, :] <= query_index[None, :, None])
    )[:, :, None, :]
    scores = (batched(queries, keys_all, 2, 2) * score_scale).reshape(
        micro, local_len, HEADS, seq_len
    )
    scores = jnp.where(allowed, scores, -1e30)
    top_score = jnp.max(scores, axis=-1, keepdims=True)
    exp_scores = jnp.exp(scores - top_score)
    weights = exp_scores / jnp.sum(exp_scores, axis=-1, keepdims=True)
    weights_low = low(weights).reshape(micro, local_len * HEADS, seq_len)
    context = low(batched(weights_low, values_all, 2, 1)).reshape(count, q_width)
    mixed_sum = hidden_in + contract(context, w_out, 1, 1)
    normed_two, norm_back_two = jax.vjp(rms_scale, mixed_sum, gain_two[:, 1])
    inputs_all = gather_rows(low(normed_two).reshape(micro, local_len, model_dim))
    inputs_all = inputs_all.reshape(every, model_dim)
    kept_all = gather_rows(
        jnp.concatenate([context, query_low], axis=1).reshape(micro, local_len, q_width + RANK)
    ).reshape(every, q_width + RANK)
    low_grad_all = low(contract(cot_all, bd_t, 1, 0))

    step = hidden_cols // CHUNKS
    hidden_parts, gate_parts, up_parts, ffn_parts, low_parts = [], [], [], [], []
    for at in range(CHUNKS):
        units = slice(at * step, (at + 1) * step)
        w_gate, w_up, w_down = (ffn_weight[units, j, :] for j in range(3))
        gate_pre = contract(inputs_all, w_gate, 1, 1)
        up_pre = contract(inputs_all, w_up, 1, 1)
        activated, gelu_back = jax.vjp(gelu_tanh, gate_pre)
        hidden_act = low(activated * up_pre)
        hidden_grad = contract(cot_all, w_down, 1, 1) + contract(
            low_grad_all, ffn_adapter[units], 1, 1
        )
        gate_grad = low(gelu_back(hidden_grad * up_pre)[0])
        up_grad = low(hidden_grad * activated)
        mine = low(
            jnp.stack(
                [
                    contract(gate_grad, inputs_all, 0, 0),
                    contract(up_grad, inputs_all, 0, 0),
                    contract(hidden_act, cot_all, 0, 0),
                ],
                axis=0,
            )
        )
        mine_low = low(contract(hidden_act, low_grad_all, 0, 0))
        ffn_parts.append((mine, swap_rep(mine)))
        low_parts.append((mine_low, swap_rep(mine_low)))
        hidden_parts.append(hidden_act)
        gate_parts.append(gate_grad)
        up_parts.append(up_grad)

    gate_grad = jnp.concatenate(gate_parts, axis=1)
    up_grad = jnp.concatenate(up_parts, axis=1)
    hidden_act = jnp.concatenate(hidden_parts, axis=1)
    normed_two_grad = sum_rows(
        low(
            contract(gate_grad, ffn_weight[:, 0, :], 1, 0)
            + contract(up_grad, ffn_weight[:, 1, :], 1, 0)
        ).reshape(micro, seq_len, model_dim)
    )
    normed_two_grad = normed_two_grad.reshape(count, model_dim).astype(jnp.float32)
    down_mine = sum_rows(
        jnp.concatenate(
            [
                low(contract(hidden_act, ffn_weight[:, 2, :], 1, 0)),
                low(contract(hidden_act, ffn_adapter, 1, 0)),
            ],
            axis=1,
        ).reshape(micro, seq_len, model_dim + RANK)
    ).reshape(count, model_dim + RANK)
    down_low = down_mine[:, model_dim:]
    result = (
        mixed_sum + down_mine[:, :model_dim].astype(jnp.float32) + contract(down_low, bd_t, 1, 1)
    )

    cot_full = cotangent.reshape(count, model_dim).astype(jnp.float32)
    mixed_part, gain_two_grad = norm_back_two(normed_two_grad)
    mixed_grad = cot_full + mixed_part
    out_grad_low = low(mixed_grad)
    out_cols = lax.all_to_all(
        out_grad_low.reshape(micro, local_len, model_dim), "fsdp", 2, 1, tiled=True
    ).reshape(every, attn_rows)
    wout_grad = contract(out_cols, kept_all[:, :q_width], 0, 0)
    context_grad = contract(out_grad_low, w_out, 1, 0)
    context_rows = low(context_grad).reshape(micro, local_len * HEADS, HD)
    prob_grad = batched(context_rows, values_all, 2, 2).reshape(micro, local_len, HEADS, seq_len)
    score_grad = weights * (prob_grad - jnp.sum(weights * prob_grad, axis=-1, keepdims=True))
    score_grad = low(score_grad).reshape(micro, local_len * HEADS, seq_len)
    query_grad = batched(score_grad, keys_all, 2, 1) * score_scale
    query_grad = query_grad.reshape(count, HEADS, HD)
    kv_grad = sum_rows(
        low(
            jnp.concatenate(
                [
                    batched(score_grad, queries, 1, 1) * score_scale,
                    batched(weights_low, context_rows, 1, 1),
                ],
                axis=2,
            )
        )
    ).reshape(count, 2 * HD)
    query_pre_grad = low(rotate(query_grad, -angles[:, None, :]).reshape(count, q_width))
    key_grad = low(rotate(kv_grad[:, :HD].astype(jnp.float32), -angles))
    value_grad = kv_grad[:, HD:]
    rank_grad = low(contract(query_pre_grad, bq_t, 1, 0))
    proj_grad = jnp.concatenate([query_pre_grad, key_grad, value_grad], axis=1)
    normed_grad = contract(proj_grad, w_proj, 1, 1) + contract(rank_grad, a_q, 1, 1)
    hidden_part, gain_one_grad = norm_back_one(normed_grad)
    input_grad = low(mixed_grad + hidden_part)

    back_all = gather_rows(
        jnp.concatenate([proj_grad, rank_grad, down_low], axis=1).reshape(
            micro, local_len, kv_end + 2 * RANK
        )
    ).reshape(every, kv_end + 2 * RANK)
    my_cols = me * attn_rows
    attn_in = contract(normed_cols, back_all[:, : kv_end + RANK], 0, 0)
    bq_grad = contract(
        lax.dynamic_slice_in_dim(back_all, my_cols, attn_rows, 1), kept_all[:, q_width:], 0, 0
    )
    bd_grad = contract(
        lax.dynamic_slice_in_dim(cot_all, my_cols, attn_rows, 1),
        back_all[:, kv_end + RANK :],
        0,
        0,
    )
    gain_now = jnp.stack([gain_one_grad, gain_two_grad], axis=1).reshape(shards, attn_rows, 2)
    gain_now = lax.all_to_all(gain_now, "fsdp", 0, 0, tiled=True).sum(axis=0)
    tail = low(jnp.concatenate([attn_in, bq_grad, bd_grad], axis=1))
    tail_out = low(wout_grad)
    tail_gain = low(gain_now)

    def total(mine, other):
        return mine.astype(jnp.float32) + other.astype(jnp.float32)

    tail = total(tail, swap_rep(tail))
    tail_out = total(tail_out, swap_rep(tail_out))
    gains_grad = total(tail_gain, swap_rep(tail_gain))
    attn_grad = jnp.concatenate([tail[:, :kv_end], tail_out], axis=1)
    adapter_grad = tail[:, kv_end:]
    ffn_grad = jnp.concatenate([total(*pair) for pair in ffn_parts], axis=1).transpose(1, 0, 2)
    ffn_low_grad = jnp.concatenate([total(*pair) for pair in low_parts], axis=0)
    return (
        low(result).reshape(micro, local_len, model_dim),
        input_grad.reshape(micro, local_len, model_dim),
        gains_grad,
        attn_grad,
        adapter_grad,
        ffn_grad,
        ffn_low_grad,
    )


def solution(mesh):
    placed = (
        P("rep", "fsdp", None),
        P("rep", "fsdp"),
        P("fsdp", None),
        P("fsdp", None),
        P("fsdp", None),
        P("fsdp", None, None),
        P("fsdp", None),
        P("rep", "fsdp", None),
    )
    return jax.shard_map(
        local,
        mesh=mesh,
        in_specs=placed,
        out_specs=(
            P("rep", "fsdp", None),
            P("rep", "fsdp", None),
            P("fsdp", None),
            P("fsdp", None),
            P("fsdp", None),
            P("fsdp", None, None),
            P("fsdp", None),
        ),
        check_vma=False,
    )
```

```python
import jax
import jax.numpy as jnp
from jax import lax
from jax.sharding import PartitionSpec as P

HEADS = 8
HD = 256
RANK = 256
CHUNKS = 4


epsilon = 1e-06


def rms_scale(values, gain_col):
    return (
        values * lax.rsqrt(jnp.mean(values * values, axis=-1, keepdims=True) + epsilon) * gain_col
    )


def angles_of(positions):
    inverse_freq = 10000.0 ** (-2.0 * jnp.arange(HD // 2, dtype=jnp.float32) / HD)
    return positions.astype(jnp.float32)[..., None] * inverse_freq


def rotate(field_in, angles):
    half_dim = field_in.shape[-1] // 2
    cosine = jnp.cos(angles)
    sine_part = jnp.sin(angles)
    lower_half = field_in[..., :half_dim]
    upper_half = field_in[..., half_dim:]
    return jnp.concatenate(
        [
            lower_half * cosine - upper_half * sine_part,
            upper_half * cosine + lower_half * sine_part,
        ],
        axis=-1,
    )


def gelu_tanh(values):
    return jax.nn.gelu(values, approximate=True)


def contract(left_op, right_op, left_dim, right_dim):
    return lax.dot_general(
        left_op,
        right_op,
        (((left_dim,), (right_dim,)), ((), ())),
        preferred_element_type=jnp.float32,
    )


def batched(left_op, right_op, left_dim, right_dim):
    return lax.dot_general(
        left_op,
        right_op,
        (((left_dim,), (right_dim,)), ((0,), (0,))),
        preferred_element_type=jnp.float32,
    )


def low(values):
    return values.astype(jnp.bfloat16)


def gather_rows(values):
    return lax.all_gather(values, "fsdp", axis=values.ndim - 2, tiled=True)


def sum_rows(values):
    return lax.psum_scatter(values, "fsdp", scatter_dimension=1, tiled=True)


def swap_rep(values):
    return lax.ppermute(values, "rep", [(0, 1), (1, 0)])


def local(
    tokens, segment_ids, norm_gains, attn_weight, adapter, ffn_weight, ffn_adapter, cotangent
):
    micro, local_len, model_dim = tokens.shape
    shards = lax.axis_size("fsdp")
    me = lax.axis_index("fsdp")
    seq_len = local_len * shards
    offset = me * local_len
    count = micro * local_len
    every = micro * seq_len
    q_width = HEADS * HD
    kv_end = q_width + 2 * HD
    score_scale = HD ** (-0.5)
    hidden_cols = ffn_weight.shape[0]
    attn_rows = attn_weight.shape[0]

    seg_cols = count // attn_rows
    seg_block = low(segment_ids).reshape(attn_rows, seg_cols)
    spare = jnp.zeros((attn_rows, 128 - 2 - seg_cols), jnp.bfloat16)
    first = gather_rows(
        jnp.concatenate(
            [
                attn_weight[:, :kv_end],
                adapter[:, : 2 * RANK],
                norm_gains,
                seg_block,
                spare,
            ],
            axis=1,
        )
    )
    second = gather_rows(jnp.concatenate([attn_weight[:, kv_end:], adapter[:, 2 * RANK :]], axis=1))
    extra = kv_end + 2 * RANK
    w_proj = first[:, :kv_end]
    a_q = first[:, kv_end : kv_end + RANK]
    bq_t = first[:, kv_end + RANK : extra]
    gain_two = first[:, extra : extra + 2].astype(jnp.float32)
    seg_all = first[:, extra + 2 : extra + 2 + seg_cols].reshape(shards, micro, local_len)
    seg_all = seg_all.transpose(1, 0, 2).reshape(micro, seq_len).astype(jnp.int32)
    w_out = second[:, :q_width]
    bd_t = second[:, q_width:]
    cot_all = gather_rows(cotangent).reshape(every, model_dim)

    hidden_in = tokens.reshape(count, model_dim).astype(jnp.float32)
    key_index = jnp.arange(seq_len, dtype=jnp.int32)
    query_index = offset + jnp.arange(local_len, dtype=jnp.int32)
    before = jnp.sum(
        (seg_all[:, None, :] < segment_ids[:, :, None]).astype(jnp.int32), axis=2
    )
    angles = angles_of(query_index[None, :] - before).reshape(count, HD // 2)
    normed, norm_back_one = jax.vjp(rms_scale, hidden_in, gain_two[:, 0])
    normed_low = low(normed)
    normed_cols = lax.all_to_all(
        normed_low.reshape(micro, local_len, model_dim), "fsdp", 2, 1, tiled=True
    ).reshape(every, attn_rows)
    projected = contract(normed_low, w_proj, 1, 0)
    query_low = low(contract(normed_low, a_q, 1, 0))
    query_pre = projected[:, :q_width] + contract(query_low, bq_t, 1, 1)
    queries = low(rotate(query_pre.reshape(count, HEADS, HD), angles[:, None, :]))
    queries = queries.reshape(micro, local_len * HEADS, HD)
    keys_low = low(rotate(projected[:, q_width : q_width + HD], angles))
    values_low = low(projected[:, q_width + HD :])
    kv_all = gather_rows(
        jnp.concatenate([keys_low, values_low], axis=1).reshape(micro, local_len, 2 * HD)
    )
    keys_all = kv_all[..., :HD]
    values_all = kv_all[..., HD:]
    allowed = (
        (segment_ids[:, :, None] == seg_all[:, None, :])
        & (key_index[None, None, :] <= query_index[None, :, None])
    )[:, :, None, :]
    scores = (batched(queries, keys_all, 2, 2) * score_scale).reshape(
        micro, local_len, HEADS, seq_len
    )
    scores = jnp.where(allowed, scores, -1e30)
    top_score = jnp.max(scores, axis=-1, keepdims=True)
    exp_scores = jnp.exp(scores - top_score)
    weights = exp_scores / jnp.sum(exp_scores, axis=-1, keepdims=True)
    weights_low = low(weights).reshape(micro, local_len * HEADS, seq_len)
    context = low(batched(weights_low, values_all, 2, 1)).reshape(count, q_width)
    mixed_sum = hidden_in + contract(context, w_out, 1, 1)
    normed_two, norm_back_two = jax.vjp(rms_scale, mixed_sum, gain_two[:, 1])
    inputs_all = gather_rows(low(normed_two).reshape(micro, local_len, model_dim))
    inputs_all = inputs_all.reshape(every, model_dim)
    kept_all = gather_rows(
        jnp.concatenate([context, query_low], axis=1).reshape(micro, local_len, q_width + RANK)
    ).reshape(every, q_width + RANK)
    low_grad_all = low(contract(cot_all, bd_t, 1, 0))

    step = hidden_cols // CHUNKS
    hidden_parts, gate_parts, up_parts, ffn_parts, low_parts = [], [], [], [], []
    for at in range(CHUNKS):
        units = slice(at * step, (at + 1) * step)
        w_gate, w_up, w_down = (ffn_weight[units, j, :] for j in range(3))
        gate_pre = contract(inputs_all, w_gate, 1, 1)
        up_pre = contract(inputs_all, w_up, 1, 1)
        activated, gelu_back = jax.vjp(gelu_tanh, gate_pre)
        hidden_act = low(activated * up_pre)
        hidden_grad = contract(cot_all, w_down, 1, 1) + contract(
            low_grad_all, ffn_adapter[units], 1, 1
        )
        gate_grad = low(gelu_back(hidden_grad * up_pre)[0])
        up_grad = low(hidden_grad * activated)
        mine = low(
            jnp.stack(
                [
                    contract(gate_grad, inputs_all, 0, 0),
                    contract(up_grad, inputs_all, 0, 0),
                    contract(hidden_act, cot_all, 0, 0),
                ],
                axis=0,
            )
        )
        mine_low = low(contract(hidden_act, low_grad_all, 0, 0))
        ffn_parts.append((mine, swap_rep(mine)))
        low_parts.append((mine_low, swap_rep(mine_low)))
        hidden_parts.append(hidden_act)
        gate_parts.append(gate_grad)
        up_parts.append(up_grad)

    gate_grad = jnp.concatenate(gate_parts, axis=1)
    up_grad = jnp.concatenate(up_parts, axis=1)
    hidden_act = jnp.concatenate(hidden_parts, axis=1)
    gate_grad, kept_all = lax.optimization_barrier((gate_grad, kept_all))
    normed_two_grad = sum_rows(
        low(
            contract(gate_grad, ffn_weight[:, 0, :], 1, 0)
            + contract(up_grad, ffn_weight[:, 1, :], 1, 0)
        ).reshape(micro, seq_len, model_dim)
    )
    normed_two_grad, _ = lax.optimization_barrier(
        (normed_two_grad, [pair[0] for pair in ffn_parts] + [ffn_parts[0][1]])
    )
    normed_two_grad = normed_two_grad.reshape(count, model_dim).astype(jnp.float32)
    cot_full = cotangent.reshape(count, model_dim).astype(jnp.float32)
    mixed_part, gain_two_grad = norm_back_two(normed_two_grad)
    mixed_grad = cot_full + mixed_part
    out_grad_low = low(mixed_grad)
    out_cols = lax.all_to_all(
        out_grad_low.reshape(micro, local_len, model_dim), "fsdp", 2, 1, tiled=True
    ).reshape(every, attn_rows)
    wout_grad = contract(out_cols, kept_all[:, :q_width], 0, 0)
    context_grad = contract(out_grad_low, w_out, 1, 0)
    context_rows = low(context_grad).reshape(micro, local_len * HEADS, HD)
    prob_grad = batched(context_rows, values_all, 2, 2).reshape(micro, local_len, HEADS, seq_len)
    score_grad = weights * (prob_grad - jnp.sum(weights * prob_grad, axis=-1, keepdims=True))
    score_grad = low(score_grad).reshape(micro, local_len * HEADS, seq_len)
    query_grad = batched(score_grad, keys_all, 2, 1) * score_scale
    query_grad = query_grad.reshape(count, HEADS, HD)
    kv_part = low(
        jnp.concatenate(
            [
                batched(score_grad, queries, 1, 1) * score_scale,
                batched(weights_low, context_rows, 1, 1),
            ],
            axis=2,
        )
    )
    kv_part, _ = lax.optimization_barrier((kv_part, ffn_parts[1][1]))
    sums = sum_rows(
        jnp.concatenate(
            [
                low(contract(hidden_act, ffn_weight[:, 2, :], 1, 0)).reshape(
                    micro, seq_len, model_dim
                ),
                low(contract(hidden_act, ffn_adapter, 1, 0)).reshape(micro, seq_len, RANK),
                kv_part,
            ],
            axis=2,
        )
    )
    sums, _ = lax.optimization_barrier((sums, ffn_parts[2][1]))
    sums = sums.reshape(count, model_dim + RANK + 2 * HD)
    kv_grad = sums[:, model_dim + RANK :]
    down_low = sums[:, model_dim : model_dim + RANK]
    result = (
        mixed_sum + sums[:, :model_dim].astype(jnp.float32) + contract(down_low, bd_t, 1, 1)
    )
    query_pre_grad = low(rotate(query_grad, -angles[:, None, :]).reshape(count, q_width))
    key_grad = low(rotate(kv_grad[:, :HD].astype(jnp.float32), -angles))
    value_grad = kv_grad[:, HD:]
    rank_grad = low(contract(query_pre_grad, bq_t, 1, 0))
    proj_grad = jnp.concatenate([query_pre_grad, key_grad, value_grad], axis=1)
    normed_grad = contract(proj_grad, w_proj, 1, 1) + contract(rank_grad, a_q, 1, 1)
    hidden_part, gain_one_grad = norm_back_one(normed_grad)
    input_grad = low(mixed_grad + hidden_part)

    back_all = gather_rows(
        jnp.concatenate([proj_grad, rank_grad, down_low], axis=1).reshape(
            micro, local_len, kv_end + 2 * RANK
        )
    ).reshape(every, kv_end + 2 * RANK)
    my_cols = me * attn_rows
    attn_in = contract(normed_cols, back_all[:, : kv_end + RANK], 0, 0)
    bq_grad = contract(
        lax.dynamic_slice_in_dim(back_all, my_cols, attn_rows, 1), kept_all[:, q_width:], 0, 0
    )
    bd_grad = contract(
        lax.dynamic_slice_in_dim(cot_all, my_cols, attn_rows, 1),
        back_all[:, kv_end + RANK :],
        0,
        0,
    )
    gain_now = jnp.stack([gain_one_grad, gain_two_grad], axis=1).reshape(shards, attn_rows, 2)
    gain_now = lax.all_to_all(gain_now, "fsdp", 0, 0, tiled=True).sum(axis=0)
    tail = low(jnp.concatenate([attn_in, bq_grad, bd_grad], axis=1))
    tail_out = low(wout_grad)
    tail_gain = low(gain_now)

    def total(mine, other):
        return mine.astype(jnp.float32) + other.astype(jnp.float32)

    tail = total(tail, swap_rep(tail))
    tail_out = total(tail_out, swap_rep(tail_out))
    gains_grad = total(tail_gain, swap_rep(tail_gain))
    attn_grad = jnp.concatenate([tail[:, :kv_end], tail_out], axis=1)
    adapter_grad = tail[:, kv_end:]
    ffn_grad = jnp.concatenate([total(*pair) for pair in ffn_parts], axis=1).transpose(1, 0, 2)
    ffn_low_grad = jnp.concatenate([total(*pair) for pair in low_parts], axis=0)
    return (
        low(result).reshape(micro, local_len, model_dim),
        input_grad.reshape(micro, local_len, model_dim),
        gains_grad,
        attn_grad,
        adapter_grad,
        ffn_grad,
        ffn_low_grad,
    )


def solution(mesh):
    placed = (
        P("rep", "fsdp", None),
        P("rep", "fsdp"),
        P("fsdp", None),
        P("fsdp", None),
        P("fsdp", None),
        P("fsdp", None, None),
        P("fsdp", None),
        P("rep", "fsdp", None),
    )
    return jax.shard_map(
        local,
        mesh=mesh,
        in_specs=placed,
        out_specs=(
            P("rep", "fsdp", None),
            P("rep", "fsdp", None),
            P("fsdp", None),
            P("fsdp", None),
            P("fsdp", None),
            P("fsdp", None, None),
            P("fsdp", None),
        ),
        check_vma=False,
    )
```

```python
import functools

import jax
import jax.numpy as jnp
from jax import lax
from jax.experimental import pallas as pl
from jax.experimental.pallas import tpu as pltpu
from jax.sharding import PartitionSpec as P

HEADS = 8
HD = 256
RANK = 256
CHUNKS = 4


epsilon = 1e-06


def rms_scale(values, gain_col):
    return (
        values * lax.rsqrt(jnp.mean(values * values, axis=-1, keepdims=True) + epsilon) * gain_col
    )


def angles_of(positions):
    inverse_freq = 10000.0 ** (-2.0 * jnp.arange(HD // 2, dtype=jnp.float32) / HD)
    return positions.astype(jnp.float32)[..., None] * inverse_freq


def rotate(field_in, angles):
    half_dim = field_in.shape[-1] // 2
    cosine = jnp.cos(angles)
    sine_part = jnp.sin(angles)
    lower_half = field_in[..., :half_dim]
    upper_half = field_in[..., half_dim:]
    return jnp.concatenate(
        [
            lower_half * cosine - upper_half * sine_part,
            upper_half * cosine + lower_half * sine_part,
        ],
        axis=-1,
    )


def gelu_tanh(values):
    return jax.nn.gelu(values, approximate=True)


def contract(left_op, right_op, left_dim, right_dim):
    return lax.dot_general(
        left_op,
        right_op,
        (((left_dim,), (right_dim,)), ((), ())),
        preferred_element_type=jnp.float32,
    )


def batched(left_op, right_op, left_dim, right_dim):
    return lax.dot_general(
        left_op,
        right_op,
        (((left_dim,), (right_dim,)), ((0,), (0,))),
        preferred_element_type=jnp.float32,
    )


def low(values):
    return values.astype(jnp.bfloat16)


def gather_rows(values):
    return lax.all_gather(values, "fsdp", axis=values.ndim - 2, tiled=True)


def sum_rows(values):
    return lax.psum_scatter(values, "fsdp", scatter_dimension=1, tiled=True)


def swap_rep(values):
    return lax.ppermute(values, "rep", [(0, 1), (1, 0)])


def grid_of(shards):
    short = 2 if shards <= 16 else 4
    return shards // (2 * short), short


def neighbours(shards):
    long_len, short_len = grid_of(shards)
    me = lax.axis_index("fsdp")
    return me, me // (2 * short_len), (me // 2) % short_len, me % 2


def greet(shards, across):
    long_len, short_len = grid_of(shards)
    me, at_long, at_short, core = neighbours(shards)
    barrier = pltpu.get_barrier_semaphore()
    around = [
        (me >= 0, {"fsdp": me + 1 - 2 * core}),
        (at_long > 0, {"fsdp": me - 2 * short_len}),
        (at_long < long_len - 1, {"fsdp": me + 2 * short_len}),
        (at_short > 0, {"fsdp": me - 2}),
        (at_short < short_len - 1, {"fsdp": me + 2}),
    ]
    if across:
        around.append((me >= 0, {"rep": 1 - lax.axis_index("rep")}))
    for has, peer in around:
        @pl.when(has)
        def _():
            pl.semaphore_signal(barrier, inc=1, device_id=peer)
    pl.semaphore_wait(barrier, sum(has.astype(jnp.int32) for has, _ in around))


def gather_kernel(shards, widths, shared, *refs):
    long_len, short_len = grid_of(shards)
    count = len(widths)
    own = refs[:count]
    out = refs[count : 2 * count]
    send_sem, recv_sem, own_sem = refs[2 * count :]
    me, at_long, at_short, core = neighbours(shards)
    stride = 2 * short_len
    partner = {"fsdp": me + 1 - 2 * core}
    half = shared // 2
    parts = []
    if shared:
        rep = lax.axis_index("rep")
        peer_rep = {"rep": 1 - rep}
        parts.append((0, pl.multiple_of(rep * half, 128), half))
        parts.append((0, shared, widths[0] - shared))
        parts += [(k, 0, widths[k]) for k in range(1, count)]
        other = (0, pl.multiple_of((1 - rep) * half, 128), half)
    else:
        parts += [(k, 0, widths[k]) for k in range(count)]
        other = None
    lanes = list(range(len(parts)))
    away = len(parts)
    if shared:
        parts.append(other)

    def copy(lane, way, slot, peer, fresh):
        k, first, width = parts[lane]
        columns = pl.ds(first, width)
        there = out[k].at[:, slot, :, columns]
        return pltpu.make_async_remote_copy(
            src_ref=own[k].at[:, :, columns] if fresh else there,
            dst_ref=there,
            send_sem=send_sem.at[lane, way, slot],
            recv_sem=recv_sem.at[away if way == 5 else lane, slot],
            device_id=peer,
        )

    greet(shards, bool(shared))
    done = []

    def start(has, which, way, slot, peer, fresh=False):
        @pl.when(has)
        def _():
            for lane in which:
                copy(lane, way, slot, peer, fresh).start()

        done.append((has, which, way, slot, peer, fresh))

    def arrive(has, which, slot):
        @pl.when(has)
        def _():
            for lane in which:
                copy(lane, 0, slot, partner, False).wait_recv()

    late = []

    def got(has, slot):
        if shared:
            start(has, [0], 5, slot, peer_rep)
            late.append((has, slot))
        start(has, lanes, 4, slot, partner)

    def from_across():
        for has, slot in late:
            arrive(has, [away], slot)
            start(has, [away], 4, slot, partner)
        late.clear()

    def spread_short(has, slot, fresh=False):
        start(has & (at_short < short_len - 1), lanes, 2, slot, {"fsdp": me + 2}, fresh)
        start(has & (at_short > 0), lanes, 3, slot, {"fsdp": me - 2}, fresh)

    def short_arrivals(has, line):
        for far in range(1, short_len):
            for sign in (-1, 1):
                source = at_short + sign * far
                ok = has & (source >= 0) & (source < short_len)
                slot = me + 2 * sign * far + (line - at_long) * stride
                arrive(ok, lanes, slot)
                if far < short_len - 1:
                    onward = at_short - sign
                    start(
                        ok & (onward >= 0) & (onward < short_len),
                        lanes,
                        2 if sign < 0 else 3,
                        slot,
                        {"fsdp": me - 2 * sign},
                    )
                got(ok, slot)

    true = me >= 0
    start(at_long < long_len - 1, lanes, 0, me, {"fsdp": me + stride}, True)
    start(at_long > 0, lanes, 1, me, {"fsdp": me - stride}, True)
    spread_short(true, me, True)
    every = list(range(len(parts)))
    start(true, every, 4, me, partner, True)
    mine = [pltpu.make_async_copy(own[k], out[k].at[:, me], own_sem.at[k]) for k in range(count)]
    for each in mine:
        each.start()
    for far in range(1, long_len):
        for sign in (-1, 1):
            source = at_long + sign * far
            ok = (source >= 0) & (source < long_len)
            slot = me + sign * far * stride
            arrive(ok, lanes, slot)
            onward = at_long - sign
            start(
                ok & (onward >= 0) & (onward < long_len),
                lanes,
                0 if sign < 0 else 1,
                slot,
                {"fsdp": me - sign * stride},
            )
            spread_short(ok, slot)
            got(ok, slot)
        if far == 1:
            short_arrivals(true, at_long)
        else:
            for sign in (-1, 1):
                source = at_long + sign * (far - 1)
                short_arrivals((source >= 0) & (source < long_len), source)
        if far > 1:
            from_across()
    for sign in (-1, 1):
        source = at_long + sign * (long_len - 1)
        short_arrivals((source >= 0) & (source < long_len), source)
    from_across()
    for line in range(long_len):
        for short in range(short_len):
            arrive(true, every, (line * short_len + short) * 2 + 1 - core)
    for has, which, way, slot, peer, fresh in done:
        @pl.when(has)
        def _():
            for lane in which:
                copy(lane, way, slot, peer, fresh).wait_send()
    for each in mine:
        each.wait()


def gather_all(shards, ident, *values, shared=0):
    widths = tuple(v.shape[2] for v in values)
    count = len(values)
    lanes = count + (2 if shared else 0)
    return pl.pallas_call(
        functools.partial(gather_kernel, shards, widths, shared),
        out_shape=[
            jax.ShapeDtypeStruct((v.shape[0], shards) + v.shape[1:], v.dtype) for v in values
        ],
        in_specs=[pl.BlockSpec(memory_space=pltpu.VMEM)] * count,
        out_specs=[pl.BlockSpec(memory_space=pl.ANY)] * count,
        scratch_shapes=[
            pltpu.SemaphoreType.DMA((lanes, 6, shards)),
            pltpu.SemaphoreType.DMA((lanes, shards)),
            pltpu.SemaphoreType.DMA((count,)),
        ],
        compiler_params=pltpu.CompilerParams(collective_id=ident, has_side_effects=True),
        name="gather_%d" % ident,
    )(*values)


def local(
    tokens, segment_ids, norm_gains, attn_weight, adapter, ffn_weight, ffn_adapter, cotangent
):
    micro, local_len, model_dim = tokens.shape
    shards = lax.axis_size("fsdp")
    me = lax.axis_index("fsdp")
    seq_len = local_len * shards
    offset = me * local_len
    count = micro * local_len
    every = micro * seq_len
    q_width = HEADS * HD
    kv_end = q_width + 2 * HD
    score_scale = HD ** (-0.5)
    hidden_cols = ffn_weight.shape[0]
    attn_rows = attn_weight.shape[0]

    seg_cols = count // attn_rows
    seg_block = low(segment_ids).reshape(attn_rows, seg_cols)
    spare = jnp.zeros((attn_rows, 128 - 2 - seg_cols), jnp.bfloat16)
    small = jnp.concatenate([norm_gains, seg_block, spare], axis=1)
    same = kv_end + 4 * RANK
    attn_all, adapter_all, small_all = gather_all(
        shards, 1, attn_weight[None], adapter[None], small[None], shared=same
    )
    cotangent_now, small_all = lax.optimization_barrier((cotangent, small_all))
    cot_all = gather_rows(cotangent_now).reshape(every, model_dim)
    attn_all = attn_all.reshape(model_dim, attn_weight.shape[1])
    adapter_all = adapter_all.reshape(model_dim, 3 * RANK)
    small_all = small_all.reshape(model_dim, 128)
    w_proj = attn_all[:, :kv_end]
    w_out = attn_all[:, kv_end:]
    a_q, bq_t, bd_t = (adapter_all[:, j * RANK : (j + 1) * RANK] for j in range(3))
    gain_two = small_all[:, :2].astype(jnp.float32)
    seg_all = small_all[:, 2 : 2 + seg_cols].reshape(shards, micro, local_len)
    seg_all = seg_all.transpose(1, 0, 2).reshape(micro, seq_len).astype(jnp.int32)

    hidden_in = tokens.reshape(count, model_dim).astype(jnp.float32)
    key_index = jnp.arange(seq_len, dtype=jnp.int32)
    query_index = offset + jnp.arange(local_len, dtype=jnp.int32)
    before = jnp.sum(
        (seg_all[:, None, :] < segment_ids[:, :, None]).astype(jnp.int32), axis=2
    )
    angles = angles_of(query_index[None, :] - before).reshape(count, HD // 2)
    normed, norm_back_one = jax.vjp(rms_scale, hidden_in, gain_two[:, 0])
    normed_low = low(normed)
    projected = contract(normed_low, w_proj, 1, 0)
    query_low = low(contract(normed_low, a_q, 1, 0))
    query_pre = projected[:, :q_width] + contract(query_low, bq_t, 1, 1)
    queries = low(rotate(query_pre.reshape(count, HEADS, HD), angles[:, None, :]))
    queries = queries.reshape(micro, local_len * HEADS, HD)
    keys_low = low(rotate(projected[:, q_width : q_width + HD], angles))
    values_low = low(projected[:, q_width + HD :])
    keys_all, values_all = (
        each.reshape(micro, seq_len, HD)
        for each in gather_all(
            shards,
            2,
            keys_low.reshape(micro, local_len, HD),
            values_low.reshape(micro, local_len, HD),
        )
    )
    allowed = (
        (segment_ids[:, :, None] == seg_all[:, None, :])
        & (key_index[None, None, :] <= query_index[None, :, None])
    )[:, :, None, :]
    scores = (batched(queries, keys_all, 2, 2) * score_scale).reshape(
        micro, local_len, HEADS, seq_len
    )
    scores = jnp.where(allowed, scores, -1e30)
    top_score = jnp.max(scores, axis=-1, keepdims=True)
    exp_scores = jnp.exp(scores - top_score)
    weights = exp_scores / jnp.sum(exp_scores, axis=-1, keepdims=True)
    weights_low = low(weights).reshape(micro, local_len * HEADS, seq_len)
    context = low(batched(weights_low, values_all, 2, 1)).reshape(count, q_width)
    mixed_sum = hidden_in + contract(context, w_out, 1, 1)
    normed_two, norm_back_two = jax.vjp(rms_scale, mixed_sum, gain_two[:, 1])
    (inputs_all,) = gather_all(shards, 3, low(normed_two).reshape(micro, local_len, model_dim))
    inputs_all = inputs_all.reshape(every, model_dim)
    kept, inputs_all = lax.optimization_barrier(
        (jnp.concatenate([context, query_low], axis=1), inputs_all)
    )
    kept_all = gather_rows(kept.reshape(micro, local_len, q_width + RANK))
    kept_all = kept_all.reshape(every, q_width + RANK)
    low_grad_all = low(contract(cot_all, bd_t, 1, 0))

    step = hidden_cols // CHUNKS
    hidden_parts, gate_parts, up_parts, ffn_parts = [], [], [], []
    for at in range(CHUNKS):
        units = slice(at * step, (at + 1) * step)
        w_gate, w_up, w_down = (ffn_weight[units, j, :] for j in range(3))
        gate_pre = contract(inputs_all, w_gate, 1, 1)
        up_pre = contract(inputs_all, w_up, 1, 1)
        activated, gelu_back = jax.vjp(gelu_tanh, gate_pre)
        hidden_act = low(activated * up_pre)
        hidden_grad = contract(cot_all, w_down, 1, 1) + contract(
            low_grad_all, ffn_adapter[units], 1, 1
        )
        gate_grad = low(gelu_back(hidden_grad * up_pre)[0])
        up_grad = low(hidden_grad * activated)
        for left, right in (
            (gate_grad, inputs_all),
            (up_grad, inputs_all),
            (hidden_act, cot_all),
        ):
            mine = low(contract(left, right, 0, 0))
            ffn_parts.append((mine, swap_rep(mine)))
        hidden_parts.append(hidden_act)
        gate_parts.append(gate_grad)
        up_parts.append(up_grad)

    gate_grad = jnp.concatenate(gate_parts, axis=1)
    up_grad = jnp.concatenate(up_parts, axis=1)
    hidden_act = jnp.concatenate(hidden_parts, axis=1)
    low_mine = low(contract(hidden_act, low_grad_all, 0, 0))
    gate_grad, kept_all = lax.optimization_barrier((gate_grad, kept_all))
    normed_two_grad = sum_rows(
        low(
            contract(gate_grad, ffn_weight[:, 0, :], 1, 0)
            + contract(up_grad, ffn_weight[:, 1, :], 1, 0)
        ).reshape(micro, seq_len, model_dim)
    )
    normed_two_grad, _ = lax.optimization_barrier(
        (normed_two_grad, [pair[0] for pair in ffn_parts] + [pair[1] for pair in ffn_parts[:4]])
    )
    normed_two_grad = normed_two_grad.reshape(count, model_dim).astype(jnp.float32)
    cot_full = cotangent.reshape(count, model_dim).astype(jnp.float32)
    mixed_part, gain_two_grad = norm_back_two(normed_two_grad)
    mixed_grad = cot_full + mixed_part
    out_grad_low = low(mixed_grad)
    both = jnp.concatenate([normed_low, out_grad_low], axis=0)
    both_cols = lax.all_to_all(
        both.reshape(2 * micro, local_len, model_dim), "fsdp", 2, 1, tiled=True
    ).reshape(2, every, attn_rows)
    normed_cols, out_cols = both_cols[0], both_cols[1]
    wout_grad = contract(out_cols, kept_all[:, :q_width], 0, 0)
    context_grad = contract(out_grad_low, w_out, 1, 0)
    context_rows = low(context_grad).reshape(micro, local_len * HEADS, HD)
    prob_grad = batched(context_rows, values_all, 2, 2).reshape(micro, local_len, HEADS, seq_len)
    score_grad = weights * (prob_grad - jnp.sum(weights * prob_grad, axis=-1, keepdims=True))
    score_grad = low(score_grad).reshape(micro, local_len * HEADS, seq_len)
    query_grad = batched(score_grad, keys_all, 2, 1) * score_scale
    query_grad = query_grad.reshape(count, HEADS, HD)
    kv_part = low(
        jnp.concatenate(
            [
                batched(score_grad, queries, 1, 1) * score_scale,
                batched(weights_low, context_rows, 1, 1),
            ],
            axis=2,
        )
    )
    kv_part, _ = lax.optimization_barrier((kv_part, [pair[1] for pair in ffn_parts[4:6]]))
    sums = sum_rows(
        jnp.concatenate(
            [
                low(contract(hidden_act, ffn_weight[:, 2, :], 1, 0)).reshape(
                    micro, seq_len, model_dim
                ),
                low(contract(hidden_act, ffn_adapter, 1, 0)).reshape(micro, seq_len, RANK),
                kv_part,
            ],
            axis=2,
        )
    )
    sums, _ = lax.optimization_barrier((sums, [pair[1] for pair in ffn_parts[6:10]]))
    sums = sums.reshape(count, model_dim + RANK + 2 * HD)
    kv_grad = sums[:, model_dim + RANK :]
    down_low = sums[:, model_dim : model_dim + RANK]
    result = (
        mixed_sum + sums[:, :model_dim].astype(jnp.float32) + contract(down_low, bd_t, 1, 1)
    )
    query_pre_grad = low(rotate(query_grad, -angles[:, None, :]).reshape(count, q_width))
    key_grad = low(rotate(kv_grad[:, :HD].astype(jnp.float32), -angles))
    value_grad = kv_grad[:, HD:]
    rank_grad = low(contract(query_pre_grad, bq_t, 1, 0))
    proj_grad = jnp.concatenate([query_pre_grad, key_grad, value_grad], axis=1)
    normed_grad = contract(proj_grad, w_proj, 1, 1) + contract(rank_grad, a_q, 1, 1)
    hidden_part, gain_one_grad = norm_back_one(normed_grad)
    input_grad = low(mixed_grad + hidden_part)

    narrow = jnp.concatenate([key_grad, value_grad, rank_grad, down_low], axis=1)
    q_all, narrow_all = (
        each.reshape(every, -1)
        for each in gather_all(
            shards,
            4,
            query_pre_grad.reshape(micro, local_len, q_width),
            narrow.reshape(micro, local_len, 2 * HD + 2 * RANK),
        )
    )
    narrow_all, _ = lax.optimization_barrier((narrow_all, [pair[1] for pair in ffn_parts[10:]]))
    my_cols = me * attn_rows
    attn_in = jnp.concatenate(
        [
            contract(normed_cols, q_all, 0, 0),
            contract(normed_cols, narrow_all[:, : 2 * HD + RANK], 0, 0),
        ],
        axis=1,
    )
    bq_grad = contract(
        lax.dynamic_slice_in_dim(q_all, my_cols, attn_rows, 1), kept_all[:, q_width:], 0, 0
    )
    bd_grad = contract(
        lax.dynamic_slice_in_dim(cot_all, my_cols, attn_rows, 1),
        narrow_all[:, 2 * HD + RANK :],
        0,
        0,
    )
    gain_now = jnp.stack([gain_one_grad, gain_two_grad], axis=1).reshape(shards, attn_rows, 2)
    gain_now = lax.all_to_all(gain_now, "fsdp", 0, 0, tiled=True).sum(axis=0)
    tail = low(jnp.concatenate([attn_in, bq_grad, bd_grad], axis=1))
    tail_out = low(wout_grad)
    tail_gain = low(gain_now)

    def total(mine, other):
        return mine.astype(jnp.float32) + other.astype(jnp.float32)

    tail = total(tail, swap_rep(tail))
    tail_out = total(tail_out, swap_rep(tail_out))
    gains_grad = total(tail_gain, swap_rep(tail_gain))
    attn_grad = jnp.concatenate([tail[:, :kv_end], tail_out], axis=1)
    adapter_grad = tail[:, kv_end:]
    ffn_grad = jnp.zeros((3, hidden_cols, model_dim), jnp.float32)
    for at, pair in enumerate(ffn_parts):
        ffn_grad = lax.dynamic_update_slice(
            ffn_grad, total(*pair)[None], (at % 3, at // 3 * step, 0)
        )
    ffn_grad = ffn_grad.transpose(1, 0, 2)
    ffn_low_grad = total(low_mine, swap_rep(low_mine))
    return (
        low(result).reshape(micro, local_len, model_dim),
        input_grad.reshape(micro, local_len, model_dim),
        gains_grad,
        attn_grad,
        adapter_grad,
        ffn_grad,
        ffn_low_grad,
    )


def solution(mesh):
    placed = (
        P("rep", "fsdp", None),
        P("rep", "fsdp"),
        P("fsdp", None),
        P("fsdp", None),
        P("fsdp", None),
        P("fsdp", None, None),
        P("fsdp", None),
        P("rep", "fsdp", None),
    )
    return jax.shard_map(
        local,
        mesh=mesh,
        in_specs=placed,
        out_specs=(
            P("rep", "fsdp", None),
            P("rep", "fsdp", None),
            P("fsdp", None),
            P("fsdp", None),
            P("fsdp", None),
            P("fsdp", None, None),
            P("fsdp", None),
        ),
        check_vma=False,
    )
```

```python
import functools

import jax
import jax.numpy as jnp
from jax import lax
from jax.experimental import pallas as pl
from jax.experimental.pallas import tpu as pltpu
from jax.sharding import PartitionSpec as P

HEADS = 8
HD = 256
RANK = 256
CHUNKS = 1
PIECES = 2
EARLY = 3


epsilon = 1e-06


def rms_scale(values, gain_col):
    return (
        values * lax.rsqrt(jnp.mean(values * values, axis=-1, keepdims=True) + epsilon) * gain_col
    )


def angles_of(positions):
    inverse_freq = 10000.0 ** (-2.0 * jnp.arange(HD // 2, dtype=jnp.float32) / HD)
    return positions.astype(jnp.float32)[..., None] * inverse_freq


def rotate(field_in, angles):
    half_dim = field_in.shape[-1] // 2
    cosine = jnp.cos(angles)
    sine_part = jnp.sin(angles)
    lower_half = field_in[..., :half_dim]
    upper_half = field_in[..., half_dim:]
    return jnp.concatenate(
        [
            lower_half * cosine - upper_half * sine_part,
            upper_half * cosine + lower_half * sine_part,
        ],
        axis=-1,
    )


def gelu_tanh(values):
    return jax.nn.gelu(values, approximate=True)


def contract(left_op, right_op, left_dim, right_dim):
    return lax.dot_general(
        left_op,
        right_op,
        (((left_dim,), (right_dim,)), ((), ())),
        preferred_element_type=jnp.float32,
    )


def batched(left_op, right_op, left_dim, right_dim):
    return lax.dot_general(
        left_op,
        right_op,
        (((left_dim,), (right_dim,)), ((0,), (0,))),
        preferred_element_type=jnp.float32,
    )


def low(values):
    return values.astype(jnp.bfloat16)


def gather_rows(values):
    return lax.all_gather(values, "fsdp", axis=values.ndim - 2, tiled=True)


def sum_rows(values):
    return lax.psum_scatter(values, "fsdp", scatter_dimension=1, tiled=True)


def total(mine, other):
    return mine.astype(jnp.float32) + other.astype(jnp.float32)


def place(whole, at, pair):
    mine, other = pair
    return lax.dynamic_update_slice(
        whole, total(mine, other)[None], (at % 3, at // 3 * mine.shape[0], 0)
    )


def swap_rep(values):
    return lax.ppermute(values, "rep", [(0, 1), (1, 0)])


def grid_of(shards):
    short = 2 if shards <= 16 else 4
    return shards // (2 * short), short


def wire_cost(times, values):
    moved = times * sum(v.size * v.dtype.itemsize for v in values)
    return pl.CostEstimate(flops=0, bytes_accessed=24 * moved + (40 << 20), transcendentals=0)


def unwritten(shape, dtype):
    return pl.pallas_call(
        lambda _: None,
        out_shape=jax.ShapeDtypeStruct(shape, dtype),
        out_specs=pl.BlockSpec(memory_space=pl.ANY),
        name="unwritten",
    )()


def neighbours(shards):
    long_len, short_len = grid_of(shards)
    me = lax.axis_index("fsdp")
    return me, me // (2 * short_len), (me // 2) % short_len, me % 2


def greet(shards, across, everyone=False):
    long_len, short_len = grid_of(shards)
    me, at_long, at_short, core = neighbours(shards)
    barrier = pltpu.get_barrier_semaphore()
    around = [
        (me >= 0, {"fsdp": me + 1 - 2 * core}),
        (at_long > 0, {"fsdp": me - 2 * short_len}),
        (at_long < long_len - 1, {"fsdp": me + 2 * short_len}),
        (at_short > 0, {"fsdp": me - 2}),
        (at_short < short_len - 1, {"fsdp": me + 2}),
    ]
    if everyone:
        around = [(me >= 0, {"fsdp": (me + far) % shards}) for far in range(1, shards)]
    if across:
        around.append((me >= 0, {"rep": 1 - lax.axis_index("rep")}))
    for has, peer in around:
        @pl.when(has)
        def _():
            pl.semaphore_signal(barrier, inc=1, device_id=peer)
    pl.semaphore_wait(barrier, sum(has.astype(jnp.int32) for has, _ in around))


def gather_kernel(shards, widths, shared, spread, *refs):
    long_len, short_len = grid_of(shards)
    count = len(widths)
    total = count + spread
    own = refs[:total]
    out = refs[total : 2 * total]
    send_sem, recv_sem, own_sem, spread_sem = refs[2 * total :]
    me, at_long, at_short, core = neighbours(shards)
    stride = 2 * short_len
    partner = {"fsdp": me + 1 - 2 * core}
    half = shared // 2
    parts = []
    if shared:
        rep = lax.axis_index("rep")
        peer_rep = {"rep": 1 - rep}
        parts.append((0, pl.multiple_of(rep * half, 128), half))
        parts.append((0, shared, widths[0] - shared))
        parts += [(k, 0, widths[k]) for k in range(1, count)]
        other = (0, pl.multiple_of((1 - rep) * half, 128), half)
    else:
        parts += [(k, 0, widths[k]) for k in range(count)]
        other = None
    lanes = list(range(len(parts)))
    away = len(parts)
    if shared:
        parts.append(other)

    def copy(lane, way, slot, peer, fresh):
        k, first, width = parts[lane]
        columns = pl.ds(first, width)
        there = out[k].at[:, slot, :, columns]
        return pltpu.make_async_remote_copy(
            src_ref=own[k].at[:, :, columns] if fresh else there,
            dst_ref=there,
            send_sem=send_sem.at[lane, way, slot],
            recv_sem=recv_sem.at[away if way == 5 else lane, slot],
            device_id=peer,
        )

    greet(shards, bool(shared), bool(spread))
    done = []

    def start(has, which, way, slot, peer, fresh=False):
        @pl.when(has)
        def _():
            for lane in which:
                copy(lane, way, slot, peer, fresh).start()

        done.append((has, which, way, slot, peer, fresh))

    def arrive(has, which, slot):
        @pl.when(has)
        def _():
            for lane in which:
                copy(lane, 0, slot, partner, False).wait_recv()

    late = []

    def got(has, slot):
        if shared:
            start(has, [0], 5, slot, peer_rep)
            late.append((has, slot))
        start(has, lanes, 4, slot, partner)

    def from_across():
        for has, slot in late:
            arrive(has, [away], slot)
            start(has, [away], 4, slot, partner)
        late.clear()

    def spread_short(has, slot, fresh=False):
        start(has & (at_short < short_len - 1), lanes, 2, slot, {"fsdp": me + 2}, fresh)
        start(has & (at_short > 0), lanes, 3, slot, {"fsdp": me - 2}, fresh)

    def short_arrivals(has, line):
        for far in range(1, short_len):
            for sign in (-1, 1):
                source = at_short + sign * far
                ok = has & (source >= 0) & (source < short_len)
                slot = me + 2 * sign * far + (line - at_long) * stride
                arrive(ok, lanes, slot)
                if far < short_len - 1:
                    onward = at_short - sign
                    start(
                        ok & (onward >= 0) & (onward < short_len),
                        lanes,
                        2 if sign < 0 else 3,
                        slot,
                        {"fsdp": me - 2 * sign},
                    )
                got(ok, slot)

    true = me >= 0
    start(at_long < long_len - 1, lanes, 0, me, {"fsdp": me + stride}, True)
    start(at_long > 0, lanes, 1, me, {"fsdp": me - stride}, True)
    spread_short(true, me, True)
    every = list(range(len(parts)))
    start(true, every, 4, me, partner, True)
    mine = [pltpu.make_async_copy(own[k], out[k].at[:, me], own_sem.at[k]) for k in range(count)]

    def share(k, peer, target):
        width = own[k].shape[2] // shards
        columns = pl.ds(pl.multiple_of(peer * width, 128), width)
        return own[k].at[:, :, columns], out[k].at[:, target]

    def dealt(k, far, back):
        peer = (me + far) % shards
        source, target = share(k, me if back else peer, peer if back else me)
        return pltpu.make_async_remote_copy(
            src_ref=source,
            dst_ref=target,
            send_sem=spread_sem.at[k - count, 0, peer],
            recv_sem=spread_sem.at[k - count, 1, peer if back else me],
            device_id={"fsdp": peer},
        )

    for k in range(count, total):
        mine.append(pltpu.make_async_copy(*share(k, me, me), own_sem.at[k]))
        for far in range(1, shards):
            dealt(k, far, False).start()
    for each in mine:
        each.start()
    for far in range(1, long_len):
        for sign in (-1, 1):
            source = at_long + sign * far
            ok = (source >= 0) & (source < long_len)
            slot = me + sign * far * stride
            arrive(ok, lanes, slot)
            onward = at_long - sign
            start(
                ok & (onward >= 0) & (onward < long_len),
                lanes,
                0 if sign < 0 else 1,
                slot,
                {"fsdp": me - sign * stride},
            )
            spread_short(ok, slot)
            got(ok, slot)
        if far == 1:
            short_arrivals(true, at_long)
        else:
            for sign in (-1, 1):
                source = at_long + sign * (far - 1)
                short_arrivals((source >= 0) & (source < long_len), source)
        if far > 1:
            from_across()
    for sign in (-1, 1):
        source = at_long + sign * (long_len - 1)
        short_arrivals((source >= 0) & (source < long_len), source)
    from_across()
    for line in range(long_len):
        for short in range(short_len):
            arrive(true, every, (line * short_len + short) * 2 + 1 - core)
    for has, which, way, slot, peer, fresh in done:
        @pl.when(has)
        def _():
            for lane in which:
                copy(lane, way, slot, peer, fresh).wait_send()
    for k in range(count, total):
        for far in range(1, shards):
            dealt(k, far, True).wait_recv()
            dealt(k, far, False).wait_send()
    for each in mine:
        each.wait()


def gather_all(shards, ident, *values, shared=0, spread=()):
    widths = tuple(v.shape[2] for v in values)
    count = len(values)
    lanes = count + (2 if shared else 0)
    shapes = [(v.shape[0], shards) + v.shape[1:] for v in values]
    dealt = []
    if spread and spread[0].shape[2] % (128 * shards):
        for v in spread:
            each = lax.all_to_all(v, "fsdp", 2, 1, tiled=True)
            dealt.append(each.reshape(v.shape[0], shards, v.shape[1], -1))
        spread = ()
    values = values + tuple(spread)
    shapes += [(v.shape[0], shards, v.shape[1], v.shape[2] // shards) for v in spread]
    results = pl.pallas_call(
        functools.partial(gather_kernel, shards, widths, shared, len(values) - count),
        out_shape=[jax.ShapeDtypeStruct(shape, v.dtype) for shape, v in zip(shapes, values)],
        in_specs=[pl.BlockSpec(memory_space=pltpu.VMEM)] * len(values),
        out_specs=[pl.BlockSpec(memory_space=pl.ANY)] * len(values),
        scratch_shapes=[
            pltpu.SemaphoreType.DMA((lanes, 6, shards)),
            pltpu.SemaphoreType.DMA((lanes, shards)),
            pltpu.SemaphoreType.DMA((len(values),)),
            pltpu.SemaphoreType.DMA((len(spread) + 1, 2, shards)),
        ],
        compiler_params=pltpu.CompilerParams(collective_id=ident, has_side_effects=True),
        cost_estimate=wire_cost(shards, values[:count]),
        name="gather_%d" % ident,
    )(*values)
    return list(results) + dealt


def scatter_kernel(shards, widths, *refs):
    long_len, short_len = grid_of(shards)
    count = len(widths)
    full = refs[:count]
    out = refs[count : 2 * count]
    held, core_in, short_in, long_in, load_sem, core_sem, short_sem, long_sem, done_sem = refs[
        2 * count :
    ]
    me, at_long, at_short, core = neighbours(shards)
    partner = {"fsdp": me + 1 - 2 * core}
    firsts = [sum(widths[:k]) for k in range(count)]

    def index(line, short):
        return line * short_len + short

    def block(k, line, short, side):
        return full[k].at[:, index(line, short) * 2 + side]

    def columns(ref, k):
        return ref.at[:, :, pl.ds(firsts[k], widths[k])]

    order = []
    for far in range(long_len - 1, 0, -1):
        for sign in (-1, 1):
            line = at_long + sign * far
            order.append(((line >= 0) & (line < long_len), line, far, sign))
    order.append((me >= 0, at_long, 0, 0))
    shorts = []
    for far in range(short_len - 1, 0, -1):
        for sign in (-1, 1):
            short = at_short + sign * far
            shorts.append(((short >= 0) & (short < short_len), short, far, sign))
    shorts.append((me >= 0, at_short, 0, 0))

    def to_core(k, line, short):
        return pltpu.make_async_remote_copy(
            src_ref=block(k, line, short, 1 - core),
            dst_ref=columns(core_in.at[index(line, short)], k),
            send_sem=core_sem.at[0, k, index(line, short)],
            recv_sem=core_sem.at[1, k, index(line, short)],
            device_id=partner,
        )

    def load(k, line, short):
        return pltpu.make_async_copy(
            block(k, line, short, core),
            columns(held.at[index(line, short)], k),
            load_sem.at[k, index(line, short)],
        )

    def along_short(line, short, sign):
        return pltpu.make_async_remote_copy(
            src_ref=held.at[index(line, short)],
            dst_ref=short_in.at[(1 - sign) // 2, index(line, short)],
            send_sem=short_sem.at[0, index(line, short)],
            recv_sem=short_sem.at[1 + (1 - sign) // 2, index(line, short)],
            device_id={"fsdp": me + 2 * sign},
        )

    def along_long(line, sign):
        return pltpu.make_async_remote_copy(
            src_ref=held.at[index(line, at_short)],
            dst_ref=long_in.at[(1 - sign) // 2, line],
            send_sem=long_sem.at[0, line],
            recv_sem=long_sem.at[1 + (1 - sign) // 2, line],
            device_id={"fsdp": me + 2 * short_len * sign},
        )

    def add(to_ref, from_ref):
        batch, rows, _ = to_ref.shape
        step = 16

        @pl.loop(0, batch * rows // step)
        def _(at):
            one = at // (rows // step)
            where = pl.ds(pl.multiple_of((at % (rows // step)) * step, step), step)
            to_ref[one, where, :] = (
                to_ref[one, where, :].astype(jnp.float32)
                + from_ref[one, where, :].astype(jnp.float32)
            ).astype(jnp.bfloat16)

    for near, short, far, sign in shorts:
        for has, line, _, _ in order:
            @pl.when(near & has)
            def _():
                for k in range(count):
                    load(k, line, short).start()

    greet(shards, False)
    for near, short, far, sign in shorts:
        for has, line, _, _ in order:
            @pl.when(near & has)
            def _():
                for k in range(count):
                    to_core(k, line, short).start()

    for near, short, far, sign in shorts:
        for has, line, far_line, sign_line in order:
            @pl.when(near & has)
            def _():
                at = index(line, short)
                for k in range(count):
                    load(k, line, short).wait()
                    to_core(k, line, short).wait_recv()
                add(held.at[at], core_in.at[at])
                if far:
                    behind = at_short - sign

                    @pl.when((behind >= 0) & (behind < short_len))
                    def _():
                        along_short(line, short, sign).wait_recv()
                        add(held.at[at], short_in.at[(1 - sign) // 2, at])

                    along_short(line, short, sign).start()
                else:
                    for way in (-1, 1):
                        behind = at_short - way

                        @pl.when((behind >= 0) & (behind < short_len))
                        def _():
                            along_short(line, short, way).wait_recv()
                            add(held.at[at], short_in.at[(1 - way) // 2, at])

                    for way in (-1, 1) if not far_line else (sign_line,):
                        behind = at_long - way

                        @pl.when((behind >= 0) & (behind < long_len))
                        def _():
                            along_long(line, way).wait_recv()
                            add(held.at[at], long_in.at[(1 - way) // 2, line])

                    if far_line:
                        along_long(line, sign_line).start()

    results = [
        pltpu.make_async_copy(columns(held.at[index(at_long, at_short)], k), out[k], done_sem.at[k])
        for k in range(count)
    ]
    for each in results:
        each.start()
    for near, short, far, sign in shorts:
        for has, line, far_line, sign_line in order:
            @pl.when(near & has)
            def _():
                for k in range(count):
                    to_core(k, line, short).wait_send()
                if far:
                    along_short(line, short, sign).wait_send()
                elif far_line:
                    along_long(line, sign_line).wait_send()
    for each in results:
        each.wait()


def scatter_sum(shards, ident, *values):
    batch, _, rows, _ = values[0].shape
    widths = tuple(v.shape[3] for v in values)
    if shards > 16:
        return [
            sum_rows(v.reshape(batch, shards * rows, w)) for v, w in zip(values, widths)
        ]
    count = len(values)
    long_len, short_len = grid_of(shards)
    pairs = shards // 2
    block = (batch, rows, sum(widths))
    return pl.pallas_call(
        functools.partial(scatter_kernel, shards, widths),
        out_shape=[jax.ShapeDtypeStruct((batch, rows, w), jnp.bfloat16) for w in widths],
        in_specs=[pl.BlockSpec(memory_space=pl.ANY)] * count,
        out_specs=[pl.BlockSpec(memory_space=pl.ANY)] * count,
        scratch_shapes=[
            pltpu.VMEM((pairs,) + block, jnp.bfloat16),
            pltpu.VMEM((pairs,) + block, jnp.bfloat16),
            pltpu.VMEM((2, pairs) + block, jnp.bfloat16),
            pltpu.VMEM((2, long_len) + block, jnp.bfloat16),
            pltpu.SemaphoreType.DMA((count, pairs)),
            pltpu.SemaphoreType.DMA((2, count, pairs)),
            pltpu.SemaphoreType.DMA((3, pairs)),
            pltpu.SemaphoreType.DMA((3, long_len)),
            pltpu.SemaphoreType.DMA((count,)),
        ],
        compiler_params=pltpu.CompilerParams(
            collective_id=ident, has_side_effects=True, vmem_limit_bytes=60 << 20
        ),
        cost_estimate=wire_cost(1, values),
        name="scatter_%d" % ident,
    )(*values)


def local(
    tokens, segment_ids, norm_gains, attn_weight, adapter, ffn_weight, ffn_adapter, cotangent
):
    micro, local_len, model_dim = tokens.shape
    shards = lax.axis_size("fsdp")
    me = lax.axis_index("fsdp")
    seq_len = local_len * shards
    offset = me * local_len
    count = micro * local_len
    every = micro * seq_len
    q_width = HEADS * HD
    kv_end = q_width + 2 * HD
    score_scale = HD ** (-0.5)
    hidden_cols = ffn_weight.shape[0]
    attn_rows = attn_weight.shape[0]

    seg_cols = count // attn_rows
    seg_block = low(segment_ids).reshape(attn_rows, seg_cols)
    spare = jnp.zeros((attn_rows, 128 - 2 - seg_cols), jnp.bfloat16)
    small = jnp.concatenate([norm_gains, seg_block, spare], axis=1)
    same = kv_end + 4 * RANK
    attn_all, adapter_all, small_all = gather_all(
        shards, 1, attn_weight[None], adapter[None], small[None], shared=same
    )
    cotangent_now, small_all = lax.optimization_barrier((cotangent, small_all))
    cot_all = gather_rows(cotangent_now).reshape(every, model_dim)
    attn_all = attn_all.reshape(model_dim, attn_weight.shape[1])
    adapter_all = adapter_all.reshape(model_dim, 3 * RANK)
    small_all = small_all.reshape(model_dim, 128)
    w_proj = attn_all[:, :kv_end]
    w_out = attn_all[:, kv_end:]
    a_q, bq_t, bd_t = (adapter_all[:, j * RANK : (j + 1) * RANK] for j in range(3))
    gain_two = small_all[:, :2].astype(jnp.float32)
    seg_all = small_all[:, 2 : 2 + seg_cols].reshape(shards, micro, local_len)
    seg_all = seg_all.transpose(1, 0, 2).reshape(micro, seq_len).astype(jnp.int32)

    hidden_in = tokens.reshape(count, model_dim).astype(jnp.float32)
    key_index = jnp.arange(seq_len, dtype=jnp.int32)
    query_index = offset + jnp.arange(local_len, dtype=jnp.int32)
    before = jnp.sum(
        (seg_all[:, None, :] < segment_ids[:, :, None]).astype(jnp.int32), axis=2
    )
    angles = angles_of(query_index[None, :] - before).reshape(count, HD // 2)
    normed, norm_back_one = jax.vjp(rms_scale, hidden_in, gain_two[:, 0])
    normed_low = low(normed)
    projected = contract(normed_low, w_proj, 1, 0)
    query_low = low(contract(normed_low, a_q, 1, 0))
    query_pre = projected[:, :q_width] + contract(query_low, bq_t, 1, 1)
    queries = low(rotate(query_pre.reshape(count, HEADS, HD), angles[:, None, :]))
    queries = queries.reshape(micro, local_len * HEADS, HD)
    keys_low = low(rotate(projected[:, q_width : q_width + HD], angles))
    values_low = low(projected[:, q_width + HD :])
    keys_all, values_all = (
        each.reshape(micro, seq_len, -1)
        for each in gather_all(
            shards,
            2,
            keys_low.reshape(micro, local_len, HD),
            values_low.reshape(micro, local_len, HD),
        )
    )
    allowed = (
        (segment_ids[:, :, None] == seg_all[:, None, :])
        & (key_index[None, None, :] <= query_index[None, :, None])
    )[:, :, None, :]
    scores = (batched(queries, keys_all, 2, 2) * score_scale).reshape(
        micro, local_len, HEADS, seq_len
    )
    scores = jnp.where(allowed, scores, -1e30)
    top_score = jnp.max(scores, axis=-1, keepdims=True)
    exp_scores = jnp.exp(scores - top_score)
    weights = exp_scores / jnp.sum(exp_scores, axis=-1, keepdims=True)
    weights_low = low(weights).reshape(micro, local_len * HEADS, seq_len)
    context = low(batched(weights_low, values_all, 2, 1)).reshape(count, q_width)
    mixed_sum = hidden_in + contract(context, w_out, 1, 1)
    normed_two, norm_back_two = jax.vjp(rms_scale, mixed_sum, gain_two[:, 1])
    (inputs_all,) = gather_all(shards, 3, low(normed_two).reshape(micro, local_len, model_dim))
    inputs_all = inputs_all.reshape(every, model_dim)
    kept, inputs_all = lax.optimization_barrier(
        (jnp.concatenate([context, query_low], axis=1), inputs_all)
    )
    kept_all = gather_rows(kept.reshape(micro, local_len, q_width + RANK))
    kept_all = kept_all.reshape(every, q_width + RANK)
    low_grad_all = low(contract(cot_all, bd_t, 1, 0))

    step = hidden_cols // CHUNKS
    hidden_parts, gate_parts, up_parts = [], [], []
    for at in range(CHUNKS):
        units = slice(at * step, (at + 1) * step)
        w_gate, w_up, w_down = (ffn_weight[units, j, :] for j in range(3))
        gate_pre = contract(inputs_all, w_gate, 1, 1)
        up_pre = contract(inputs_all, w_up, 1, 1)
        activated, gelu_back = jax.vjp(gelu_tanh, gate_pre)
        hidden_act = low(activated * up_pre)
        hidden_grad = contract(cot_all, w_down, 1, 1) + contract(
            low_grad_all, ffn_adapter[units], 1, 1
        )
        gate_grad = low(gelu_back(hidden_grad * up_pre)[0])
        up_grad = low(hidden_grad * activated)
        hidden_parts.append(hidden_act)
        gate_parts.append(gate_grad)
        up_parts.append(up_grad)

    gate_grad = jnp.concatenate(gate_parts, axis=1)
    up_grad = jnp.concatenate(up_parts, axis=1)
    hidden_act = jnp.concatenate(hidden_parts, axis=1)
    step = hidden_cols // PIECES
    first_mine = low(contract(gate_grad[:, :step], inputs_all, 0, 0))
    down_part = low(contract(hidden_act, ffn_weight[:, 2, :], 1, 0))
    low_part = low(contract(hidden_act, ffn_adapter, 1, 0))
    first_other = swap_rep(first_mine)
    down_part, low_part, gate_grad, up_grad, hidden_act, first_mine = lax.optimization_barrier(
        (down_part, low_part, gate_grad, up_grad, hidden_act, first_mine)
    )
    down_sum = sum_rows(down_part.reshape(micro, seq_len, model_dim))
    ffn_parts = []
    for at in range(PIECES):
        units = slice(at * step, (at + 1) * step)
        for left, right in (
            (gate_grad, inputs_all),
            (up_grad, inputs_all),
            (hidden_act, cot_all),
        ):
            if not ffn_parts:
                ffn_parts.append((first_mine, first_other))
                continue
            mine = low(contract(left[:, units], right, 0, 0))
            ffn_parts.append((mine, swap_rep(mine)))
    low_mine = low(contract(hidden_act, low_grad_all, 0, 0))
    low_other = swap_rep(low_mine)
    gate_grad, up_grad, kept_all, _ = lax.optimization_barrier(
        (
            gate_grad,
            up_grad,
            kept_all,
            [pair[0] for pair in ffn_parts],
        )
    )
    (normed_two_grad,) = scatter_sum(
        shards,
        5,
        low(
            contract(gate_grad, ffn_weight[:, 0, :], 1, 0)
            + contract(up_grad, ffn_weight[:, 1, :], 1, 0)
        ).reshape(micro, shards, local_len, model_dim),
    )
    normed_two_grad, down_sum, _ = lax.optimization_barrier(
        (normed_two_grad, down_sum, [pair[1] for pair in ffn_parts[:2]])
    )
    normed_two_grad = normed_two_grad.reshape(count, model_dim).astype(jnp.float32)
    cot_full = cotangent.reshape(count, model_dim).astype(jnp.float32)
    mixed_part, gain_two_grad = norm_back_two(normed_two_grad)
    mixed_grad = cot_full + mixed_part
    out_grad_low = low(mixed_grad)
    context_grad = contract(out_grad_low, w_out, 1, 0)
    context_rows = low(context_grad).reshape(micro, local_len * HEADS, HD)
    prob_grad = batched(context_rows, values_all, 2, 2).reshape(micro, local_len, HEADS, seq_len)
    score_grad = weights * (prob_grad - jnp.sum(weights * prob_grad, axis=-1, keepdims=True))
    score_grad = low(score_grad).reshape(micro, local_len * HEADS, seq_len)
    query_grad = batched(score_grad, keys_all, 2, 1) * score_scale
    query_grad = query_grad.reshape(count, HEADS, HD)
    query_pre_grad = low(rotate(query_grad, -angles[:, None, :]).reshape(count, q_width))
    key_part = low(batched(score_grad, queries, 1, 1) * score_scale)
    value_part = low(batched(weights_low, context_rows, 1, 1))
    ffn_grad = unwritten((3, hidden_cols, model_dim), jnp.float32)
    for at in range(EARLY):
        ffn_grad = place(ffn_grad, at, ffn_parts[at])
    key_part, value_part, query_pre_grad, ffn_grad, ffn_parts[3:4] = lax.optimization_barrier(
        (key_part, value_part, query_pre_grad, ffn_grad, ffn_parts[3:4])
    )
    q_all = gather_rows(query_pre_grad.reshape(micro, local_len, q_width))
    q_all = q_all.reshape(every, q_width)
    key_sum, value_sum, down_low = (
        each.reshape(count, -1)
        for each in scatter_sum(
            shards,
            6,
            *(
                each.reshape(micro, shards, local_len, -1)
                for each in (key_part, value_part, low_part)
            ),
        )
    )
    result = (
        mixed_sum
        + down_sum.reshape(count, model_dim).astype(jnp.float32)
        + contract(down_low, bd_t, 1, 1)
    )
    key_grad = low(rotate(key_sum.astype(jnp.float32), -angles))
    value_grad = value_sum
    rank_grad = low(contract(query_pre_grad, bq_t, 1, 0))
    proj_grad = jnp.concatenate([query_pre_grad, key_grad, value_grad], axis=1)
    normed_grad = contract(proj_grad, w_proj, 1, 1) + contract(rank_grad, a_q, 1, 1)
    hidden_part, gain_one_grad = norm_back_one(normed_grad)
    input_grad = low(mixed_grad + hidden_part)

    narrow = jnp.concatenate([key_grad, value_grad, rank_grad, down_low], axis=1)
    narrow, ffn_parts[3:5] = lax.optimization_barrier((narrow, ffn_parts[3:5]))
    gain_parts = jnp.zeros((1, 16, model_dim), jnp.bfloat16)
    gain_parts = gain_parts.at[0, 0].set(low(gain_one_grad)).at[0, 1].set(low(gain_two_grad))
    narrow_all, normed_cols, out_cols, gain_cols = gather_all(
        shards,
        4,
        narrow.reshape(micro, local_len, 2 * HD + 2 * RANK),
        spread=(
            normed_low.reshape(micro, local_len, model_dim),
            out_grad_low.reshape(micro, local_len, model_dim),
            gain_parts,
        ),
    )
    narrow_all = narrow_all.reshape(every, 2 * HD + 2 * RANK)
    normed_cols = normed_cols.reshape(every, attn_rows)
    wout_grad = contract(out_cols.reshape(every, attn_rows), kept_all[:, :q_width], 0, 0)
    gain_now = jnp.sum(gain_cols[0, :, :2].astype(jnp.float32), axis=0)
    my_cols = me * attn_rows
    attn_q = low(contract(normed_cols, q_all, 0, 0))
    attn_rest = contract(normed_cols, narrow_all[:, : 2 * HD + RANK], 0, 0)
    bq_grad = contract(
        lax.dynamic_slice_in_dim(q_all, my_cols, attn_rows, 1), kept_all[:, q_width:], 0, 0
    )
    bd_grad = contract(
        lax.dynamic_slice_in_dim(cot_all, my_cols, attn_rows, 1),
        narrow_all[:, 2 * HD + RANK :],
        0,
        0,
    )
    tail = low(jnp.concatenate([attn_rest, bq_grad, bd_grad], axis=1))
    tail_out = low(wout_grad)
    tail_gain = low(gain_now)
    crossing = [swap_rep(each) for each in (tail_out, tail, attn_q)]
    attn_q, tail, tail_out, ffn_parts[3:], low_mine, low_other = lax.optimization_barrier(
        (attn_q, tail, tail_out, ffn_parts[3:], low_mine, low_other)
    )
    gains_grad = total(tail_gain, swap_rep(tail_gain)).transpose(1, 0)
    for at in range(EARLY, 3 * PIECES):
        ffn_grad = place(ffn_grad, at, ffn_parts[at])
    ffn_grad = ffn_grad.transpose(1, 0, 2)
    ffn_low_grad = total(low_mine, low_other)
    tail = total(tail, crossing[1])
    attn_grad = unwritten(attn_weight.shape, jnp.float32)
    for first, part in (
        (kv_end, total(tail_out, crossing[0])),
        (q_width, tail[:, : 2 * HD]),
        (0, total(attn_q, crossing[2])),
    ):
        attn_grad = lax.dynamic_update_slice(attn_grad, part, (0, first))
    adapter_grad = tail[:, 2 * HD :]
    return (
        low(result).reshape(micro, local_len, model_dim),
        input_grad.reshape(micro, local_len, model_dim),
        gains_grad,
        attn_grad,
        adapter_grad,
        ffn_grad,
        ffn_low_grad,
    )


def solution(mesh):
    placed = (
        P("rep", "fsdp", None),
        P("rep", "fsdp"),
        P("fsdp", None),
        P("fsdp", None),
        P("fsdp", None),
        P("fsdp", None, None),
        P("fsdp", None),
        P("rep", "fsdp", None),
    )
    return jax.shard_map(
        local,
        mesh=mesh,
        in_specs=placed,
        out_specs=(
            P("rep", "fsdp", None),
            P("rep", "fsdp", None),
            P("fsdp", None),
            P("fsdp", None),
            P("fsdp", None),
            P("fsdp", None, None),
            P("fsdp", None),
        ),
        check_vma=False,
    )
```

```python
import functools

import jax
import jax.numpy as jnp
from jax import lax
from jax.experimental import pallas as pl
from jax.experimental.pallas import tpu as pltpu
from jax.sharding import PartitionSpec as P

HEADS = 8
HD = 256
RANK = 256
CHUNKS = 1
PIECES = 2
EARLY = 3


epsilon = 1e-06


def rms_scale(values, gain_col):
    return (
        values * lax.rsqrt(jnp.mean(values * values, axis=-1, keepdims=True) + epsilon) * gain_col
    )


def angles_of(positions):
    inverse_freq = 10000.0 ** (-2.0 * jnp.arange(HD // 2, dtype=jnp.float32) / HD)
    return positions.astype(jnp.float32)[..., None] * inverse_freq


def rotate(field_in, angles):
    half_dim = field_in.shape[-1] // 2
    cosine = jnp.cos(angles)
    sine_part = jnp.sin(angles)
    lower_half = field_in[..., :half_dim]
    upper_half = field_in[..., half_dim:]
    return jnp.concatenate(
        [
            lower_half * cosine - upper_half * sine_part,
            upper_half * cosine + lower_half * sine_part,
        ],
        axis=-1,
    )


def gelu_tanh(values):
    return jax.nn.gelu(values, approximate=True)


def contract(left_op, right_op, left_dim, right_dim):
    return lax.dot_general(
        left_op,
        right_op,
        (((left_dim,), (right_dim,)), ((), ())),
        preferred_element_type=jnp.float32,
    )


def batched(left_op, right_op, left_dim, right_dim):
    return lax.dot_general(
        left_op,
        right_op,
        (((left_dim,), (right_dim,)), ((0,), (0,))),
        preferred_element_type=jnp.float32,
    )


def low(values):
    return values.astype(jnp.bfloat16)


def gather_rows(values):
    return lax.all_gather(values, "fsdp", axis=values.ndim - 2, tiled=True)


def sum_rows(values):
    return lax.psum_scatter(values, "fsdp", scatter_dimension=1, tiled=True)


def total(mine, other):
    return mine.astype(jnp.float32) + other.astype(jnp.float32)


def place(whole, at, pair):
    mine, other = pair
    return lax.dynamic_update_slice(
        whole, total(mine, other)[None], (at % 3, at // 3 * mine.shape[0], 0)
    )


def swap_rep(values):
    return lax.ppermute(values, "rep", [(0, 1), (1, 0)])


def grid_of(shards):
    short = 2 if shards <= 16 else 4
    return shards // (2 * short), short


def wire_cost(times, values):
    moved = times * sum(v.size * v.dtype.itemsize for v in values)
    return pl.CostEstimate(flops=0, bytes_accessed=24 * moved + (40 << 20), transcendentals=0)


def unwritten(shape, dtype):
    return pl.pallas_call(
        lambda _: None,
        out_shape=jax.ShapeDtypeStruct(shape, dtype),
        out_specs=pl.BlockSpec(memory_space=pl.ANY),
        name="unwritten",
    )()


def neighbours(shards):
    long_len, short_len = grid_of(shards)
    me = lax.axis_index("fsdp")
    return me, me // (2 * short_len), (me // 2) % short_len, me % 2


def greet(shards, across, everyone=False):
    long_len, short_len = grid_of(shards)
    me, at_long, at_short, core = neighbours(shards)
    barrier = pltpu.get_barrier_semaphore()
    around = [
        (me >= 0, {"fsdp": me + 1 - 2 * core}),
        (at_long > 0, {"fsdp": me - 2 * short_len}),
        (at_long < long_len - 1, {"fsdp": me + 2 * short_len}),
        (at_short > 0, {"fsdp": me - 2}),
        (at_short < short_len - 1, {"fsdp": me + 2}),
    ]
    if everyone:
        around = [(me >= 0, {"fsdp": (me + far) % shards}) for far in range(1, shards)]
    if across:
        around.append((me >= 0, {"rep": 1 - lax.axis_index("rep")}))
    for has, peer in around:
        @pl.when(has)
        def _():
            pl.semaphore_signal(barrier, inc=1, device_id=peer)
    pl.semaphore_wait(barrier, sum(has.astype(jnp.int32) for has, _ in around))


def gather_kernel(shards, widths, shared, spread, *refs):
    long_len, short_len = grid_of(shards)
    count = len(widths)
    total = count + spread
    own = refs[:total]
    out = refs[total : 2 * total]
    send_sem, recv_sem, own_sem, spread_sem = refs[2 * total :]
    me, at_long, at_short, core = neighbours(shards)
    stride = 2 * short_len
    partner = {"fsdp": me + 1 - 2 * core}
    half = shared // 2
    parts = []
    if shared:
        rep = lax.axis_index("rep")
        peer_rep = {"rep": 1 - rep}
        parts.append((0, pl.multiple_of(rep * half, 128), half))
        parts.append((0, shared, widths[0] - shared))
        parts += [(k, 0, widths[k]) for k in range(1, count)]
        other = (0, pl.multiple_of((1 - rep) * half, 128), half)
    else:
        parts += [(k, 0, widths[k]) for k in range(count)]
        other = None
    lanes = list(range(len(parts)))
    away = len(parts)
    if shared:
        parts.append(other)

    def copy(lane, way, slot, peer, fresh):
        k, first, width = parts[lane]
        columns = pl.ds(first, width)
        there = out[k].at[:, slot, :, columns]
        return pltpu.make_async_remote_copy(
            src_ref=own[k].at[:, :, columns] if fresh else there,
            dst_ref=there,
            send_sem=send_sem.at[lane, way, slot],
            recv_sem=recv_sem.at[away if way == 5 else lane, slot],
            device_id=peer,
        )

    greet(shards, bool(shared), bool(spread))
    done = []

    def start(has, which, way, slot, peer, fresh=False):
        @pl.when(has)
        def _():
            for lane in which:
                copy(lane, way, slot, peer, fresh).start()

        done.append((has, which, way, slot, peer, fresh))

    def arrive(has, which, slot):
        @pl.when(has)
        def _():
            for lane in which:
                copy(lane, 0, slot, partner, False).wait_recv()

    late = []

    def got(has, slot):
        if shared:
            start(has, [0], 5, slot, peer_rep)
            late.append((has, slot))
        start(has, lanes, 4, slot, partner)

    def from_across():
        for has, slot in late:
            arrive(has, [away], slot)
            start(has, [away], 4, slot, partner)
        late.clear()

    def spread_short(has, slot, fresh=False):
        start(has & (at_short < short_len - 1), lanes, 2, slot, {"fsdp": me + 2}, fresh)
        start(has & (at_short > 0), lanes, 3, slot, {"fsdp": me - 2}, fresh)

    def short_arrivals(has, line):
        for far in range(1, short_len):
            for sign in (-1, 1):
                source = at_short + sign * far
                ok = has & (source >= 0) & (source < short_len)
                slot = me + 2 * sign * far + (line - at_long) * stride
                arrive(ok, lanes, slot)
                if far < short_len - 1:
                    onward = at_short - sign
                    start(
                        ok & (onward >= 0) & (onward < short_len),
                        lanes,
                        2 if sign < 0 else 3,
                        slot,
                        {"fsdp": me - 2 * sign},
                    )
                got(ok, slot)

    true = me >= 0
    start(at_long < long_len - 1, lanes, 0, me, {"fsdp": me + stride}, True)
    start(at_long > 0, lanes, 1, me, {"fsdp": me - stride}, True)
    spread_short(true, me, True)
    every = list(range(len(parts)))
    start(true, every, 4, me, partner, True)
    mine = [pltpu.make_async_copy(own[k], out[k].at[:, me], own_sem.at[k]) for k in range(count)]

    def share(k, peer, target):
        width = own[k].shape[2] // shards
        columns = pl.ds(pl.multiple_of(peer * width, 128), width)
        return own[k].at[:, :, columns], out[k].at[:, target]

    def dealt(k, far, back):
        peer = (me + far) % shards
        source, target = share(k, me if back else peer, peer if back else me)
        return pltpu.make_async_remote_copy(
            src_ref=source,
            dst_ref=target,
            send_sem=spread_sem.at[k - count, 0, peer],
            recv_sem=spread_sem.at[k - count, 1, peer if back else me],
            device_id={"fsdp": peer},
        )

    for k in range(count, total):
        mine.append(pltpu.make_async_copy(*share(k, me, me), own_sem.at[k]))
        for far in range(1, shards):
            dealt(k, far, False).start()
    for each in mine:
        each.start()
    for far in range(1, long_len):
        for sign in (-1, 1):
            source = at_long + sign * far
            ok = (source >= 0) & (source < long_len)
            slot = me + sign * far * stride
            arrive(ok, lanes, slot)
            onward = at_long - sign
            start(
                ok & (onward >= 0) & (onward < long_len),
                lanes,
                0 if sign < 0 else 1,
                slot,
                {"fsdp": me - sign * stride},
            )
            spread_short(ok, slot)
            got(ok, slot)
        if far == 1:
            short_arrivals(true, at_long)
        else:
            for sign in (-1, 1):
                source = at_long + sign * (far - 1)
                short_arrivals((source >= 0) & (source < long_len), source)
        if far > 1:
            from_across()
    for sign in (-1, 1):
        source = at_long + sign * (long_len - 1)
        short_arrivals((source >= 0) & (source < long_len), source)
    from_across()
    for line in range(long_len):
        for short in range(short_len):
            arrive(true, every, (line * short_len + short) * 2 + 1 - core)
    for has, which, way, slot, peer, fresh in done:
        @pl.when(has)
        def _():
            for lane in which:
                copy(lane, way, slot, peer, fresh).wait_send()
    for k in range(count, total):
        for far in range(1, shards):
            dealt(k, far, True).wait_recv()
            dealt(k, far, False).wait_send()
    for each in mine:
        each.wait()


def gather_all(shards, ident, *values, shared=0, spread=()):
    widths = tuple(v.shape[2] for v in values)
    count = len(values)
    lanes = count + (2 if shared else 0)
    shapes = [(v.shape[0], shards) + v.shape[1:] for v in values]
    dealt = []
    if spread and spread[0].shape[2] % (128 * shards):
        for v in spread:
            each = lax.all_to_all(v, "fsdp", 2, 1, tiled=True)
            dealt.append(each.reshape(v.shape[0], shards, v.shape[1], -1))
        spread = ()
    values = values + tuple(spread)
    shapes += [(v.shape[0], shards, v.shape[1], v.shape[2] // shards) for v in spread]
    results = pl.pallas_call(
        functools.partial(gather_kernel, shards, widths, shared, len(values) - count),
        out_shape=[jax.ShapeDtypeStruct(shape, v.dtype) for shape, v in zip(shapes, values)],
        in_specs=[pl.BlockSpec(memory_space=pltpu.VMEM)] * len(values),
        out_specs=[pl.BlockSpec(memory_space=pl.ANY)] * len(values),
        scratch_shapes=[
            pltpu.SemaphoreType.DMA((lanes, 6, shards)),
            pltpu.SemaphoreType.DMA((lanes, shards)),
            pltpu.SemaphoreType.DMA((len(values),)),
            pltpu.SemaphoreType.DMA((len(spread) + 1, 2, shards)),
        ],
        compiler_params=pltpu.CompilerParams(collective_id=ident, has_side_effects=True),
        cost_estimate=wire_cost(shards, values[:count]),
        name="gather_%d" % ident,
    )(*values)
    return list(results) + dealt


def scatter_kernel(shards, widths, *refs):
    long_len, short_len = grid_of(shards)
    count = len(widths)
    full = refs[:count]
    out = refs[count : 2 * count]
    held, core_in, short_in, long_in, load_sem, core_sem, short_sem, long_sem, done_sem = refs[
        2 * count :
    ]
    me, at_long, at_short, core = neighbours(shards)
    partner = {"fsdp": me + 1 - 2 * core}
    firsts = [sum(widths[:k]) for k in range(count)]

    def index(line, short):
        return line * short_len + short

    def block(k, line, short, side):
        return full[k].at[:, index(line, short) * 2 + side]

    def columns(ref, k):
        return ref.at[:, :, pl.ds(firsts[k], widths[k])]

    order = []
    for far in range(long_len - 1, 0, -1):
        for sign in (-1, 1):
            line = at_long + sign * far
            order.append(((line >= 0) & (line < long_len), line, far, sign))
    order.append((me >= 0, at_long, 0, 0))
    shorts = []
    for far in range(short_len - 1, 0, -1):
        for sign in (-1, 1):
            short = at_short + sign * far
            shorts.append(((short >= 0) & (short < short_len), short, far, sign))
    shorts.append((me >= 0, at_short, 0, 0))

    def to_core(k, line, short):
        return pltpu.make_async_remote_copy(
            src_ref=block(k, line, short, 1 - core),
            dst_ref=columns(core_in.at[index(line, short)], k),
            send_sem=core_sem.at[0, k, index(line, short)],
            recv_sem=core_sem.at[1, k, index(line, short)],
            device_id=partner,
        )

    def load(k, line, short):
        return pltpu.make_async_copy(
            block(k, line, short, core),
            columns(held.at[index(line, short)], k),
            load_sem.at[k, index(line, short)],
        )

    def along_short(line, short, sign):
        return pltpu.make_async_remote_copy(
            src_ref=held.at[index(line, short)],
            dst_ref=short_in.at[(1 - sign) // 2, index(line, short)],
            send_sem=short_sem.at[0, index(line, short)],
            recv_sem=short_sem.at[1 + (1 - sign) // 2, index(line, short)],
            device_id={"fsdp": me + 2 * sign},
        )

    def along_long(line, sign):
        return pltpu.make_async_remote_copy(
            src_ref=held.at[index(line, at_short)],
            dst_ref=long_in.at[(1 - sign) // 2, line],
            send_sem=long_sem.at[0, line],
            recv_sem=long_sem.at[1 + (1 - sign) // 2, line],
            device_id={"fsdp": me + 2 * short_len * sign},
        )

    def add(to_ref, from_ref):
        batch, rows, _ = to_ref.shape
        step = 16

        @pl.loop(0, batch * rows // step)
        def _(at):
            one = at // (rows // step)
            where = pl.ds(pl.multiple_of((at % (rows // step)) * step, step), step)
            to_ref[one, where, :] = (
                to_ref[one, where, :].astype(jnp.float32)
                + from_ref[one, where, :].astype(jnp.float32)
            ).astype(jnp.bfloat16)

    for near, short, far, sign in shorts:
        for has, line, _, _ in order:
            @pl.when(near & has)
            def _():
                for k in range(count):
                    load(k, line, short).start()

    greet(shards, False)
    for near, short, far, sign in shorts:
        for has, line, _, _ in order:
            @pl.when(near & has)
            def _():
                for k in range(count):
                    to_core(k, line, short).start()

    for near, short, far, sign in shorts:
        for has, line, far_line, sign_line in order:
            @pl.when(near & has)
            def _():
                at = index(line, short)
                for k in range(count):
                    load(k, line, short).wait()
                    to_core(k, line, short).wait_recv()
                add(held.at[at], core_in.at[at])
                if far:
                    behind = at_short - sign

                    @pl.when((behind >= 0) & (behind < short_len))
                    def _():
                        along_short(line, short, sign).wait_recv()
                        add(held.at[at], short_in.at[(1 - sign) // 2, at])

                    along_short(line, short, sign).start()
                else:
                    for way in (-1, 1):
                        behind = at_short - way

                        @pl.when((behind >= 0) & (behind < short_len))
                        def _():
                            along_short(line, short, way).wait_recv()
                            add(held.at[at], short_in.at[(1 - way) // 2, at])

                    for way in (-1, 1) if not far_line else (sign_line,):
                        behind = at_long - way

                        @pl.when((behind >= 0) & (behind < long_len))
                        def _():
                            along_long(line, way).wait_recv()
                            add(held.at[at], long_in.at[(1 - way) // 2, line])

                    if far_line:
                        along_long(line, sign_line).start()

    results = [
        pltpu.make_async_copy(columns(held.at[index(at_long, at_short)], k), out[k], done_sem.at[k])
        for k in range(count)
    ]
    for each in results:
        each.start()
    for near, short, far, sign in shorts:
        for has, line, far_line, sign_line in order:
            @pl.when(near & has)
            def _():
                for k in range(count):
                    to_core(k, line, short).wait_send()
                if far:
                    along_short(line, short, sign).wait_send()
                elif far_line:
                    along_long(line, sign_line).wait_send()
    for each in results:
        each.wait()


def scatter_sum(shards, ident, *values):
    batch, _, rows, _ = values[0].shape
    widths = tuple(v.shape[3] for v in values)
    if shards > 16:
        return [
            sum_rows(v.reshape(batch, shards * rows, w)) for v, w in zip(values, widths)
        ]
    count = len(values)
    long_len, short_len = grid_of(shards)
    pairs = shards // 2
    block = (batch, rows, sum(widths))
    return pl.pallas_call(
        functools.partial(scatter_kernel, shards, widths),
        out_shape=[jax.ShapeDtypeStruct((batch, rows, w), jnp.bfloat16) for w in widths],
        in_specs=[pl.BlockSpec(memory_space=pl.ANY)] * count,
        out_specs=[pl.BlockSpec(memory_space=pl.ANY)] * count,
        scratch_shapes=[
            pltpu.VMEM((pairs,) + block, jnp.bfloat16),
            pltpu.VMEM((pairs,) + block, jnp.bfloat16),
            pltpu.VMEM((2, pairs) + block, jnp.bfloat16),
            pltpu.VMEM((2, long_len) + block, jnp.bfloat16),
            pltpu.SemaphoreType.DMA((count, pairs)),
            pltpu.SemaphoreType.DMA((2, count, pairs)),
            pltpu.SemaphoreType.DMA((3, pairs)),
            pltpu.SemaphoreType.DMA((3, long_len)),
            pltpu.SemaphoreType.DMA((count,)),
        ],
        compiler_params=pltpu.CompilerParams(
            collective_id=ident, has_side_effects=True, vmem_limit_bytes=60 << 20
        ),
        cost_estimate=wire_cost(1, values),
        name="scatter_%d" % ident,
    )(*values)


def product_kernel(shards, gate, up, weight, out, *scratch):
    planes, pair, core_in, short_in, long_in = scratch[:5]
    plane_sem, core_sem, short_sem, long_sem, done_sem = scratch[5:]
    long_len, _ = grid_of(shards)
    me, at_long, at_short, core = neighbours(shards)
    rows = pair.shape[3]
    load = pltpu.make_async_copy(weight.at[pl.ds(0, 2)], planes, plane_sem)
    load.start()

    lines = []
    first, last = me * 0, me * 0 + long_len - 1
    for _ in range(long_len - 1):
        up_side = (last - at_long >= at_long - first).astype(jnp.int32)
        lines.append((first + up_side * (last - first), 2 * up_side - 1))
        first, last = first + 1 - up_side, last - up_side
    lines.append((at_long, None))
    steps = [(line, sign, 1 - at_short) for line, sign in lines]
    steps += [(line, sign, at_short) for line, sign in lines]

    def held(at):
        return pair.at[at, :, core]

    def compute(at):
        where = pl.ds(pl.multiple_of(at * 2 * rows, 2 * rows), 2 * rows)
        left = gate[:, where, :].reshape(4 * rows, gate.shape[2])
        right = up[:, where, :].reshape(4 * rows, up.shape[2])

        @pl.loop(0, pair.shape[4] // 512)
        def _(tile):
            columns = pl.ds(pl.multiple_of(tile * 512, 512), 512)
            sums = jnp.dot(left, planes[0, :, columns], preferred_element_type=jnp.float32)
            sums += jnp.dot(right, planes[1, :, columns], preferred_element_type=jnp.float32)
            pair[at, :, :, :, columns] = sums.astype(jnp.bfloat16).reshape(2, 2, rows, 512)

    def to_core(at):
        return pltpu.make_async_remote_copy(
            src_ref=pair.at[at, :, 1 - core],
            dst_ref=core_in.at[at],
            send_sem=core_sem.at[0, at],
            recv_sem=core_sem.at[1, at],
            device_id={"fsdp": me + 1 - 2 * core},
        )

    def along_short(line, short):
        return pltpu.make_async_remote_copy(
            src_ref=held(line * 2 + short),
            dst_ref=short_in.at[line],
            send_sem=short_sem.at[0, line],
            recv_sem=short_sem.at[1, line],
            device_id={"fsdp": me + 2 - 4 * at_short},
        )

    def along_long(line, sign):
        return pltpu.make_async_remote_copy(
            src_ref=held(line * 2 + at_short),
            dst_ref=long_in.at[(1 - sign) // 2, line],
            send_sem=long_sem.at[0, line],
            recv_sem=long_sem.at[1 + (1 - sign) // 2, line],
            device_id={"fsdp": me + 4 * sign},
        )

    def add(at, other):
        @pl.loop(0, 2 * rows // 16)
        def _(group):
            one = group // (rows // 16)
            where = pl.ds(pl.multiple_of((group % (rows // 16)) * 16, 16), 16)
            pair[at, one, core, where, :] = (
                pair[at, one, core, where, :].astype(jnp.float32)
                + other[one, where, :].astype(jnp.float32)
            ).astype(jnp.bfloat16)

    def from_behind(at, line, sign):
        behind = at_long - sign

        @pl.when((behind >= 0) & (behind < long_len))
        def _():
            along_long(line, sign).wait_recv()
            add(at, long_in.at[(1 - sign) // 2, line])

    def settle(at_step):
        line, sign, short = steps[at_step]
        at = line * 2 + short
        to_core(at).wait_recv()
        add(at, core_in.at[at])
        if at_step < long_len:
            along_short(line, short).start()
            return
        along_short(line, short).wait_recv()
        add(at, short_in.at[line])
        if sign is None:
            from_behind(at, line, 1)
            from_behind(at, line, -1)
        else:
            from_behind(at, line, sign)
            along_long(line, sign).start()

    greet(shards, False)
    load.wait()
    for at_step, (line, _, short) in enumerate(steps):
        compute(line * 2 + short)
        to_core(line * 2 + short).start()
        if at_step:
            settle(at_step - 1)
    settle(len(steps) - 1)
    result = pltpu.make_async_copy(held(at_long * 2 + at_short), out, done_sem)
    result.start()
    for at_step, (line, sign, short) in enumerate(steps):
        to_core(line * 2 + short).wait_send()
        if at_step < long_len:
            along_short(line, short).wait_send()
        elif sign is not None:
            along_long(line, sign).wait_send()
    result.wait()


def product_sum(shards, ident, gate, up, weight):
    batch, every, units = gate.shape
    columns = weight.shape[2]
    rows = every // shards
    long_len, short_len = grid_of(shards)
    block = (batch, rows, columns)
    pairs = shards // 2
    return pl.pallas_call(
        functools.partial(product_kernel, shards),
        out_shape=jax.ShapeDtypeStruct(block, jnp.bfloat16),
        in_specs=[
            pl.BlockSpec(memory_space=pltpu.VMEM),
            pl.BlockSpec(memory_space=pltpu.VMEM),
            pl.BlockSpec(memory_space=pl.ANY),
        ],
        out_specs=pl.BlockSpec(memory_space=pl.ANY),
        scratch_shapes=[
            pltpu.VMEM((2, units, columns), jnp.bfloat16),
            pltpu.VMEM((pairs, batch, 2, rows, columns), jnp.bfloat16),
            pltpu.VMEM((pairs,) + block, jnp.bfloat16),
            pltpu.VMEM((long_len,) + block, jnp.bfloat16),
            pltpu.VMEM((2, long_len) + block, jnp.bfloat16),
            pltpu.SemaphoreType.DMA,
            pltpu.SemaphoreType.DMA((2, pairs)),
            pltpu.SemaphoreType.DMA((2, long_len)),
            pltpu.SemaphoreType.DMA((3, long_len)),
            pltpu.SemaphoreType.DMA,
        ],
        compiler_params=pltpu.CompilerParams(
            collective_id=ident, has_side_effects=True, vmem_limit_bytes=60 << 20
        ),
        cost_estimate=wire_cost(shards, [jax.ShapeDtypeStruct(block, jnp.bfloat16)]),
        name="product_%d" % ident,
    )(gate, up, weight)


def local(
    tokens, segment_ids, norm_gains, attn_weight, adapter, ffn_weight, ffn_adapter, cotangent
):
    micro, local_len, model_dim = tokens.shape
    shards = lax.axis_size("fsdp")
    me = lax.axis_index("fsdp")
    seq_len = local_len * shards
    offset = me * local_len
    count = micro * local_len
    every = micro * seq_len
    q_width = HEADS * HD
    kv_end = q_width + 2 * HD
    score_scale = HD ** (-0.5)
    hidden_cols = ffn_weight.shape[0]
    attn_rows = attn_weight.shape[0]

    seg_cols = count // attn_rows
    seg_block = low(segment_ids).reshape(attn_rows, seg_cols)
    spare = jnp.zeros((attn_rows, 128 - 2 - seg_cols), jnp.bfloat16)
    small = jnp.concatenate([norm_gains, seg_block, spare], axis=1)
    same = kv_end + 4 * RANK
    attn_all, adapter_all, small_all = gather_all(
        shards, 1, attn_weight[None], adapter[None], small[None], shared=same
    )
    cotangent_now, small_all = lax.optimization_barrier((cotangent, small_all))
    cot_all = gather_rows(cotangent_now).reshape(every, model_dim)
    attn_all = attn_all.reshape(model_dim, attn_weight.shape[1])
    adapter_all = adapter_all.reshape(model_dim, 3 * RANK)
    small_all = small_all.reshape(model_dim, 128)
    w_proj = attn_all[:, :kv_end]
    w_out = attn_all[:, kv_end:]
    a_q, bq_t, bd_t = (adapter_all[:, j * RANK : (j + 1) * RANK] for j in range(3))
    gain_two = small_all[:, :2].astype(jnp.float32)
    seg_all = small_all[:, 2 : 2 + seg_cols].reshape(shards, micro, local_len)
    seg_all = seg_all.transpose(1, 0, 2).reshape(micro, seq_len).astype(jnp.int32)

    hidden_in = tokens.reshape(count, model_dim).astype(jnp.float32)
    key_index = jnp.arange(seq_len, dtype=jnp.int32)
    query_index = offset + jnp.arange(local_len, dtype=jnp.int32)
    before = jnp.sum(
        (seg_all[:, None, :] < segment_ids[:, :, None]).astype(jnp.int32), axis=2
    )
    angles = angles_of(query_index[None, :] - before).reshape(count, HD // 2)
    normed, norm_back_one = jax.vjp(rms_scale, hidden_in, gain_two[:, 0])
    normed_low = low(normed)
    projected = contract(normed_low, w_proj, 1, 0)
    query_low = low(contract(normed_low, a_q, 1, 0))
    query_pre = projected[:, :q_width] + contract(query_low, bq_t, 1, 1)
    queries = low(rotate(query_pre.reshape(count, HEADS, HD), angles[:, None, :]))
    queries = queries.reshape(micro, local_len * HEADS, HD)
    keys_low = low(rotate(projected[:, q_width : q_width + HD], angles))
    values_low = low(projected[:, q_width + HD :])
    keys_all, values_all = (
        each.reshape(micro, seq_len, -1)
        for each in gather_all(
            shards,
            2,
            keys_low.reshape(micro, local_len, HD),
            values_low.reshape(micro, local_len, HD),
        )
    )
    allowed = (
        (segment_ids[:, :, None] == seg_all[:, None, :])
        & (key_index[None, None, :] <= query_index[None, :, None])
    )[:, :, None, :]
    scores = (batched(queries, keys_all, 2, 2) * score_scale).reshape(
        micro, local_len, HEADS, seq_len
    )
    scores = jnp.where(allowed, scores, -1e30)
    top_score = jnp.max(scores, axis=-1, keepdims=True)
    exp_scores = jnp.exp(scores - top_score)
    weights = exp_scores / jnp.sum(exp_scores, axis=-1, keepdims=True)
    weights_low = low(weights).reshape(micro, local_len * HEADS, seq_len)
    context = low(batched(weights_low, values_all, 2, 1)).reshape(count, q_width)
    mixed_sum = hidden_in + contract(context, w_out, 1, 1)
    normed_two, norm_back_two = jax.vjp(rms_scale, mixed_sum, gain_two[:, 1])
    (inputs_all,) = gather_all(shards, 3, low(normed_two).reshape(micro, local_len, model_dim))
    inputs_all = inputs_all.reshape(every, model_dim)
    kept, inputs_all = lax.optimization_barrier(
        (jnp.concatenate([context, query_low], axis=1), inputs_all)
    )
    kept_all = gather_rows(kept.reshape(micro, local_len, q_width + RANK))
    kept_all = kept_all.reshape(every, q_width + RANK)
    low_grad_all = low(contract(cot_all, bd_t, 1, 0))

    step = hidden_cols // CHUNKS
    hidden_parts, gate_parts, up_parts = [], [], []
    for at in range(CHUNKS):
        units = slice(at * step, (at + 1) * step)
        w_gate, w_up, w_down = (ffn_weight[units, j, :] for j in range(3))
        gate_pre = contract(inputs_all, w_gate, 1, 1)
        up_pre = contract(inputs_all, w_up, 1, 1)
        activated, gelu_back = jax.vjp(gelu_tanh, gate_pre)
        hidden_act = low(activated * up_pre)
        hidden_grad = contract(cot_all, w_down, 1, 1) + contract(
            low_grad_all, ffn_adapter[units], 1, 1
        )
        gate_grad = low(gelu_back(hidden_grad * up_pre)[0])
        up_grad = low(hidden_grad * activated)
        hidden_parts.append(hidden_act)
        gate_parts.append(gate_grad)
        up_parts.append(up_grad)

    gate_grad = jnp.concatenate(gate_parts, axis=1)
    up_grad = jnp.concatenate(up_parts, axis=1)
    hidden_act = jnp.concatenate(hidden_parts, axis=1)
    step = hidden_cols // PIECES
    first_mine = low(contract(gate_grad[:, :step], inputs_all, 0, 0))
    down_part = low(contract(hidden_act, ffn_weight[:, 2, :], 1, 0))
    low_part = low(contract(hidden_act, ffn_adapter, 1, 0))
    first_other = swap_rep(first_mine)
    down_part, low_part, gate_grad, up_grad, hidden_act, first_mine = lax.optimization_barrier(
        (down_part, low_part, gate_grad, up_grad, hidden_act, first_mine)
    )
    down_sum = sum_rows(down_part.reshape(micro, seq_len, model_dim))
    ffn_parts = []
    for at in range(PIECES):
        units = slice(at * step, (at + 1) * step)
        for left, right in (
            (gate_grad, inputs_all),
            (up_grad, inputs_all),
            (hidden_act, cot_all),
        ):
            if not ffn_parts:
                ffn_parts.append((first_mine, first_other))
                continue
            mine = low(contract(left[:, units], right, 0, 0))
            ffn_parts.append((mine, swap_rep(mine)))
    low_mine = low(contract(hidden_act, low_grad_all, 0, 0))
    low_other = swap_rep(low_mine)
    gate_grad, up_grad, kept_all, _ = lax.optimization_barrier(
        (
            gate_grad,
            up_grad,
            kept_all,
            [pair[0] for pair in ffn_parts],
        )
    )
    if grid_of(shards)[1] == 2 and micro == 2:
        normed_two_grad = product_sum(
            shards,
            5,
            gate_grad.reshape(micro, seq_len, hidden_cols),
            up_grad.reshape(micro, seq_len, hidden_cols),
            ffn_weight.transpose(1, 0, 2),
        )
    else:
        (normed_two_grad,) = scatter_sum(
            shards,
            5,
            low(
                contract(gate_grad, ffn_weight[:, 0, :], 1, 0)
                + contract(up_grad, ffn_weight[:, 1, :], 1, 0)
            ).reshape(micro, shards, local_len, model_dim),
        )
    normed_two_grad, down_sum, _ = lax.optimization_barrier(
        (normed_two_grad, down_sum, [pair[1] for pair in ffn_parts[:2]])
    )
    normed_two_grad = normed_two_grad.reshape(count, model_dim).astype(jnp.float32)
    cot_full = cotangent.reshape(count, model_dim).astype(jnp.float32)
    mixed_part, gain_two_grad = norm_back_two(normed_two_grad)
    mixed_grad = cot_full + mixed_part
    out_grad_low = low(mixed_grad)
    context_grad = contract(out_grad_low, w_out, 1, 0)
    context_rows = low(context_grad).reshape(micro, local_len * HEADS, HD)
    prob_grad = batched(context_rows, values_all, 2, 2).reshape(micro, local_len, HEADS, seq_len)
    score_grad = weights * (prob_grad - jnp.sum(weights * prob_grad, axis=-1, keepdims=True))
    score_grad = low(score_grad).reshape(micro, local_len * HEADS, seq_len)
    query_grad = batched(score_grad, keys_all, 2, 1) * score_scale
    query_grad = query_grad.reshape(count, HEADS, HD)
    query_pre_grad = low(rotate(query_grad, -angles[:, None, :]).reshape(count, q_width))
    key_part = low(batched(score_grad, queries, 1, 1) * score_scale)
    value_part = low(batched(weights_low, context_rows, 1, 1))
    ffn_grad = unwritten((3, hidden_cols, model_dim), jnp.float32)
    for at in range(EARLY):
        ffn_grad = place(ffn_grad, at, ffn_parts[at])
    key_part, value_part, query_pre_grad, ffn_grad, ffn_parts[3:4] = lax.optimization_barrier(
        (key_part, value_part, query_pre_grad, ffn_grad, ffn_parts[3:4])
    )
    q_all = gather_rows(query_pre_grad.reshape(micro, local_len, q_width))
    q_all = q_all.reshape(every, q_width)
    key_sum, value_sum, down_low = (
        each.reshape(count, -1)
        for each in scatter_sum(
            shards,
            6,
            *(
                each.reshape(micro, shards, local_len, -1)
                for each in (key_part, value_part, low_part)
            ),
        )
    )
    result = (
        mixed_sum
        + down_sum.reshape(count, model_dim).astype(jnp.float32)
        + contract(down_low, bd_t, 1, 1)
    )
    key_grad = low(rotate(key_sum.astype(jnp.float32), -angles))
    value_grad = value_sum
    rank_grad = low(contract(query_pre_grad, bq_t, 1, 0))
    proj_grad = jnp.concatenate([query_pre_grad, key_grad, value_grad], axis=1)
    normed_grad = contract(proj_grad, w_proj, 1, 1) + contract(rank_grad, a_q, 1, 1)
    hidden_part, gain_one_grad = norm_back_one(normed_grad)
    input_grad = low(mixed_grad + hidden_part)

    narrow = jnp.concatenate([key_grad, value_grad, rank_grad, down_low], axis=1)
    narrow, ffn_parts[3:5] = lax.optimization_barrier((narrow, ffn_parts[3:5]))
    gain_parts = jnp.zeros((1, 16, model_dim), jnp.bfloat16)
    gain_parts = gain_parts.at[0, 0].set(low(gain_one_grad)).at[0, 1].set(low(gain_two_grad))
    narrow_all, normed_cols, out_cols, gain_cols = gather_all(
        shards,
        4,
        narrow.reshape(micro, local_len, 2 * HD + 2 * RANK),
        spread=(
            normed_low.reshape(micro, local_len, model_dim),
            out_grad_low.reshape(micro, local_len, model_dim),
            gain_parts,
        ),
    )
    narrow_all = narrow_all.reshape(every, 2 * HD + 2 * RANK)
    normed_cols = normed_cols.reshape(every, attn_rows)
    wout_grad = contract(out_cols.reshape(every, attn_rows), kept_all[:, :q_width], 0, 0)
    gain_now = jnp.sum(gain_cols[0, :, :2].astype(jnp.float32), axis=0)
    my_cols = me * attn_rows
    attn_q = low(contract(normed_cols, q_all, 0, 0))
    attn_rest = contract(normed_cols, narrow_all[:, : 2 * HD + RANK], 0, 0)
    bq_grad = contract(
        lax.dynamic_slice_in_dim(q_all, my_cols, attn_rows, 1), kept_all[:, q_width:], 0, 0
    )
    bd_grad = contract(
        lax.dynamic_slice_in_dim(cot_all, my_cols, attn_rows, 1),
        narrow_all[:, 2 * HD + RANK :],
        0,
        0,
    )
    tail = low(jnp.concatenate([attn_rest, bq_grad, bd_grad], axis=1))
    tail_out = low(wout_grad)
    tail_gain = low(gain_now)
    crossing = [swap_rep(each) for each in (tail_out, tail, attn_q)]
    attn_q, tail, tail_out, ffn_parts[3:], low_mine, low_other = lax.optimization_barrier(
        (attn_q, tail, tail_out, ffn_parts[3:], low_mine, low_other)
    )
    gains_grad = total(tail_gain, swap_rep(tail_gain)).transpose(1, 0)
    for at in range(EARLY, 3 * PIECES):
        ffn_grad = place(ffn_grad, at, ffn_parts[at])
    ffn_grad = ffn_grad.transpose(1, 0, 2)
    ffn_low_grad = total(low_mine, low_other)
    tail = total(tail, crossing[1])
    attn_grad = unwritten(attn_weight.shape, jnp.float32)
    for first, part in (
        (kv_end, total(tail_out, crossing[0])),
        (q_width, tail[:, : 2 * HD]),
        (0, total(attn_q, crossing[2])),
    ):
        attn_grad = lax.dynamic_update_slice(attn_grad, part, (0, first))
    adapter_grad = tail[:, 2 * HD :]
    return (
        low(result).reshape(micro, local_len, model_dim),
        input_grad.reshape(micro, local_len, model_dim),
        gains_grad,
        attn_grad,
        adapter_grad,
        ffn_grad,
        ffn_low_grad,
    )


def solution(mesh):
    placed = (
        P("rep", "fsdp", None),
        P("rep", "fsdp"),
        P("fsdp", None),
        P("fsdp", None),
        P("fsdp", None),
        P("fsdp", None, None),
        P("fsdp", None),
        P("rep", "fsdp", None),
    )
    return jax.shard_map(
        local,
        mesh=mesh,
        in_specs=placed,
        out_specs=(
            P("rep", "fsdp", None),
            P("rep", "fsdp", None),
            P("fsdp", None),
            P("fsdp", None),
            P("fsdp", None),
            P("fsdp", None, None),
            P("fsdp", None),
        ),
        check_vma=False,
    )
```

```python
import functools

import jax
import jax.numpy as jnp
from jax import lax
from jax.experimental import pallas as pl
from jax.experimental.pallas import tpu as pltpu
from jax.sharding import PartitionSpec as P

HEADS = 8
HD = 256
RANK = 256
CHUNKS = 1
PIECES = 2


epsilon = 1e-06


def rms_scale(values, gain_col):
    return (
        values * lax.rsqrt(jnp.mean(values * values, axis=-1, keepdims=True) + epsilon) * gain_col
    )


def angles_of(positions):
    inverse_freq = 10000.0 ** (-2.0 * jnp.arange(HD // 2, dtype=jnp.float32) / HD)
    return positions.astype(jnp.float32)[..., None] * inverse_freq


def rotate(field_in, angles):
    half_dim = field_in.shape[-1] // 2
    cosine = jnp.cos(angles)
    sine_part = jnp.sin(angles)
    lower_half = field_in[..., :half_dim]
    upper_half = field_in[..., half_dim:]
    return jnp.concatenate(
        [
            lower_half * cosine - upper_half * sine_part,
            upper_half * cosine + lower_half * sine_part,
        ],
        axis=-1,
    )


def gelu_tanh(values):
    return jax.nn.gelu(values, approximate=True)


def contract(left_op, right_op, left_dim, right_dim):
    return lax.dot_general(
        left_op,
        right_op,
        (((left_dim,), (right_dim,)), ((), ())),
        preferred_element_type=jnp.float32,
    )


def batched(left_op, right_op, left_dim, right_dim):
    return lax.dot_general(
        left_op,
        right_op,
        (((left_dim,), (right_dim,)), ((0,), (0,))),
        preferred_element_type=jnp.float32,
    )


def low(values):
    return values.astype(jnp.bfloat16)


def gather_rows(values):
    return lax.all_gather(values, "fsdp", axis=values.ndim - 2, tiled=True)


def sum_rows(values):
    return lax.psum_scatter(values, "fsdp", scatter_dimension=1, tiled=True)


def total(mine, other):
    return mine.astype(jnp.float32) + other.astype(jnp.float32)


def place_kernel(kinds, *refs):
    out = refs[-1]
    for kind in range(kinds):

        @pl.when(pl.program_id(0) == kind)
        def _():
            mine, other = refs[2 * kind], refs[2 * kind + 1]
            out[0] = total(mine[...], other[...])


def place(whole, group, groups, pairs):
    kinds = len(pairs)
    rows, columns = pairs[0][0].shape
    tile = min(rows, 128)
    tiles = rows // tile

    def part(kind):
        return pl.BlockSpec(
            (tile, columns),
            lambda k, j: (jnp.where(k == kind, j, jnp.where(k < kind, 0, tiles - 1)), 0),
        )

    in_specs = [part(kind) for kind in range(kinds) for _ in range(2)]
    operands = [each for pair in pairs for each in pair]
    aliases = {}
    if whole is not None:
        aliases = {len(operands): 0}
        in_specs.append(pl.BlockSpec(memory_space=pl.ANY))
        operands.append(whole)
    moved = kinds * rows * columns
    return pl.pallas_call(
        functools.partial(place_kernel, kinds),
        grid=(kinds, tiles),
        out_shape=jax.ShapeDtypeStruct((kinds, groups * rows, columns), jnp.float32),
        in_specs=in_specs,
        out_specs=pl.BlockSpec((1, tile, columns), lambda k, j: (k, group * tiles + j, 0)),
        input_output_aliases=aliases,
        cost_estimate=pl.CostEstimate(flops=moved, bytes_accessed=8 * moved, transcendentals=0),
        compiler_params=pltpu.CompilerParams(vmem_limit_bytes=24 << 20),
        name="place_%d" % group,
    )(*operands)


def swap_rep(values):
    return lax.ppermute(values, "rep", [(0, 1), (1, 0)])


def grid_of(shards):
    short = 2 if shards <= 16 else 4
    return shards // (2 * short), short


def wire_cost(times, values):
    moved = times * sum(v.size * v.dtype.itemsize for v in values)
    return pl.CostEstimate(flops=0, bytes_accessed=24 * moved + (40 << 20), transcendentals=0)


def unwritten(shape, dtype):
    return pl.pallas_call(
        lambda _: None,
        out_shape=jax.ShapeDtypeStruct(shape, dtype),
        out_specs=pl.BlockSpec(memory_space=pl.ANY),
        name="unwritten",
    )()


def neighbours(shards):
    long_len, short_len = grid_of(shards)
    me = lax.axis_index("fsdp")
    return me, me // (2 * short_len), (me // 2) % short_len, me % 2


def greet(shards, across, everyone=False):
    long_len, short_len = grid_of(shards)
    me, at_long, at_short, core = neighbours(shards)
    barrier = pltpu.get_barrier_semaphore()
    around = [
        (me >= 0, {"fsdp": me + 1 - 2 * core}),
        (at_long > 0, {"fsdp": me - 2 * short_len}),
        (at_long < long_len - 1, {"fsdp": me + 2 * short_len}),
        (at_short > 0, {"fsdp": me - 2}),
        (at_short < short_len - 1, {"fsdp": me + 2}),
    ]
    if everyone:
        around = [(me >= 0, {"fsdp": (me + far) % shards}) for far in range(1, shards)]
    if across:
        around.append((me >= 0, {"rep": 1 - lax.axis_index("rep")}))
    for has, peer in around:
        @pl.when(has)
        def _():
            pl.semaphore_signal(barrier, inc=1, device_id=peer)
    pl.semaphore_wait(barrier, sum(has.astype(jnp.int32) for has, _ in around))


def gather_kernel(shards, widths, shared, spread, *refs):
    long_len, short_len = grid_of(shards)
    count = len(widths)
    total = count + spread
    own = refs[:total]
    out = refs[total : 2 * total]
    send_sem, recv_sem, own_sem, spread_sem = refs[2 * total :]
    me, at_long, at_short, core = neighbours(shards)
    stride = 2 * short_len
    partner = {"fsdp": me + 1 - 2 * core}
    half = shared // 2
    parts = []
    if shared:
        rep = lax.axis_index("rep")
        peer_rep = {"rep": 1 - rep}
        parts.append((0, pl.multiple_of(rep * half, 128), half))
        parts.append((0, shared, widths[0] - shared))
        parts += [(k, 0, widths[k]) for k in range(1, count)]
        other = (0, pl.multiple_of((1 - rep) * half, 128), half)
    else:
        parts += [(k, 0, widths[k]) for k in range(count)]
        other = None
    lanes = list(range(len(parts)))
    away = len(parts)
    if shared:
        parts.append(other)

    def copy(lane, way, slot, peer, fresh):
        k, first, width = parts[lane]
        columns = pl.ds(first, width)
        there = out[k].at[:, slot, :, columns]
        return pltpu.make_async_remote_copy(
            src_ref=own[k].at[:, :, columns] if fresh else there,
            dst_ref=there,
            send_sem=send_sem.at[lane, way, slot],
            recv_sem=recv_sem.at[away if way == 5 else lane, slot],
            device_id=peer,
        )

    greet(shards, bool(shared), bool(spread))
    done = []

    def start(has, which, way, slot, peer, fresh=False):
        @pl.when(has)
        def _():
            for lane in which:
                copy(lane, way, slot, peer, fresh).start()

        done.append((has, which, way, slot, peer, fresh))

    def arrive(has, which, slot):
        @pl.when(has)
        def _():
            for lane in which:
                copy(lane, 0, slot, partner, False).wait_recv()

    late = []

    def got(has, slot):
        if shared:
            start(has, [0], 5, slot, peer_rep)
            late.append((has, slot))
        start(has, lanes, 4, slot, partner)

    def from_across():
        for has, slot in late:
            arrive(has, [away], slot)
            start(has, [away], 4, slot, partner)
        late.clear()

    def spread_short(has, slot, fresh=False):
        start(has & (at_short < short_len - 1), lanes, 2, slot, {"fsdp": me + 2}, fresh)
        start(has & (at_short > 0), lanes, 3, slot, {"fsdp": me - 2}, fresh)

    def short_arrivals(has, line):
        for far in range(1, short_len):
            for sign in (-1, 1):
                source = at_short + sign * far
                ok = has & (source >= 0) & (source < short_len)
                slot = me + 2 * sign * far + (line - at_long) * stride
                arrive(ok, lanes, slot)
                if far < short_len - 1:
                    onward = at_short - sign
                    start(
                        ok & (onward >= 0) & (onward < short_len),
                        lanes,
                        2 if sign < 0 else 3,
                        slot,
                        {"fsdp": me - 2 * sign},
                    )
                got(ok, slot)

    true = me >= 0
    start(at_long < long_len - 1, lanes, 0, me, {"fsdp": me + stride}, True)
    start(at_long > 0, lanes, 1, me, {"fsdp": me - stride}, True)
    spread_short(true, me, True)
    every = list(range(len(parts)))
    start(true, every, 4, me, partner, True)
    mine = [pltpu.make_async_copy(own[k], out[k].at[:, me], own_sem.at[k]) for k in range(count)]

    def share(k, peer, target):
        width = own[k].shape[2] // shards
        columns = pl.ds(pl.multiple_of(peer * width, 128), width)
        return own[k].at[:, :, columns], out[k].at[:, target]

    def dealt(k, far, back):
        peer = (me + far) % shards
        source, target = share(k, me if back else peer, peer if back else me)
        return pltpu.make_async_remote_copy(
            src_ref=source,
            dst_ref=target,
            send_sem=spread_sem.at[k - count, 0, peer],
            recv_sem=spread_sem.at[k - count, 1, peer if back else me],
            device_id={"fsdp": peer},
        )

    for k in range(count, total):
        mine.append(pltpu.make_async_copy(*share(k, me, me), own_sem.at[k]))
        for far in range(1, shards):
            dealt(k, far, False).start()
    for each in mine:
        each.start()
    for far in range(1, long_len):
        for sign in (-1, 1):
            source = at_long + sign * far
            ok = (source >= 0) & (source < long_len)
            slot = me + sign * far * stride
            arrive(ok, lanes, slot)
            onward = at_long - sign
            start(
                ok & (onward >= 0) & (onward < long_len),
                lanes,
                0 if sign < 0 else 1,
                slot,
                {"fsdp": me - sign * stride},
            )
            spread_short(ok, slot)
            got(ok, slot)
        if far == 1:
            short_arrivals(true, at_long)
        else:
            for sign in (-1, 1):
                source = at_long + sign * (far - 1)
                short_arrivals((source >= 0) & (source < long_len), source)
        if far > 1:
            from_across()
    for sign in (-1, 1):
        source = at_long + sign * (long_len - 1)
        short_arrivals((source >= 0) & (source < long_len), source)
    from_across()
    for line in range(long_len):
        for short in range(short_len):
            arrive(true, every, (line * short_len + short) * 2 + 1 - core)
    for has, which, way, slot, peer, fresh in done:
        @pl.when(has)
        def _():
            for lane in which:
                copy(lane, way, slot, peer, fresh).wait_send()
    for k in range(count, total):
        for far in range(1, shards):
            dealt(k, far, True).wait_recv()
            dealt(k, far, False).wait_send()
    for each in mine:
        each.wait()


def gather_all(shards, ident, *values, shared=0, spread=()):
    widths = tuple(v.shape[2] for v in values)
    count = len(values)
    lanes = count + (2 if shared else 0)
    shapes = [(v.shape[0], shards) + v.shape[1:] for v in values]
    dealt = []
    if spread and spread[0].shape[2] % (128 * shards):
        for v in spread:
            each = lax.all_to_all(v, "fsdp", 2, 1, tiled=True)
            dealt.append(each.reshape(v.shape[0], shards, v.shape[1], -1))
        spread = ()
    values = values + tuple(spread)
    shapes += [(v.shape[0], shards, v.shape[1], v.shape[2] // shards) for v in spread]
    results = pl.pallas_call(
        functools.partial(gather_kernel, shards, widths, shared, len(values) - count),
        out_shape=[jax.ShapeDtypeStruct(shape, v.dtype) for shape, v in zip(shapes, values)],
        in_specs=[pl.BlockSpec(memory_space=pltpu.VMEM)] * len(values),
        out_specs=[pl.BlockSpec(memory_space=pl.ANY)] * len(values),
        scratch_shapes=[
            pltpu.SemaphoreType.DMA((lanes, 6, shards)),
            pltpu.SemaphoreType.DMA((lanes, shards)),
            pltpu.SemaphoreType.DMA((len(values),)),
            pltpu.SemaphoreType.DMA((len(spread) + 1, 2, shards)),
        ],
        compiler_params=pltpu.CompilerParams(collective_id=ident, has_side_effects=True),
        cost_estimate=wire_cost(shards, values[:count]),
        name="gather_%d" % ident,
    )(*values)
    return list(results) + dealt


def scatter_kernel(shards, widths, *refs):
    long_len, short_len = grid_of(shards)
    count = len(widths)
    full = refs[:count]
    out = refs[count : 2 * count]
    held, core_in, short_in, long_in, load_sem, core_sem, short_sem, long_sem, done_sem = refs[
        2 * count :
    ]
    me, at_long, at_short, core = neighbours(shards)
    partner = {"fsdp": me + 1 - 2 * core}
    firsts = [sum(widths[:k]) for k in range(count)]

    def index(line, short):
        return line * short_len + short

    def block(k, line, short, side):
        return full[k].at[:, index(line, short) * 2 + side]

    def columns(ref, k):
        return ref.at[:, :, pl.ds(firsts[k], widths[k])]

    order = []
    for far in range(long_len - 1, 0, -1):
        for sign in (-1, 1):
            line = at_long + sign * far
            order.append(((line >= 0) & (line < long_len), line, far, sign))
    order.append((me >= 0, at_long, 0, 0))
    shorts = []
    for far in range(short_len - 1, 0, -1):
        for sign in (-1, 1):
            short = at_short + sign * far
            shorts.append(((short >= 0) & (short < short_len), short, far, sign))
    shorts.append((me >= 0, at_short, 0, 0))

    def to_core(k, line, short):
        return pltpu.make_async_remote_copy(
            src_ref=block(k, line, short, 1 - core),
            dst_ref=columns(core_in.at[index(line, short)], k),
            send_sem=core_sem.at[0, k, index(line, short)],
            recv_sem=core_sem.at[1, k, index(line, short)],
            device_id=partner,
        )

    def load(k, line, short):
        return pltpu.make_async_copy(
            block(k, line, short, core),
            columns(held.at[index(line, short)], k),
            load_sem.at[k, index(line, short)],
        )

    def along_short(line, short, sign):
        return pltpu.make_async_remote_copy(
            src_ref=held.at[index(line, short)],
            dst_ref=short_in.at[(1 - sign) // 2, index(line, short)],
            send_sem=short_sem.at[0, index(line, short)],
            recv_sem=short_sem.at[1 + (1 - sign) // 2, index(line, short)],
            device_id={"fsdp": me + 2 * sign},
        )

    def along_long(line, sign):
        return pltpu.make_async_remote_copy(
            src_ref=held.at[index(line, at_short)],
            dst_ref=long_in.at[(1 - sign) // 2, line],
            send_sem=long_sem.at[0, line],
            recv_sem=long_sem.at[1 + (1 - sign) // 2, line],
            device_id={"fsdp": me + 2 * short_len * sign},
        )

    def add(to_ref, from_ref):
        batch, rows, _ = to_ref.shape
        step = 16

        @pl.loop(0, batch * rows // step)
        def _(at):
            one = at // (rows // step)
            where = pl.ds(pl.multiple_of((at % (rows // step)) * step, step), step)
            to_ref[one, where, :] = (
                to_ref[one, where, :].astype(jnp.float32)
                + from_ref[one, where, :].astype(jnp.float32)
            ).astype(jnp.bfloat16)

    for near, short, far, sign in shorts:
        for has, line, _, _ in order:
            @pl.when(near & has)
            def _():
                for k in range(count):
                    load(k, line, short).start()

    greet(shards, False)
    for near, short, far, sign in shorts:
        for has, line, _, _ in order:
            @pl.when(near & has)
            def _():
                for k in range(count):
                    to_core(k, line, short).start()

    for near, short, far, sign in shorts:
        for has, line, far_line, sign_line in order:
            @pl.when(near & has)
            def _():
                at = index(line, short)
                for k in range(count):
                    load(k, line, short).wait()
                    to_core(k, line, short).wait_recv()
                add(held.at[at], core_in.at[at])
                if far:
                    behind = at_short - sign

                    @pl.when((behind >= 0) & (behind < short_len))
                    def _():
                        along_short(line, short, sign).wait_recv()
                        add(held.at[at], short_in.at[(1 - sign) // 2, at])

                    along_short(line, short, sign).start()
                else:
                    for way in (-1, 1):
                        behind = at_short - way

                        @pl.when((behind >= 0) & (behind < short_len))
                        def _():
                            along_short(line, short, way).wait_recv()
                            add(held.at[at], short_in.at[(1 - way) // 2, at])

                    for way in (-1, 1) if not far_line else (sign_line,):
                        behind = at_long - way

                        @pl.when((behind >= 0) & (behind < long_len))
                        def _():
                            along_long(line, way).wait_recv()
                            add(held.at[at], long_in.at[(1 - way) // 2, line])

                    if far_line:
                        along_long(line, sign_line).start()

    results = [
        pltpu.make_async_copy(columns(held.at[index(at_long, at_short)], k), out[k], done_sem.at[k])
        for k in range(count)
    ]
    for each in results:
        each.start()
    for near, short, far, sign in shorts:
        for has, line, far_line, sign_line in order:
            @pl.when(near & has)
            def _():
                for k in range(count):
                    to_core(k, line, short).wait_send()
                if far:
                    along_short(line, short, sign).wait_send()
                elif far_line:
                    along_long(line, sign_line).wait_send()
    for each in results:
        each.wait()


def scatter_sum(shards, ident, *values):
    batch, _, rows, _ = values[0].shape
    widths = tuple(v.shape[3] for v in values)
    if shards > 16:
        return [
            sum_rows(v.reshape(batch, shards * rows, w)) for v, w in zip(values, widths)
        ]
    count = len(values)
    long_len, short_len = grid_of(shards)
    pairs = shards // 2
    block = (batch, rows, sum(widths))
    return pl.pallas_call(
        functools.partial(scatter_kernel, shards, widths),
        out_shape=[jax.ShapeDtypeStruct((batch, rows, w), jnp.bfloat16) for w in widths],
        in_specs=[pl.BlockSpec(memory_space=pl.ANY)] * count,
        out_specs=[pl.BlockSpec(memory_space=pl.ANY)] * count,
        scratch_shapes=[
            pltpu.VMEM((pairs,) + block, jnp.bfloat16),
            pltpu.VMEM((pairs,) + block, jnp.bfloat16),
            pltpu.VMEM((2, pairs) + block, jnp.bfloat16),
            pltpu.VMEM((2, long_len) + block, jnp.bfloat16),
            pltpu.SemaphoreType.DMA((count, pairs)),
            pltpu.SemaphoreType.DMA((2, count, pairs)),
            pltpu.SemaphoreType.DMA((3, pairs)),
            pltpu.SemaphoreType.DMA((3, long_len)),
            pltpu.SemaphoreType.DMA((count,)),
        ],
        compiler_params=pltpu.CompilerParams(
            collective_id=ident, has_side_effects=True, vmem_limit_bytes=60 << 20
        ),
        cost_estimate=wire_cost(1, values),
        name="scatter_%d" % ident,
    )(*values)


def product_kernel(shards, gate, up, weight, out, *scratch):
    planes, pair, core_in, short_in, long_in = scratch[:5]
    plane_sem, core_sem, short_sem, long_sem, done_sem = scratch[5:]
    long_len, _ = grid_of(shards)
    me, at_long, at_short, core = neighbours(shards)
    rows = pair.shape[3]
    load = pltpu.make_async_copy(weight.at[pl.ds(0, 2)], planes, plane_sem)
    load.start()

    lines = []
    first, last = me * 0, me * 0 + long_len - 1
    for _ in range(long_len - 1):
        up_side = (last - at_long >= at_long - first).astype(jnp.int32)
        lines.append((first + up_side * (last - first), 2 * up_side - 1))
        first, last = first + 1 - up_side, last - up_side
    lines.append((at_long, None))
    steps = [(line, sign, 1 - at_short) for line, sign in lines]
    steps += [(line, sign, at_short) for line, sign in lines]

    def held(at):
        return pair.at[at, :, core]

    def compute(at):
        where = pl.ds(pl.multiple_of(at * 2 * rows, 2 * rows), 2 * rows)
        left = gate[:, where, :].reshape(4 * rows, gate.shape[2])
        right = up[:, where, :].reshape(4 * rows, up.shape[2])

        @pl.loop(0, pair.shape[4] // 512)
        def _(tile):
            columns = pl.ds(pl.multiple_of(tile * 512, 512), 512)
            sums = jnp.dot(left, planes[0, :, columns], preferred_element_type=jnp.float32)
            sums += jnp.dot(right, planes[1, :, columns], preferred_element_type=jnp.float32)
            pair[at, :, :, :, columns] = sums.astype(jnp.bfloat16).reshape(2, 2, rows, 512)

    def to_core(at):
        return pltpu.make_async_remote_copy(
            src_ref=pair.at[at, :, 1 - core],
            dst_ref=core_in.at[at],
            send_sem=core_sem.at[0, at],
            recv_sem=core_sem.at[1, at],
            device_id={"fsdp": me + 1 - 2 * core},
        )

    def along_short(line, short):
        return pltpu.make_async_remote_copy(
            src_ref=held(line * 2 + short),
            dst_ref=short_in.at[line],
            send_sem=short_sem.at[0, line],
            recv_sem=short_sem.at[1, line],
            device_id={"fsdp": me + 2 - 4 * at_short},
        )

    def along_long(line, sign):
        return pltpu.make_async_remote_copy(
            src_ref=held(line * 2 + at_short),
            dst_ref=long_in.at[(1 - sign) // 2, line],
            send_sem=long_sem.at[0, line],
            recv_sem=long_sem.at[1 + (1 - sign) // 2, line],
            device_id={"fsdp": me + 4 * sign},
        )

    def add(at, other):
        @pl.loop(0, 2 * rows // 16)
        def _(group):
            one = group // (rows // 16)
            where = pl.ds(pl.multiple_of((group % (rows // 16)) * 16, 16), 16)
            pair[at, one, core, where, :] = (
                pair[at, one, core, where, :].astype(jnp.float32)
                + other[one, where, :].astype(jnp.float32)
            ).astype(jnp.bfloat16)

    def from_behind(at, line, sign):
        behind = at_long - sign

        @pl.when((behind >= 0) & (behind < long_len))
        def _():
            along_long(line, sign).wait_recv()
            add(at, long_in.at[(1 - sign) // 2, line])

    def settle(at_step):
        line, sign, short = steps[at_step]
        at = line * 2 + short
        to_core(at).wait_recv()
        add(at, core_in.at[at])
        if at_step < long_len:
            along_short(line, short).start()
            return
        along_short(line, short).wait_recv()
        add(at, short_in.at[line])
        if sign is None:
            from_behind(at, line, 1)
            from_behind(at, line, -1)
        else:
            from_behind(at, line, sign)
            along_long(line, sign).start()

    greet(shards, False)
    load.wait()
    for at_step, (line, _, short) in enumerate(steps):
        compute(line * 2 + short)
        to_core(line * 2 + short).start()
        if at_step:
            settle(at_step - 1)
    settle(len(steps) - 1)
    result = pltpu.make_async_copy(held(at_long * 2 + at_short), out, done_sem)
    result.start()
    for at_step, (line, sign, short) in enumerate(steps):
        to_core(line * 2 + short).wait_send()
        if at_step < long_len:
            along_short(line, short).wait_send()
        elif sign is not None:
            along_long(line, sign).wait_send()
    result.wait()


def product_sum(shards, ident, gate, up, weight):
    batch, every, units = gate.shape
    columns = weight.shape[2]
    rows = every // shards
    long_len, short_len = grid_of(shards)
    block = (batch, rows, columns)
    pairs = shards // 2
    return pl.pallas_call(
        functools.partial(product_kernel, shards),
        out_shape=jax.ShapeDtypeStruct(block, jnp.bfloat16),
        in_specs=[
            pl.BlockSpec(memory_space=pltpu.VMEM),
            pl.BlockSpec(memory_space=pltpu.VMEM),
            pl.BlockSpec(memory_space=pl.ANY),
        ],
        out_specs=pl.BlockSpec(memory_space=pl.ANY),
        scratch_shapes=[
            pltpu.VMEM((2, units, columns), jnp.bfloat16),
            pltpu.VMEM((pairs, batch, 2, rows, columns), jnp.bfloat16),
            pltpu.VMEM((pairs,) + block, jnp.bfloat16),
            pltpu.VMEM((long_len,) + block, jnp.bfloat16),
            pltpu.VMEM((2, long_len) + block, jnp.bfloat16),
            pltpu.SemaphoreType.DMA,
            pltpu.SemaphoreType.DMA((2, pairs)),
            pltpu.SemaphoreType.DMA((2, long_len)),
            pltpu.SemaphoreType.DMA((3, long_len)),
            pltpu.SemaphoreType.DMA,
        ],
        compiler_params=pltpu.CompilerParams(
            collective_id=ident, has_side_effects=True, vmem_limit_bytes=60 << 20
        ),
        cost_estimate=wire_cost(shards, [jax.ShapeDtypeStruct(block, jnp.bfloat16)]),
        name="product_%d" % ident,
    )(gate, up, weight)


def local(
    tokens, segment_ids, norm_gains, attn_weight, adapter, ffn_weight, ffn_adapter, cotangent
):
    micro, local_len, model_dim = tokens.shape
    shards = lax.axis_size("fsdp")
    me = lax.axis_index("fsdp")
    seq_len = local_len * shards
    offset = me * local_len
    count = micro * local_len
    every = micro * seq_len
    q_width = HEADS * HD
    kv_end = q_width + 2 * HD
    score_scale = HD ** (-0.5)
    hidden_cols = ffn_weight.shape[0]
    attn_rows = attn_weight.shape[0]

    seg_cols = count // attn_rows
    seg_block = low(segment_ids).reshape(attn_rows, seg_cols)
    spare = jnp.zeros((attn_rows, 128 - 2 - seg_cols), jnp.bfloat16)
    small = jnp.concatenate([norm_gains, seg_block, spare], axis=1)
    same = kv_end + 4 * RANK
    attn_all, adapter_all, small_all = gather_all(
        shards, 1, attn_weight[None], adapter[None], small[None], shared=same
    )
    cotangent_now, small_all = lax.optimization_barrier((cotangent, small_all))
    cot_all = gather_rows(cotangent_now).reshape(every, model_dim)
    attn_all = attn_all.reshape(model_dim, attn_weight.shape[1])
    adapter_all = adapter_all.reshape(model_dim, 3 * RANK)
    small_all = small_all.reshape(model_dim, 128)
    w_proj = attn_all[:, :kv_end]
    w_out = attn_all[:, kv_end:]
    a_q, bq_t, bd_t = (adapter_all[:, j * RANK : (j + 1) * RANK] for j in range(3))
    gain_two = small_all[:, :2].astype(jnp.float32)
    seg_all = small_all[:, 2 : 2 + seg_cols].reshape(shards, micro, local_len)
    seg_all = seg_all.transpose(1, 0, 2).reshape(micro, seq_len).astype(jnp.int32)

    hidden_in = tokens.reshape(count, model_dim).astype(jnp.float32)
    key_index = jnp.arange(seq_len, dtype=jnp.int32)
    query_index = offset + jnp.arange(local_len, dtype=jnp.int32)
    before = jnp.sum(
        (seg_all[:, None, :] < segment_ids[:, :, None]).astype(jnp.int32), axis=2
    )
    angles = angles_of(query_index[None, :] - before).reshape(count, HD // 2)
    normed, norm_back_one = jax.vjp(rms_scale, hidden_in, gain_two[:, 0])
    normed_low = low(normed)
    projected = contract(normed_low, w_proj, 1, 0)
    query_low = low(contract(normed_low, a_q, 1, 0))
    query_pre = projected[:, :q_width] + contract(query_low, bq_t, 1, 1)
    queries = low(rotate(query_pre.reshape(count, HEADS, HD), angles[:, None, :]))
    queries = queries.reshape(micro, local_len * HEADS, HD)
    keys_low = low(rotate(projected[:, q_width : q_width + HD], angles))
    values_low = low(projected[:, q_width + HD :])
    keys_all, values_all = (
        each.reshape(micro, seq_len, -1)
        for each in gather_all(
            shards,
            2,
            keys_low.reshape(micro, local_len, HD),
            values_low.reshape(micro, local_len, HD),
        )
    )
    allowed = (
        (segment_ids[:, :, None] == seg_all[:, None, :])
        & (key_index[None, None, :] <= query_index[None, :, None])
    )[:, :, None, :]
    scores = (batched(queries, keys_all, 2, 2) * score_scale).reshape(
        micro, local_len, HEADS, seq_len
    )
    scores = jnp.where(allowed, scores, -1e30)
    top_score = jnp.max(scores, axis=-1, keepdims=True)
    exp_scores = jnp.exp(scores - top_score)
    weights = exp_scores / jnp.sum(exp_scores, axis=-1, keepdims=True)
    weights_low = low(weights).reshape(micro, local_len * HEADS, seq_len)
    context = low(batched(weights_low, values_all, 2, 1)).reshape(count, q_width)
    mixed_sum = hidden_in + contract(context, w_out, 1, 1)
    normed_two, norm_back_two = jax.vjp(rms_scale, mixed_sum, gain_two[:, 1])
    (inputs_all,) = gather_all(shards, 3, low(normed_two).reshape(micro, local_len, model_dim))
    inputs_all = inputs_all.reshape(every, model_dim)
    kept, inputs_all = lax.optimization_barrier(
        (jnp.concatenate([context, query_low], axis=1), inputs_all)
    )
    kept_all = gather_rows(kept.reshape(micro, local_len, q_width + RANK))
    kept_all = kept_all.reshape(every, q_width + RANK)
    low_grad_all = low(contract(cot_all, bd_t, 1, 0))

    step = hidden_cols // CHUNKS
    hidden_parts, gate_parts, up_parts = [], [], []
    for at in range(CHUNKS):
        units = slice(at * step, (at + 1) * step)
        w_gate, w_up, w_down = (ffn_weight[units, j, :] for j in range(3))
        gate_pre = contract(inputs_all, w_gate, 1, 1)
        up_pre = contract(inputs_all, w_up, 1, 1)
        activated, gelu_back = jax.vjp(gelu_tanh, gate_pre)
        hidden_act = low(activated * up_pre)
        hidden_grad = contract(cot_all, w_down, 1, 1) + contract(
            low_grad_all, ffn_adapter[units], 1, 1
        )
        gate_grad = low(gelu_back(hidden_grad * up_pre)[0])
        up_grad = low(hidden_grad * activated)
        hidden_parts.append(hidden_act)
        gate_parts.append(gate_grad)
        up_parts.append(up_grad)

    gate_grad = jnp.concatenate(gate_parts, axis=1)
    up_grad = jnp.concatenate(up_parts, axis=1)
    hidden_act = jnp.concatenate(hidden_parts, axis=1)
    step = hidden_cols // PIECES
    first_mine = low(contract(gate_grad[:, :step], inputs_all, 0, 0))
    down_part = low(contract(hidden_act, ffn_weight[:, 2, :], 1, 0))
    low_part = low(contract(hidden_act, ffn_adapter, 1, 0))
    first_other = swap_rep(first_mine)
    down_part, low_part, gate_grad, up_grad, hidden_act, first_mine = lax.optimization_barrier(
        (down_part, low_part, gate_grad, up_grad, hidden_act, first_mine)
    )
    down_sum = sum_rows(down_part.reshape(micro, seq_len, model_dim))
    ffn_parts = []
    for at in range(PIECES):
        units = slice(at * step, (at + 1) * step)
        for left, right in (
            (gate_grad, inputs_all),
            (up_grad, inputs_all),
            (hidden_act, cot_all),
        ):
            if not ffn_parts:
                ffn_parts.append((first_mine, first_other))
                continue
            mine = low(contract(left[:, units], right, 0, 0))
            ffn_parts.append((mine, swap_rep(mine)))
    low_mine = low(contract(hidden_act, low_grad_all, 0, 0))
    low_other = swap_rep(low_mine)
    gate_grad, up_grad, kept_all, _ = lax.optimization_barrier(
        (
            gate_grad,
            up_grad,
            kept_all,
            [pair[0] for pair in ffn_parts],
        )
    )
    if grid_of(shards)[1] == 2 and micro == 2:
        normed_two_grad = product_sum(
            shards,
            5,
            gate_grad.reshape(micro, seq_len, hidden_cols),
            up_grad.reshape(micro, seq_len, hidden_cols),
            ffn_weight.transpose(1, 0, 2),
        )
    else:
        (normed_two_grad,) = scatter_sum(
            shards,
            5,
            low(
                contract(gate_grad, ffn_weight[:, 0, :], 1, 0)
                + contract(up_grad, ffn_weight[:, 1, :], 1, 0)
            ).reshape(micro, shards, local_len, model_dim),
        )
    normed_two_grad, down_sum, _ = lax.optimization_barrier(
        (normed_two_grad, down_sum, [pair[1] for pair in ffn_parts[:2]])
    )
    normed_two_grad = normed_two_grad.reshape(count, model_dim).astype(jnp.float32)
    cot_full = cotangent.reshape(count, model_dim).astype(jnp.float32)
    mixed_part, gain_two_grad = norm_back_two(normed_two_grad)
    mixed_grad = cot_full + mixed_part
    out_grad_low = low(mixed_grad)
    context_grad = contract(out_grad_low, w_out, 1, 0)
    context_rows = low(context_grad).reshape(micro, local_len * HEADS, HD)
    prob_grad = batched(context_rows, values_all, 2, 2).reshape(micro, local_len, HEADS, seq_len)
    score_grad = weights * (prob_grad - jnp.sum(weights * prob_grad, axis=-1, keepdims=True))
    score_grad = low(score_grad).reshape(micro, local_len * HEADS, seq_len)
    query_grad = batched(score_grad, keys_all, 2, 1) * score_scale
    query_grad = query_grad.reshape(count, HEADS, HD)
    query_pre_grad = low(rotate(query_grad, -angles[:, None, :]).reshape(count, q_width))
    key_part = low(batched(score_grad, queries, 1, 1) * score_scale)
    value_part = low(batched(weights_low, context_rows, 1, 1))
    ffn_grad = place(None, 0, PIECES, ffn_parts[:3])
    key_part, value_part, query_pre_grad, ffn_grad = lax.optimization_barrier(
        (key_part, value_part, query_pre_grad, ffn_grad)
    )
    q_all = gather_rows(query_pre_grad.reshape(micro, local_len, q_width))
    q_all = q_all.reshape(every, q_width)
    key_sum, value_sum, down_low = (
        each.reshape(count, -1)
        for each in scatter_sum(
            shards,
            6,
            *(
                each.reshape(micro, shards, local_len, -1)
                for each in (key_part, value_part, low_part)
            ),
        )
    )
    result = (
        mixed_sum
        + down_sum.reshape(count, model_dim).astype(jnp.float32)
        + contract(down_low, bd_t, 1, 1)
    )
    key_grad = low(rotate(key_sum.astype(jnp.float32), -angles))
    value_grad = value_sum
    rank_grad = low(contract(query_pre_grad, bq_t, 1, 0))
    proj_grad = jnp.concatenate([query_pre_grad, key_grad, value_grad], axis=1)
    normed_grad = contract(proj_grad, w_proj, 1, 1) + contract(rank_grad, a_q, 1, 1)
    hidden_part, gain_one_grad = norm_back_one(normed_grad)
    input_grad = low(mixed_grad + hidden_part)

    narrow = jnp.concatenate([key_grad, value_grad, rank_grad, down_low], axis=1)
    narrow, ffn_parts[3:4] = lax.optimization_barrier((narrow, ffn_parts[3:4]))
    gain_parts = jnp.zeros((1, 16, model_dim), jnp.bfloat16)
    gain_parts = gain_parts.at[0, 0].set(low(gain_one_grad)).at[0, 1].set(low(gain_two_grad))
    narrow_all, normed_cols, out_cols, gain_cols = gather_all(
        shards,
        4,
        narrow.reshape(micro, local_len, 2 * HD + 2 * RANK),
        spread=(
            normed_low.reshape(micro, local_len, model_dim),
            out_grad_low.reshape(micro, local_len, model_dim),
            gain_parts,
        ),
    )
    narrow_all = narrow_all.reshape(every, 2 * HD + 2 * RANK)
    normed_cols = normed_cols.reshape(every, attn_rows)
    wout_grad = contract(out_cols.reshape(every, attn_rows), kept_all[:, :q_width], 0, 0)
    gain_now = jnp.sum(gain_cols[0, :, :2].astype(jnp.float32), axis=0)
    my_cols = me * attn_rows
    attn_q = low(contract(normed_cols, q_all, 0, 0))
    attn_rest = contract(normed_cols, narrow_all[:, : 2 * HD + RANK], 0, 0)
    bq_grad = contract(
        lax.dynamic_slice_in_dim(q_all, my_cols, attn_rows, 1), kept_all[:, q_width:], 0, 0
    )
    bd_grad = contract(
        lax.dynamic_slice_in_dim(cot_all, my_cols, attn_rows, 1),
        narrow_all[:, 2 * HD + RANK :],
        0,
        0,
    )
    tail = low(jnp.concatenate([attn_rest, bq_grad, bd_grad], axis=1))
    tail_out = low(wout_grad)
    tail_gain = low(gain_now)
    crossing = [swap_rep(each) for each in (tail_out, tail, attn_q)]
    attn_q, tail, tail_out, ffn_parts[3:], low_mine, low_other = lax.optimization_barrier(
        (attn_q, tail, tail_out, ffn_parts[3:], low_mine, low_other)
    )
    gains_grad = total(tail_gain, swap_rep(tail_gain)).transpose(1, 0)
    ffn_grad = place(ffn_grad, 1, PIECES, ffn_parts[3:])
    ffn_grad = ffn_grad.transpose(1, 0, 2)
    ffn_low_grad = total(low_mine, low_other)
    tail = total(tail, crossing[1])
    attn_grad = unwritten(attn_weight.shape, jnp.float32)
    for first, part in (
        (kv_end, total(tail_out, crossing[0])),
        (q_width, tail[:, : 2 * HD]),
        (0, total(attn_q, crossing[2])),
    ):
        attn_grad = lax.dynamic_update_slice(attn_grad, part, (0, first))
    adapter_grad = tail[:, 2 * HD :]
    return (
        low(result).reshape(micro, local_len, model_dim),
        input_grad.reshape(micro, local_len, model_dim),
        gains_grad,
        attn_grad,
        adapter_grad,
        ffn_grad,
        ffn_low_grad,
    )


def solution(mesh):
    placed = (
        P("rep", "fsdp", None),
        P("rep", "fsdp"),
        P("fsdp", None),
        P("fsdp", None),
        P("fsdp", None),
        P("fsdp", None, None),
        P("fsdp", None),
        P("rep", "fsdp", None),
    )
    return jax.shard_map(
        local,
        mesh=mesh,
        in_specs=placed,
        out_specs=(
            P("rep", "fsdp", None),
            P("rep", "fsdp", None),
            P("fsdp", None),
            P("fsdp", None),
            P("fsdp", None),
            P("fsdp", None, None),
            P("fsdp", None),
        ),
        check_vma=False,
    )
```

```python
import functools

import jax
import jax.numpy as jnp
from jax import lax
from jax.experimental import pallas as pl
from jax.experimental.pallas import tpu as pltpu
from jax.sharding import PartitionSpec as P

HEADS = 8
HD = 256
RANK = 256
CHUNKS = 1
PIECES = 2


epsilon = 1e-06


def rms_scale(values, gain_col):
    return (
        values * lax.rsqrt(jnp.mean(values * values, axis=-1, keepdims=True) + epsilon) * gain_col
    )


def angles_of(positions):
    inverse_freq = 10000.0 ** (-2.0 * jnp.arange(HD // 2, dtype=jnp.float32) / HD)
    return positions.astype(jnp.float32)[..., None] * inverse_freq


def rotate(field_in, angles):
    half_dim = field_in.shape[-1] // 2
    cosine = jnp.cos(angles)
    sine_part = jnp.sin(angles)
    lower_half = field_in[..., :half_dim]
    upper_half = field_in[..., half_dim:]
    return jnp.concatenate(
        [
            lower_half * cosine - upper_half * sine_part,
            upper_half * cosine + lower_half * sine_part,
        ],
        axis=-1,
    )


def gelu_tanh(values):
    return jax.nn.gelu(values, approximate=True)


def contract(left_op, right_op, left_dim, right_dim):
    return lax.dot_general(
        left_op,
        right_op,
        (((left_dim,), (right_dim,)), ((), ())),
        preferred_element_type=jnp.float32,
    )


def batched(left_op, right_op, left_dim, right_dim):
    return lax.dot_general(
        left_op,
        right_op,
        (((left_dim,), (right_dim,)), ((0,), (0,))),
        preferred_element_type=jnp.float32,
    )


def low(values):
    return values.astype(jnp.bfloat16)


def gather_rows(values):
    return lax.all_gather(values, "fsdp", axis=values.ndim - 2, tiled=True)


def sum_rows(values):
    return lax.psum_scatter(values, "fsdp", scatter_dimension=1, tiled=True)


def total(mine, other):
    return mine.astype(jnp.float32) + other.astype(jnp.float32)


def place_kernel(kinds, *refs):
    out = refs[-1]
    for kind in range(kinds):

        @pl.when(pl.program_id(0) == kind)
        def _():
            mine, other = refs[2 * kind], refs[2 * kind + 1]
            out[0] = total(mine[...], other[...])


def place(whole, group, groups, pairs):
    kinds = len(pairs)
    rows, columns = pairs[0][0].shape
    tile = min(rows, 128)
    tiles = rows // tile

    def part(kind):
        return pl.BlockSpec(
            (tile, columns),
            lambda k, j: (jnp.where(k == kind, j, jnp.where(k < kind, 0, tiles - 1)), 0),
        )

    in_specs = [part(kind) for kind in range(kinds) for _ in range(2)]
    operands = [each for pair in pairs for each in pair]
    aliases = {}
    if whole is not None:
        aliases = {len(operands): 0}
        in_specs.append(pl.BlockSpec(memory_space=pl.ANY))
        operands.append(whole)
    moved = kinds * rows * columns
    return pl.pallas_call(
        functools.partial(place_kernel, kinds),
        grid=(kinds, tiles),
        out_shape=jax.ShapeDtypeStruct((kinds, groups * rows, columns), jnp.float32),
        in_specs=in_specs,
        out_specs=pl.BlockSpec((1, tile, columns), lambda k, j: (k, group * tiles + j, 0)),
        input_output_aliases=aliases,
        cost_estimate=pl.CostEstimate(flops=moved, bytes_accessed=8 * moved, transcendentals=0),
        compiler_params=pltpu.CompilerParams(vmem_limit_bytes=24 << 20),
        name="place_%d" % group,
    )(*operands)


def swap_rep(values):
    return lax.ppermute(values, "rep", [(0, 1), (1, 0)])


def grid_of(shards):
    short = 2 if shards <= 16 else 4
    return shards // (2 * short), short


def wire_cost(times, values):
    moved = times * sum(v.size * v.dtype.itemsize for v in values)
    return pl.CostEstimate(flops=0, bytes_accessed=24 * moved + (40 << 20), transcendentals=0)


def unwritten(shape, dtype):
    return pl.pallas_call(
        lambda _: None,
        out_shape=jax.ShapeDtypeStruct(shape, dtype),
        out_specs=pl.BlockSpec(memory_space=pl.ANY),
        name="unwritten",
    )()


def neighbours(shards):
    long_len, short_len = grid_of(shards)
    me = lax.axis_index("fsdp")
    return me, me // (2 * short_len), (me // 2) % short_len, me % 2


def greet(shards, across, everyone=False):
    long_len, short_len = grid_of(shards)
    me, at_long, at_short, core = neighbours(shards)
    barrier = pltpu.get_barrier_semaphore()
    around = [
        (me >= 0, {"fsdp": me + 1 - 2 * core}),
        (at_long > 0, {"fsdp": me - 2 * short_len}),
        (at_long < long_len - 1, {"fsdp": me + 2 * short_len}),
        (at_short > 0, {"fsdp": me - 2}),
        (at_short < short_len - 1, {"fsdp": me + 2}),
    ]
    if everyone:
        around = [(me >= 0, {"fsdp": (me + far) % shards}) for far in range(1, shards)]
    if across:
        around.append((me >= 0, {"rep": 1 - lax.axis_index("rep")}))
    for has, peer in around:
        @pl.when(has)
        def _():
            pl.semaphore_signal(barrier, inc=1, device_id=peer)
    pl.semaphore_wait(barrier, sum(has.astype(jnp.int32) for has, _ in around))


def gather_kernel(shards, widths, shared, spread, *refs):
    long_len, short_len = grid_of(shards)
    count = len(widths)
    total = count + spread
    own = refs[:total]
    out = refs[total : 2 * total]
    send_sem, recv_sem, own_sem, spread_sem = refs[2 * total :]
    me, at_long, at_short, core = neighbours(shards)
    stride = 2 * short_len
    partner = {"fsdp": me + 1 - 2 * core}
    half = shared // 2
    parts = []
    if shared:
        rep = lax.axis_index("rep")
        peer_rep = {"rep": 1 - rep}
        parts.append((0, pl.multiple_of(rep * half, 128), half))
        parts.append((0, shared, widths[0] - shared))
        parts += [(k, 0, widths[k]) for k in range(1, count)]
        other = (0, pl.multiple_of((1 - rep) * half, 128), half)
    else:
        parts += [(k, 0, widths[k]) for k in range(count)]
        other = None
    lanes = list(range(len(parts)))
    away = len(parts)
    if shared:
        parts.append(other)

    def copy(lane, way, slot, peer, fresh):
        k, first, width = parts[lane]
        columns = pl.ds(first, width)
        there = out[k].at[:, slot, :, columns]
        return pltpu.make_async_remote_copy(
            src_ref=own[k].at[:, :, columns] if fresh else there,
            dst_ref=there,
            send_sem=send_sem.at[lane, way, slot],
            recv_sem=recv_sem.at[away if way == 5 else lane, slot],
            device_id=peer,
        )

    greet(shards, bool(shared), bool(spread))
    done = []

    def start(has, which, way, slot, peer, fresh=False):
        @pl.when(has)
        def _():
            for lane in which:
                copy(lane, way, slot, peer, fresh).start()

        done.append((has, which, way, slot, peer, fresh))

    def arrive(has, which, slot):
        @pl.when(has)
        def _():
            for lane in which:
                copy(lane, 0, slot, partner, False).wait_recv()

    late = []

    def got(has, slot):
        if shared:
            start(has, [0], 5, slot, peer_rep)
            late.append((has, slot))
        start(has, lanes, 4, slot, partner)

    def from_across():
        for has, slot in late:
            arrive(has, [away], slot)
            start(has, [away], 4, slot, partner)
        late.clear()

    def spread_short(has, slot, fresh=False):
        start(has & (at_short < short_len - 1), lanes, 2, slot, {"fsdp": me + 2}, fresh)
        start(has & (at_short > 0), lanes, 3, slot, {"fsdp": me - 2}, fresh)

    def short_arrivals(has, line):
        for far in range(1, short_len):
            for sign in (-1, 1):
                source = at_short + sign * far
                ok = has & (source >= 0) & (source < short_len)
                slot = me + 2 * sign * far + (line - at_long) * stride
                arrive(ok, lanes, slot)
                if far < short_len - 1:
                    onward = at_short - sign
                    start(
                        ok & (onward >= 0) & (onward < short_len),
                        lanes,
                        2 if sign < 0 else 3,
                        slot,
                        {"fsdp": me - 2 * sign},
                    )
                got(ok, slot)

    true = me >= 0
    start(at_long < long_len - 1, lanes, 0, me, {"fsdp": me + stride}, True)
    start(at_long > 0, lanes, 1, me, {"fsdp": me - stride}, True)
    spread_short(true, me, True)
    every = list(range(len(parts)))
    start(true, every, 4, me, partner, True)
    mine = [pltpu.make_async_copy(own[k], out[k].at[:, me], own_sem.at[k]) for k in range(count)]

    def share(k, peer, target):
        width = own[k].shape[2] // shards
        columns = pl.ds(pl.multiple_of(peer * width, 128), width)
        return own[k].at[:, :, columns], out[k].at[:, target]

    def dealt(k, far, back):
        peer = (me + far) % shards
        source, target = share(k, me if back else peer, peer if back else me)
        return pltpu.make_async_remote_copy(
            src_ref=source,
            dst_ref=target,
            send_sem=spread_sem.at[k - count, 0, peer],
            recv_sem=spread_sem.at[k - count, 1, peer if back else me],
            device_id={"fsdp": peer},
        )

    for k in range(count, total):
        mine.append(pltpu.make_async_copy(*share(k, me, me), own_sem.at[k]))
        for far in range(1, shards):
            dealt(k, far, False).start()
    for each in mine:
        each.start()
    for far in range(1, long_len):
        for sign in (-1, 1):
            source = at_long + sign * far
            ok = (source >= 0) & (source < long_len)
            slot = me + sign * far * stride
            arrive(ok, lanes, slot)
            onward = at_long - sign
            start(
                ok & (onward >= 0) & (onward < long_len),
                lanes,
                0 if sign < 0 else 1,
                slot,
                {"fsdp": me - sign * stride},
            )
            spread_short(ok, slot)
            got(ok, slot)
        if far == 1:
            short_arrivals(true, at_long)
        else:
            for sign in (-1, 1):
                source = at_long + sign * (far - 1)
                short_arrivals((source >= 0) & (source < long_len), source)
        if far > 1:
            from_across()
    for sign in (-1, 1):
        source = at_long + sign * (long_len - 1)
        short_arrivals((source >= 0) & (source < long_len), source)
    from_across()
    for line in range(long_len):
        for short in range(short_len):
            arrive(true, every, (line * short_len + short) * 2 + 1 - core)
    for has, which, way, slot, peer, fresh in done:
        @pl.when(has)
        def _():
            for lane in which:
                copy(lane, way, slot, peer, fresh).wait_send()
    for k in range(count, total):
        for far in range(1, shards):
            dealt(k, far, True).wait_recv()
            dealt(k, far, False).wait_send()
    for each in mine:
        each.wait()


def gather_all(shards, ident, *values, shared=0, spread=()):
    widths = tuple(v.shape[2] for v in values)
    count = len(values)
    lanes = count + (2 if shared else 0)
    shapes = [(v.shape[0], shards) + v.shape[1:] for v in values]
    dealt = []
    if spread and spread[0].shape[2] % (128 * shards):
        for v in spread:
            each = lax.all_to_all(v, "fsdp", 2, 1, tiled=True)
            dealt.append(each.reshape(v.shape[0], shards, v.shape[1], -1))
        spread = ()
    values = values + tuple(spread)
    shapes += [(v.shape[0], shards, v.shape[1], v.shape[2] // shards) for v in spread]
    results = pl.pallas_call(
        functools.partial(gather_kernel, shards, widths, shared, len(values) - count),
        out_shape=[jax.ShapeDtypeStruct(shape, v.dtype) for shape, v in zip(shapes, values)],
        in_specs=[pl.BlockSpec(memory_space=pltpu.VMEM)] * len(values),
        out_specs=[pl.BlockSpec(memory_space=pl.ANY)] * len(values),
        scratch_shapes=[
            pltpu.SemaphoreType.DMA((lanes, 6, shards)),
            pltpu.SemaphoreType.DMA((lanes, shards)),
            pltpu.SemaphoreType.DMA((len(values),)),
            pltpu.SemaphoreType.DMA((len(spread) + 1, 2, shards)),
        ],
        compiler_params=pltpu.CompilerParams(collective_id=ident, has_side_effects=True),
        cost_estimate=wire_cost(shards, values[:count]),
        name="gather_%d" % ident,
    )(*values)
    return list(results) + dealt


def scatter_kernel(shards, widths, *refs):
    long_len, short_len = grid_of(shards)
    count = len(widths)
    full = refs[:count]
    out = refs[count : 2 * count]
    held, core_in, short_in, long_in, load_sem, core_sem, short_sem, long_sem, done_sem = refs[
        2 * count :
    ]
    me, at_long, at_short, core = neighbours(shards)
    partner = {"fsdp": me + 1 - 2 * core}
    firsts = [sum(widths[:k]) for k in range(count)]

    def index(line, short):
        return line * short_len + short

    def block(k, line, short, side):
        return full[k].at[:, index(line, short) * 2 + side]

    def columns(ref, k):
        return ref.at[:, :, pl.ds(firsts[k], widths[k])]

    order = []
    for far in range(long_len - 1, 0, -1):
        for sign in (-1, 1):
            line = at_long + sign * far
            order.append(((line >= 0) & (line < long_len), line, far, sign))
    order.append((me >= 0, at_long, 0, 0))
    shorts = []
    for far in range(short_len - 1, 0, -1):
        for sign in (-1, 1):
            short = at_short + sign * far
            shorts.append(((short >= 0) & (short < short_len), short, far, sign))
    shorts.append((me >= 0, at_short, 0, 0))

    def to_core(k, line, short):
        return pltpu.make_async_remote_copy(
            src_ref=block(k, line, short, 1 - core),
            dst_ref=columns(core_in.at[index(line, short)], k),
            send_sem=core_sem.at[0, k, index(line, short)],
            recv_sem=core_sem.at[1, k, index(line, short)],
            device_id=partner,
        )

    def load(k, line, short):
        return pltpu.make_async_copy(
            block(k, line, short, core),
            columns(held.at[index(line, short)], k),
            load_sem.at[k, index(line, short)],
        )

    def along_short(line, short, sign):
        return pltpu.make_async_remote_copy(
            src_ref=held.at[index(line, short)],
            dst_ref=short_in.at[(1 - sign) // 2, index(line, short)],
            send_sem=short_sem.at[0, index(line, short)],
            recv_sem=short_sem.at[1 + (1 - sign) // 2, index(line, short)],
            device_id={"fsdp": me + 2 * sign},
        )

    def along_long(line, sign):
        return pltpu.make_async_remote_copy(
            src_ref=held.at[index(line, at_short)],
            dst_ref=long_in.at[(1 - sign) // 2, line],
            send_sem=long_sem.at[0, line],
            recv_sem=long_sem.at[1 + (1 - sign) // 2, line],
            device_id={"fsdp": me + 2 * short_len * sign},
        )

    def add(to_ref, from_ref):
        batch, rows, _ = to_ref.shape
        step = 16

        @pl.loop(0, batch * rows // step)
        def _(at):
            one = at // (rows // step)
            where = pl.ds(pl.multiple_of((at % (rows // step)) * step, step), step)
            to_ref[one, where, :] = (
                to_ref[one, where, :].astype(jnp.float32)
                + from_ref[one, where, :].astype(jnp.float32)
            ).astype(jnp.bfloat16)

    for near, short, far, sign in shorts:
        for has, line, _, _ in order:
            @pl.when(near & has)
            def _():
                for k in range(count):
                    load(k, line, short).start()

    greet(shards, False)
    for near, short, far, sign in shorts:
        for has, line, _, _ in order:
            @pl.when(near & has)
            def _():
                for k in range(count):
                    to_core(k, line, short).start()

    for near, short, far, sign in shorts:
        for has, line, far_line, sign_line in order:
            @pl.when(near & has)
            def _():
                at = index(line, short)
                for k in range(count):
                    load(k, line, short).wait()
                    to_core(k, line, short).wait_recv()
                add(held.at[at], core_in.at[at])
                if far:
                    behind = at_short - sign

                    @pl.when((behind >= 0) & (behind < short_len))
                    def _():
                        along_short(line, short, sign).wait_recv()
                        add(held.at[at], short_in.at[(1 - sign) // 2, at])

                    along_short(line, short, sign).start()
                else:
                    for way in (-1, 1):
                        behind = at_short - way

                        @pl.when((behind >= 0) & (behind < short_len))
                        def _():
                            along_short(line, short, way).wait_recv()
                            add(held.at[at], short_in.at[(1 - way) // 2, at])

                    for way in (-1, 1) if not far_line else (sign_line,):
                        behind = at_long - way

                        @pl.when((behind >= 0) & (behind < long_len))
                        def _():
                            along_long(line, way).wait_recv()
                            add(held.at[at], long_in.at[(1 - way) // 2, line])

                    if far_line:
                        along_long(line, sign_line).start()

    results = [
        pltpu.make_async_copy(columns(held.at[index(at_long, at_short)], k), out[k], done_sem.at[k])
        for k in range(count)
    ]
    for each in results:
        each.start()
    for near, short, far, sign in shorts:
        for has, line, far_line, sign_line in order:
            @pl.when(near & has)
            def _():
                for k in range(count):
                    to_core(k, line, short).wait_send()
                if far:
                    along_short(line, short, sign).wait_send()
                elif far_line:
                    along_long(line, sign_line).wait_send()
    for each in results:
        each.wait()


def scatter_sum(shards, ident, *values):
    batch, _, rows, _ = values[0].shape
    widths = tuple(v.shape[3] for v in values)
    if shards > 16:
        return [
            sum_rows(v.reshape(batch, shards * rows, w)) for v, w in zip(values, widths)
        ]
    count = len(values)
    long_len, short_len = grid_of(shards)
    pairs = shards // 2
    block = (batch, rows, sum(widths))
    return pl.pallas_call(
        functools.partial(scatter_kernel, shards, widths),
        out_shape=[jax.ShapeDtypeStruct((batch, rows, w), jnp.bfloat16) for w in widths],
        in_specs=[pl.BlockSpec(memory_space=pl.ANY)] * count,
        out_specs=[pl.BlockSpec(memory_space=pl.ANY)] * count,
        scratch_shapes=[
            pltpu.VMEM((pairs,) + block, jnp.bfloat16),
            pltpu.VMEM((pairs,) + block, jnp.bfloat16),
            pltpu.VMEM((2, pairs) + block, jnp.bfloat16),
            pltpu.VMEM((2, long_len) + block, jnp.bfloat16),
            pltpu.SemaphoreType.DMA((count, pairs)),
            pltpu.SemaphoreType.DMA((2, count, pairs)),
            pltpu.SemaphoreType.DMA((3, pairs)),
            pltpu.SemaphoreType.DMA((3, long_len)),
            pltpu.SemaphoreType.DMA((count,)),
        ],
        compiler_params=pltpu.CompilerParams(
            collective_id=ident, has_side_effects=True, vmem_limit_bytes=60 << 20
        ),
        cost_estimate=wire_cost(1, values),
        name="scatter_%d" % ident,
    )(*values)


def product_kernel(shards, gate, up, weight, out, *scratch):
    planes, pair, core_in, short_in, long_in = scratch[:5]
    plane_sem, core_sem, short_sem, long_sem, done_sem = scratch[5:]
    long_len, _ = grid_of(shards)
    me, at_long, at_short, core = neighbours(shards)
    rows = pair.shape[3]
    load = pltpu.make_async_copy(weight.at[pl.ds(0, 2)], planes, plane_sem)
    load.start()

    lines = []
    first, last = me * 0, me * 0 + long_len - 1
    for _ in range(long_len - 1):
        up_side = (last - at_long >= at_long - first).astype(jnp.int32)
        lines.append((first + up_side * (last - first), 2 * up_side - 1))
        first, last = first + 1 - up_side, last - up_side
    lines.append((at_long, None))
    steps = [(line, sign, 1 - at_short) for line, sign in lines]
    steps += [(line, sign, at_short) for line, sign in lines]

    def held(at):
        return pair.at[at, :, core]

    def compute(at):
        where = pl.ds(pl.multiple_of(at * 2 * rows, 2 * rows), 2 * rows)
        left = gate[:, where, :].reshape(4 * rows, gate.shape[2])
        right = up[:, where, :].reshape(4 * rows, up.shape[2])

        @pl.loop(0, pair.shape[4] // 512)
        def _(tile):
            columns = pl.ds(pl.multiple_of(tile * 512, 512), 512)
            sums = jnp.dot(left, planes[0, :, columns], preferred_element_type=jnp.float32)
            sums += jnp.dot(right, planes[1, :, columns], preferred_element_type=jnp.float32)
            pair[at, :, :, :, columns] = sums.astype(jnp.bfloat16).reshape(2, 2, rows, 512)

    def to_core(at):
        return pltpu.make_async_remote_copy(
            src_ref=pair.at[at, :, 1 - core],
            dst_ref=core_in.at[at],
            send_sem=core_sem.at[0, at],
            recv_sem=core_sem.at[1, at],
            device_id={"fsdp": me + 1 - 2 * core},
        )

    def along_short(line, short):
        return pltpu.make_async_remote_copy(
            src_ref=held(line * 2 + short),
            dst_ref=short_in.at[line],
            send_sem=short_sem.at[0, line],
            recv_sem=short_sem.at[1, line],
            device_id={"fsdp": me + 2 - 4 * at_short},
        )

    def along_long(line, sign):
        return pltpu.make_async_remote_copy(
            src_ref=held(line * 2 + at_short),
            dst_ref=long_in.at[(1 - sign) // 2, line],
            send_sem=long_sem.at[0, line],
            recv_sem=long_sem.at[1 + (1 - sign) // 2, line],
            device_id={"fsdp": me + 4 * sign},
        )

    def add(at, other):
        @pl.loop(0, 2 * rows // 16)
        def _(group):
            one = group // (rows // 16)
            where = pl.ds(pl.multiple_of((group % (rows // 16)) * 16, 16), 16)
            pair[at, one, core, where, :] = (
                pair[at, one, core, where, :].astype(jnp.float32)
                + other[one, where, :].astype(jnp.float32)
            ).astype(jnp.bfloat16)

    def from_behind(at, line, sign):
        behind = at_long - sign

        @pl.when((behind >= 0) & (behind < long_len))
        def _():
            along_long(line, sign).wait_recv()
            add(at, long_in.at[(1 - sign) // 2, line])

    def settle(at_step):
        line, sign, short = steps[at_step]
        at = line * 2 + short
        to_core(at).wait_recv()
        add(at, core_in.at[at])
        if at_step < long_len:
            along_short(line, short).start()
            return
        along_short(line, short).wait_recv()
        add(at, short_in.at[line])
        if sign is None:
            from_behind(at, line, 1)
            from_behind(at, line, -1)
        else:
            from_behind(at, line, sign)
            along_long(line, sign).start()

    greet(shards, False)
    load.wait()
    for at_step, (line, _, short) in enumerate(steps):
        compute(line * 2 + short)
        to_core(line * 2 + short).start()
        if at_step:
            settle(at_step - 1)
    settle(len(steps) - 1)
    result = pltpu.make_async_copy(held(at_long * 2 + at_short), out, done_sem)
    result.start()
    for at_step, (line, sign, short) in enumerate(steps):
        to_core(line * 2 + short).wait_send()
        if at_step < long_len:
            along_short(line, short).wait_send()
        elif sign is not None:
            along_long(line, sign).wait_send()
    result.wait()


def product_sum(shards, ident, gate, up, weight):
    batch, every, units = gate.shape
    columns = weight.shape[2]
    rows = every // shards
    long_len, short_len = grid_of(shards)
    block = (batch, rows, columns)
    pairs = shards // 2
    return pl.pallas_call(
        functools.partial(product_kernel, shards),
        out_shape=jax.ShapeDtypeStruct(block, jnp.bfloat16),
        in_specs=[
            pl.BlockSpec(memory_space=pltpu.VMEM),
            pl.BlockSpec(memory_space=pltpu.VMEM),
            pl.BlockSpec(memory_space=pl.ANY),
        ],
        out_specs=pl.BlockSpec(memory_space=pl.ANY),
        scratch_shapes=[
            pltpu.VMEM((2, units, columns), jnp.bfloat16),
            pltpu.VMEM((pairs, batch, 2, rows, columns), jnp.bfloat16),
            pltpu.VMEM((pairs,) + block, jnp.bfloat16),
            pltpu.VMEM((long_len,) + block, jnp.bfloat16),
            pltpu.VMEM((2, long_len) + block, jnp.bfloat16),
            pltpu.SemaphoreType.DMA,
            pltpu.SemaphoreType.DMA((2, pairs)),
            pltpu.SemaphoreType.DMA((2, long_len)),
            pltpu.SemaphoreType.DMA((3, long_len)),
            pltpu.SemaphoreType.DMA,
        ],
        compiler_params=pltpu.CompilerParams(
            collective_id=ident, has_side_effects=True, vmem_limit_bytes=60 << 20
        ),
        cost_estimate=wire_cost(shards, [jax.ShapeDtypeStruct(block, jnp.bfloat16)]),
        name="product_%d" % ident,
    )(gate, up, weight)


def local(
    tokens, segment_ids, norm_gains, attn_weight, adapter, ffn_weight, ffn_adapter, cotangent
):
    micro, local_len, model_dim = tokens.shape
    shards = lax.axis_size("fsdp")
    me = lax.axis_index("fsdp")
    seq_len = local_len * shards
    offset = me * local_len
    count = micro * local_len
    every = micro * seq_len
    q_width = HEADS * HD
    kv_end = q_width + 2 * HD
    score_scale = HD ** (-0.5)
    hidden_cols = ffn_weight.shape[0]
    attn_rows = attn_weight.shape[0]

    seg_cols = count // attn_rows
    seg_block = low(segment_ids).reshape(attn_rows, seg_cols)
    spare = jnp.zeros((attn_rows, 128 - 2 - seg_cols), jnp.bfloat16)
    small = jnp.concatenate([norm_gains, seg_block, spare], axis=1)
    same = kv_end + 4 * RANK
    attn_all, adapter_all, small_all = gather_all(
        shards, 1, attn_weight[None], adapter[None], small[None], shared=same
    )
    cotangent_now, small_all = lax.optimization_barrier((cotangent, small_all))
    cot_all = gather_rows(cotangent_now).reshape(every, model_dim)
    attn_all = attn_all.reshape(model_dim, attn_weight.shape[1])
    adapter_all = adapter_all.reshape(model_dim, 3 * RANK)
    small_all = small_all.reshape(model_dim, 128)
    w_proj = attn_all[:, :kv_end]
    w_out = attn_all[:, kv_end:]
    a_q, bq_t, bd_t = (adapter_all[:, j * RANK : (j + 1) * RANK] for j in range(3))
    gain_two = small_all[:, :2].astype(jnp.float32)
    seg_all = small_all[:, 2 : 2 + seg_cols].reshape(shards, micro, local_len)
    seg_all = seg_all.transpose(1, 0, 2).reshape(micro, seq_len).astype(jnp.int32)

    hidden_in = tokens.reshape(count, model_dim).astype(jnp.float32)
    key_index = jnp.arange(seq_len, dtype=jnp.int32)
    query_index = offset + jnp.arange(local_len, dtype=jnp.int32)
    before = jnp.sum(
        (seg_all[:, None, :] < segment_ids[:, :, None]).astype(jnp.int32), axis=2
    )
    angles = angles_of(query_index[None, :] - before).reshape(count, HD // 2)
    normed, norm_back_one = jax.vjp(rms_scale, hidden_in, gain_two[:, 0])
    normed_low = low(normed)
    projected = contract(normed_low, w_proj, 1, 0)
    query_low = low(contract(normed_low, a_q, 1, 0))
    query_pre = projected[:, :q_width] + contract(query_low, bq_t, 1, 1)
    queries = low(rotate(query_pre.reshape(count, HEADS, HD), angles[:, None, :]))
    queries = queries.reshape(micro, local_len * HEADS, HD)
    keys_low = low(rotate(projected[:, q_width : q_width + HD], angles))
    values_low = low(projected[:, q_width + HD :])
    keys_all, values_all = (
        each.reshape(micro, seq_len, -1)
        for each in gather_all(
            shards,
            2,
            keys_low.reshape(micro, local_len, HD),
            values_low.reshape(micro, local_len, HD),
        )
    )
    allowed = (
        (segment_ids[:, :, None] == seg_all[:, None, :])
        & (key_index[None, None, :] <= query_index[None, :, None])
    )[:, :, None, :]
    scores = (batched(queries, keys_all, 2, 2) * score_scale).reshape(
        micro, local_len, HEADS, seq_len
    )
    scores = jnp.where(allowed, scores, -1e30)
    top_score = jnp.max(scores, axis=-1, keepdims=True)
    exp_scores = jnp.exp(scores - top_score)
    weights = exp_scores / jnp.sum(exp_scores, axis=-1, keepdims=True)
    weights_low = low(weights).reshape(micro, local_len * HEADS, seq_len)
    context = low(batched(weights_low, values_all, 2, 1)).reshape(count, q_width)
    mixed_sum = hidden_in + contract(context, w_out, 1, 1)
    normed_two, norm_back_two = jax.vjp(rms_scale, mixed_sum, gain_two[:, 1])
    (inputs_all,) = gather_all(shards, 3, low(normed_two).reshape(micro, local_len, model_dim))
    inputs_all = inputs_all.reshape(every, model_dim)
    kept, inputs_all = lax.optimization_barrier(
        (jnp.concatenate([context, query_low], axis=1), inputs_all)
    )
    kept_all = gather_rows(kept.reshape(micro, local_len, q_width + RANK))
    kept_all = kept_all.reshape(every, q_width + RANK)
    low_grad_all = low(contract(cot_all, bd_t, 1, 0))

    step = hidden_cols // CHUNKS
    hidden_parts, gate_parts, up_parts = [], [], []
    for at in range(CHUNKS):
        units = slice(at * step, (at + 1) * step)
        w_gate, w_up, w_down = (ffn_weight[units, j, :] for j in range(3))
        gate_pre = contract(inputs_all, w_gate, 1, 1)
        up_pre = contract(inputs_all, w_up, 1, 1)
        activated, gelu_back = jax.vjp(gelu_tanh, gate_pre)
        hidden_act = low(activated * up_pre)
        hidden_grad = contract(cot_all, w_down, 1, 1) + contract(
            low_grad_all, ffn_adapter[units], 1, 1
        )
        gate_grad = low(gelu_back(hidden_grad * up_pre)[0])
        up_grad = low(hidden_grad * activated)
        hidden_parts.append(hidden_act)
        gate_parts.append(gate_grad)
        up_parts.append(up_grad)

    gate_grad = jnp.concatenate(gate_parts, axis=1)
    up_grad = jnp.concatenate(up_parts, axis=1)
    hidden_act = jnp.concatenate(hidden_parts, axis=1)
    step = hidden_cols // PIECES

    def weight_grads(at, gate_now, up_now, hidden_now):
        units = slice(at * step, (at + 1) * step)
        made = []
        for left, right in (
            (gate_now, inputs_all),
            (up_now, inputs_all),
            (hidden_now, cot_all),
        ):
            mine = low(contract(left[:, units], right, 0, 0))
            made.append((mine, swap_rep(mine)))
        return made

    ffn_parts = weight_grads(0, gate_grad, up_grad, hidden_act)
    gate_grad, up_grad, kept_all, _ = lax.optimization_barrier(
        (gate_grad, up_grad, kept_all, [pair[0] for pair in ffn_parts])
    )
    if grid_of(shards)[1] == 2 and micro == 2:
        normed_two_grad = product_sum(
            shards,
            5,
            gate_grad.reshape(micro, seq_len, hidden_cols),
            up_grad.reshape(micro, seq_len, hidden_cols),
            ffn_weight.transpose(1, 0, 2),
        )
    else:
        (normed_two_grad,) = scatter_sum(
            shards,
            5,
            low(
                contract(gate_grad, ffn_weight[:, 0, :], 1, 0)
                + contract(up_grad, ffn_weight[:, 1, :], 1, 0)
            ).reshape(micro, shards, local_len, model_dim),
        )
    normed_two_grad, gate_grad, up_grad, hidden_act, _ = lax.optimization_barrier(
        (normed_two_grad, gate_grad, up_grad, hidden_act, [pair[1] for pair in ffn_parts[:2]])
    )
    down_part = low(contract(hidden_act, ffn_weight[:, 2, :], 1, 0))
    low_part = low(contract(hidden_act, ffn_adapter, 1, 0))
    down_part, gate_grad, up_grad, hidden_act = lax.optimization_barrier(
        (down_part, gate_grad, up_grad, hidden_act)
    )
    down_sum = sum_rows(down_part.reshape(micro, seq_len, model_dim))
    ffn_parts += weight_grads(1, gate_grad, up_grad, hidden_act)
    low_mine = low(contract(hidden_act, low_grad_all, 0, 0))
    low_other = swap_rep(low_mine)
    normed_two_grad, low_part, low_mine, _ = lax.optimization_barrier(
        (normed_two_grad, low_part, low_mine, [pair[0] for pair in ffn_parts])
    )
    normed_two_grad = normed_two_grad.reshape(count, model_dim).astype(jnp.float32)
    cot_full = cotangent.reshape(count, model_dim).astype(jnp.float32)
    mixed_part, gain_two_grad = norm_back_two(normed_two_grad)
    mixed_grad = cot_full + mixed_part
    out_grad_low = low(mixed_grad)
    context_grad = contract(out_grad_low, w_out, 1, 0)
    context_rows = low(context_grad).reshape(micro, local_len * HEADS, HD)
    prob_grad = batched(context_rows, values_all, 2, 2).reshape(micro, local_len, HEADS, seq_len)
    score_grad = weights * (prob_grad - jnp.sum(weights * prob_grad, axis=-1, keepdims=True))
    score_grad = low(score_grad).reshape(micro, local_len * HEADS, seq_len)
    query_grad = batched(score_grad, keys_all, 2, 1) * score_scale
    query_grad = query_grad.reshape(count, HEADS, HD)
    query_pre_grad = low(rotate(query_grad, -angles[:, None, :]).reshape(count, q_width))
    key_part = low(batched(score_grad, queries, 1, 1) * score_scale)
    value_part = low(batched(weights_low, context_rows, 1, 1))
    key_part, value_part, query_pre_grad, ffn_parts[2:3] = lax.optimization_barrier(
        (key_part, value_part, query_pre_grad, ffn_parts[2:3])
    )
    q_all = gather_rows(query_pre_grad.reshape(micro, local_len, q_width))
    q_all = q_all.reshape(every, q_width)
    key_sum, value_sum, down_low = (
        each.reshape(count, -1)
        for each in scatter_sum(
            shards,
            6,
            *(
                each.reshape(micro, shards, local_len, -1)
                for each in (key_part, value_part, low_part)
            ),
        )
    )
    result = (
        mixed_sum
        + down_sum.reshape(count, model_dim).astype(jnp.float32)
        + contract(down_low, bd_t, 1, 1)
    )
    key_grad = low(rotate(key_sum.astype(jnp.float32), -angles))
    value_grad = value_sum
    rank_grad = low(contract(query_pre_grad, bq_t, 1, 0))
    proj_grad = jnp.concatenate([query_pre_grad, key_grad, value_grad], axis=1)
    normed_grad = contract(proj_grad, w_proj, 1, 1) + contract(rank_grad, a_q, 1, 1)
    hidden_part, gain_one_grad = norm_back_one(normed_grad)
    input_grad = low(mixed_grad + hidden_part)

    narrow = jnp.concatenate([key_grad, value_grad, rank_grad, down_low], axis=1)
    narrow, ffn_parts[3:4] = lax.optimization_barrier((narrow, ffn_parts[3:4]))
    gain_parts = jnp.zeros((1, 16, model_dim), jnp.bfloat16)
    gain_parts = gain_parts.at[0, 0].set(low(gain_one_grad)).at[0, 1].set(low(gain_two_grad))
    narrow_all, normed_cols, out_cols, gain_cols = gather_all(
        shards,
        4,
        narrow.reshape(micro, local_len, 2 * HD + 2 * RANK),
        spread=(
            normed_low.reshape(micro, local_len, model_dim),
            out_grad_low.reshape(micro, local_len, model_dim),
            gain_parts,
        ),
    )
    narrow_all, ffn_parts[:3] = lax.optimization_barrier((narrow_all, ffn_parts[:3]))
    ffn_grad = place(None, 0, PIECES, ffn_parts[:3])
    narrow_all = narrow_all.reshape(every, 2 * HD + 2 * RANK)
    normed_cols = normed_cols.reshape(every, attn_rows)
    wout_grad = contract(out_cols.reshape(every, attn_rows), kept_all[:, :q_width], 0, 0)
    gain_now = jnp.sum(gain_cols[0, :, :2].astype(jnp.float32), axis=0)
    my_cols = me * attn_rows
    attn_q = low(contract(normed_cols, q_all, 0, 0))
    attn_rest = contract(normed_cols, narrow_all[:, : 2 * HD + RANK], 0, 0)
    bq_grad = contract(
        lax.dynamic_slice_in_dim(q_all, my_cols, attn_rows, 1), kept_all[:, q_width:], 0, 0
    )
    bd_grad = contract(
        lax.dynamic_slice_in_dim(cot_all, my_cols, attn_rows, 1),
        narrow_all[:, 2 * HD + RANK :],
        0,
        0,
    )
    tail = low(jnp.concatenate([attn_rest, bq_grad, bd_grad], axis=1))
    tail_out = low(wout_grad)
    tail_gain = low(gain_now)
    crossing = [swap_rep(each) for each in (tail_out, tail, attn_q)]
    attn_q, tail, tail_out, ffn_parts[3:], low_mine, low_other = lax.optimization_barrier(
        (attn_q, tail, tail_out, ffn_parts[3:], low_mine, low_other)
    )
    gains_grad = total(tail_gain, swap_rep(tail_gain)).transpose(1, 0)
    ffn_grad = place(ffn_grad, 1, PIECES, ffn_parts[3:])
    ffn_grad = ffn_grad.transpose(1, 0, 2)
    ffn_low_grad = total(low_mine, low_other)
    tail = total(tail, crossing[1])
    attn_grad = unwritten(attn_weight.shape, jnp.float32)
    for first, part in (
        (kv_end, total(tail_out, crossing[0])),
        (q_width, tail[:, : 2 * HD]),
        (0, total(attn_q, crossing[2])),
    ):
        attn_grad = lax.dynamic_update_slice(attn_grad, part, (0, first))
    adapter_grad = tail[:, 2 * HD :]
    return (
        low(result).reshape(micro, local_len, model_dim),
        input_grad.reshape(micro, local_len, model_dim),
        gains_grad,
        attn_grad,
        adapter_grad,
        ffn_grad,
        ffn_low_grad,
    )


def solution(mesh):
    placed = (
        P("rep", "fsdp", None),
        P("rep", "fsdp"),
        P("fsdp", None),
        P("fsdp", None),
        P("fsdp", None),
        P("fsdp", None, None),
        P("fsdp", None),
        P("rep", "fsdp", None),
    )
    return jax.shard_map(
        local,
        mesh=mesh,
        in_specs=placed,
        out_specs=(
            P("rep", "fsdp", None),
            P("rep", "fsdp", None),
            P("fsdp", None),
            P("fsdp", None),
            P("fsdp", None),
            P("fsdp", None, None),
            P("fsdp", None),
        ),
        check_vma=False,
    )
```

```python
import functools

import jax
import jax.numpy as jnp
from jax import lax
from jax.experimental import pallas as pl
from jax.experimental.pallas import tpu as pltpu
from jax.sharding import PartitionSpec as P

HEADS = 8
HD = 256
RANK = 256
CHUNKS = 1
PIECES = 2


epsilon = 1e-06


def rms_scale(values, gain_col):
    return (
        values * lax.rsqrt(jnp.mean(values * values, axis=-1, keepdims=True) + epsilon) * gain_col
    )


def angles_of(positions):
    inverse_freq = 10000.0 ** (-2.0 * jnp.arange(HD // 2, dtype=jnp.float32) / HD)
    return positions.astype(jnp.float32)[..., None] * inverse_freq


def rotate(field_in, angles):
    half_dim = field_in.shape[-1] // 2
    cosine = jnp.cos(angles)
    sine_part = jnp.sin(angles)
    lower_half = field_in[..., :half_dim]
    upper_half = field_in[..., half_dim:]
    return jnp.concatenate(
        [
            lower_half * cosine - upper_half * sine_part,
            upper_half * cosine + lower_half * sine_part,
        ],
        axis=-1,
    )


def gelu_tanh(values):
    return jax.nn.gelu(values, approximate=True)


def contract(left_op, right_op, left_dim, right_dim):
    return lax.dot_general(
        left_op,
        right_op,
        (((left_dim,), (right_dim,)), ((), ())),
        preferred_element_type=jnp.float32,
    )


def batched(left_op, right_op, left_dim, right_dim):
    return lax.dot_general(
        left_op,
        right_op,
        (((left_dim,), (right_dim,)), ((0,), (0,))),
        preferred_element_type=jnp.float32,
    )


def low(values):
    return values.astype(jnp.bfloat16)


def gather_rows(values):
    return lax.all_gather(values, "fsdp", axis=values.ndim - 2, tiled=True)


def sum_rows(values):
    return lax.psum_scatter(values, "fsdp", scatter_dimension=1, tiled=True)


def total(mine, other):
    return mine.astype(jnp.float32) + other.astype(jnp.float32)


def place_kernel(kinds, *refs):
    out = refs[-1]
    for kind in range(kinds):

        @pl.when(pl.program_id(0) == kind)
        def _():
            mine, other = refs[2 * kind], refs[2 * kind + 1]
            out[0] = total(mine[...], other[...])


def place(whole, group, groups, pairs):
    kinds = len(pairs)
    rows, columns = pairs[0][0].shape
    tile = min(rows, 128)
    tiles = rows // tile

    def part(kind):
        return pl.BlockSpec(
            (tile, columns),
            lambda k, j: (jnp.where(k == kind, j, jnp.where(k < kind, 0, tiles - 1)), 0),
        )

    in_specs = [part(kind) for kind in range(kinds) for _ in range(2)]
    operands = [each for pair in pairs for each in pair]
    aliases = {}
    if whole is not None:
        aliases = {len(operands): 0}
        in_specs.append(pl.BlockSpec(memory_space=pl.ANY))
        operands.append(whole)
    moved = kinds * rows * columns
    return pl.pallas_call(
        functools.partial(place_kernel, kinds),
        grid=(kinds, tiles),
        out_shape=jax.ShapeDtypeStruct((kinds, groups * rows, columns), jnp.float32),
        in_specs=in_specs,
        out_specs=pl.BlockSpec((1, tile, columns), lambda k, j: (k, group * tiles + j, 0)),
        input_output_aliases=aliases,
        cost_estimate=pl.CostEstimate(flops=moved, bytes_accessed=8 * moved, transcendentals=0),
        compiler_params=pltpu.CompilerParams(vmem_limit_bytes=24 << 20),
        name="place_%d" % group,
    )(*operands)


def swap_rep(values):
    return lax.ppermute(values, "rep", [(0, 1), (1, 0)])


def grid_of(shards):
    short = 2 if shards <= 16 else 4
    return shards // (2 * short), short


def wire_cost(times, values):
    moved = times * sum(v.size * v.dtype.itemsize for v in values)
    return pl.CostEstimate(flops=0, bytes_accessed=24 * moved + (40 << 20), transcendentals=0)


def unwritten(shape, dtype):
    return pl.pallas_call(
        lambda _: None,
        out_shape=jax.ShapeDtypeStruct(shape, dtype),
        out_specs=pl.BlockSpec(memory_space=pl.ANY),
        name="unwritten",
    )()


def neighbours(shards):
    long_len, short_len = grid_of(shards)
    me = lax.axis_index("fsdp")
    return me, me // (2 * short_len), (me // 2) % short_len, me % 2


def greet(shards, across, everyone=False):
    long_len, short_len = grid_of(shards)
    me, at_long, at_short, core = neighbours(shards)
    barrier = pltpu.get_barrier_semaphore()
    around = [
        (me >= 0, {"fsdp": me + 1 - 2 * core}),
        (at_long > 0, {"fsdp": me - 2 * short_len}),
        (at_long < long_len - 1, {"fsdp": me + 2 * short_len}),
        (at_short > 0, {"fsdp": me - 2}),
        (at_short < short_len - 1, {"fsdp": me + 2}),
    ]
    if everyone:
        around = [(me >= 0, {"fsdp": (me + far) % shards}) for far in range(1, shards)]
    if across:
        around.append((me >= 0, {"rep": 1 - lax.axis_index("rep")}))
    for has, peer in around:
        @pl.when(has)
        def _():
            pl.semaphore_signal(barrier, inc=1, device_id=peer)
    pl.semaphore_wait(barrier, sum(has.astype(jnp.int32) for has, _ in around))


def gather_kernel(shards, widths, shared, spread, *refs):
    long_len, short_len = grid_of(shards)
    count = len(widths)
    total = count + spread
    own = refs[:total]
    out = refs[total : 2 * total]
    send_sem, recv_sem, own_sem, spread_sem = refs[2 * total :]
    me, at_long, at_short, core = neighbours(shards)
    stride = 2 * short_len
    partner = {"fsdp": me + 1 - 2 * core}
    half = shared // 2
    parts = []
    if shared:
        rep = lax.axis_index("rep")
        peer_rep = {"rep": 1 - rep}
        parts.append((0, pl.multiple_of(rep * half, 128), half))
        parts.append((0, shared, widths[0] - shared))
        parts += [(k, 0, widths[k]) for k in range(1, count)]
        other = (0, pl.multiple_of((1 - rep) * half, 128), half)
    else:
        parts += [(k, 0, widths[k]) for k in range(count)]
        other = None
    lanes = list(range(len(parts)))
    away = len(parts)
    if shared:
        parts.append(other)

    def copy(lane, way, slot, peer, fresh):
        k, first, width = parts[lane]
        columns = pl.ds(first, width)
        there = out[k].at[:, slot, :, columns]
        return pltpu.make_async_remote_copy(
            src_ref=own[k].at[:, :, columns] if fresh else there,
            dst_ref=there,
            send_sem=send_sem.at[lane, way, slot],
            recv_sem=recv_sem.at[away if way == 5 else lane, slot],
            device_id=peer,
        )

    greet(shards, bool(shared), bool(spread))
    done = []

    def start(has, which, way, slot, peer, fresh=False):
        @pl.when(has)
        def _():
            for lane in which:
                copy(lane, way, slot, peer, fresh).start()

        done.append((has, which, way, slot, peer, fresh))

    def arrive(has, which, slot):
        @pl.when(has)
        def _():
            for lane in which:
                copy(lane, 0, slot, partner, False).wait_recv()

    late = []

    def got(has, slot):
        if shared:
            start(has, [0], 5, slot, peer_rep)
            late.append((has, slot))
        start(has, lanes, 4, slot, partner)

    def from_across():
        for has, slot in late:
            arrive(has, [away], slot)
            start(has, [away], 4, slot, partner)
        late.clear()

    def spread_short(has, slot, fresh=False):
        start(has & (at_short < short_len - 1), lanes, 2, slot, {"fsdp": me + 2}, fresh)
        start(has & (at_short > 0), lanes, 3, slot, {"fsdp": me - 2}, fresh)

    def short_arrivals(has, line):
        for far in range(1, short_len):
            for sign in (-1, 1):
                source = at_short + sign * far
                ok = has & (source >= 0) & (source < short_len)
                slot = me + 2 * sign * far + (line - at_long) * stride
                arrive(ok, lanes, slot)
                if far < short_len - 1:
                    onward = at_short - sign
                    start(
                        ok & (onward >= 0) & (onward < short_len),
                        lanes,
                        2 if sign < 0 else 3,
                        slot,
                        {"fsdp": me - 2 * sign},
                    )
                got(ok, slot)

    true = me >= 0
    start(at_long < long_len - 1, lanes, 0, me, {"fsdp": me + stride}, True)
    start(at_long > 0, lanes, 1, me, {"fsdp": me - stride}, True)
    spread_short(true, me, True)
    every = list(range(len(parts)))
    start(true, every, 4, me, partner, True)
    mine = [pltpu.make_async_copy(own[k], out[k].at[:, me], own_sem.at[k]) for k in range(count)]

    def share(k, peer, target):
        width = own[k].shape[2] // shards
        columns = pl.ds(pl.multiple_of(peer * width, 128), width)
        return own[k].at[:, :, columns], out[k].at[:, target]

    def dealt(k, far, back):
        peer = (me + far) % shards
        source, target = share(k, me if back else peer, peer if back else me)
        return pltpu.make_async_remote_copy(
            src_ref=source,
            dst_ref=target,
            send_sem=spread_sem.at[k - count, 0, peer],
            recv_sem=spread_sem.at[k - count, 1, peer if back else me],
            device_id={"fsdp": peer},
        )

    for k in range(count, total):
        mine.append(pltpu.make_async_copy(*share(k, me, me), own_sem.at[k]))
        for far in range(1, shards):
            dealt(k, far, False).start()
    for each in mine:
        each.start()
    for far in range(1, long_len):
        for sign in (-1, 1):
            source = at_long + sign * far
            ok = (source >= 0) & (source < long_len)
            slot = me + sign * far * stride
            arrive(ok, lanes, slot)
            onward = at_long - sign
            start(
                ok & (onward >= 0) & (onward < long_len),
                lanes,
                0 if sign < 0 else 1,
                slot,
                {"fsdp": me - sign * stride},
            )
            spread_short(ok, slot)
            got(ok, slot)
        if far == 1:
            short_arrivals(true, at_long)
        else:
            for sign in (-1, 1):
                source = at_long + sign * (far - 1)
                short_arrivals((source >= 0) & (source < long_len), source)
        if far > 1:
            from_across()
    for sign in (-1, 1):
        source = at_long + sign * (long_len - 1)
        short_arrivals((source >= 0) & (source < long_len), source)
    from_across()
    for line in range(long_len):
        for short in range(short_len):
            arrive(true, every, (line * short_len + short) * 2 + 1 - core)
    for has, which, way, slot, peer, fresh in done:
        @pl.when(has)
        def _():
            for lane in which:
                copy(lane, way, slot, peer, fresh).wait_send()
    for k in range(count, total):
        for far in range(1, shards):
            dealt(k, far, True).wait_recv()
            dealt(k, far, False).wait_send()
    for each in mine:
        each.wait()


def gather_all(shards, ident, *values, shared=0, spread=()):
    widths = tuple(v.shape[2] for v in values)
    count = len(values)
    lanes = count + (2 if shared else 0)
    shapes = [(v.shape[0], shards) + v.shape[1:] for v in values]
    dealt = []
    if spread and spread[0].shape[2] % (128 * shards):
        for v in spread:
            each = lax.all_to_all(v, "fsdp", 2, 1, tiled=True)
            dealt.append(each.reshape(v.shape[0], shards, v.shape[1], -1))
        spread = ()
    values = values + tuple(spread)
    shapes += [(v.shape[0], shards, v.shape[1], v.shape[2] // shards) for v in spread]
    results = pl.pallas_call(
        functools.partial(gather_kernel, shards, widths, shared, len(values) - count),
        out_shape=[jax.ShapeDtypeStruct(shape, v.dtype) for shape, v in zip(shapes, values)],
        in_specs=[pl.BlockSpec(memory_space=pltpu.VMEM)] * len(values),
        out_specs=[pl.BlockSpec(memory_space=pl.ANY)] * len(values),
        scratch_shapes=[
            pltpu.SemaphoreType.DMA((lanes, 6, shards)),
            pltpu.SemaphoreType.DMA((lanes, shards)),
            pltpu.SemaphoreType.DMA((len(values),)),
            pltpu.SemaphoreType.DMA((len(spread) + 1, 2, shards)),
        ],
        compiler_params=pltpu.CompilerParams(collective_id=ident, has_side_effects=True),
        cost_estimate=wire_cost(shards, values[:count]),
        name="gather_%d" % ident,
    )(*values)
    return list(results) + dealt


def scatter_kernel(shards, widths, *refs):
    long_len, short_len = grid_of(shards)
    count = len(widths)
    full = refs[:count]
    out = refs[count : 2 * count]
    held, core_in, short_in, long_in, load_sem, core_sem, short_sem, long_sem, done_sem = refs[
        2 * count :
    ]
    me, at_long, at_short, core = neighbours(shards)
    partner = {"fsdp": me + 1 - 2 * core}
    firsts = [sum(widths[:k]) for k in range(count)]

    def index(line, short):
        return line * short_len + short

    def block(k, line, short, side):
        return full[k].at[:, index(line, short) * 2 + side]

    def columns(ref, k):
        return ref.at[:, :, pl.ds(firsts[k], widths[k])]

    order = []
    for far in range(long_len - 1, 0, -1):
        for sign in (-1, 1):
            line = at_long + sign * far
            order.append(((line >= 0) & (line < long_len), line, far, sign))
    order.append((me >= 0, at_long, 0, 0))
    shorts = []
    for far in range(short_len - 1, 0, -1):
        for sign in (-1, 1):
            short = at_short + sign * far
            shorts.append(((short >= 0) & (short < short_len), short, far, sign))
    shorts.append((me >= 0, at_short, 0, 0))

    def to_core(k, line, short):
        return pltpu.make_async_remote_copy(
            src_ref=block(k, line, short, 1 - core),
            dst_ref=columns(core_in.at[index(line, short)], k),
            send_sem=core_sem.at[0, k, index(line, short)],
            recv_sem=core_sem.at[1, k, index(line, short)],
            device_id=partner,
        )

    def load(k, line, short):
        return pltpu.make_async_copy(
            block(k, line, short, core),
            columns(held.at[index(line, short)], k),
            load_sem.at[k, index(line, short)],
        )

    def along_short(line, short, sign):
        return pltpu.make_async_remote_copy(
            src_ref=held.at[index(line, short)],
            dst_ref=short_in.at[(1 - sign) // 2, index(line, short)],
            send_sem=short_sem.at[0, index(line, short)],
            recv_sem=short_sem.at[1 + (1 - sign) // 2, index(line, short)],
            device_id={"fsdp": me + 2 * sign},
        )

    def along_long(line, sign):
        return pltpu.make_async_remote_copy(
            src_ref=held.at[index(line, at_short)],
            dst_ref=long_in.at[(1 - sign) // 2, line],
            send_sem=long_sem.at[0, line],
            recv_sem=long_sem.at[1 + (1 - sign) // 2, line],
            device_id={"fsdp": me + 2 * short_len * sign},
        )

    def add(to_ref, from_ref):
        batch, rows, _ = to_ref.shape
        step = 16

        @pl.loop(0, batch * rows // step)
        def _(at):
            one = at // (rows // step)
            where = pl.ds(pl.multiple_of((at % (rows // step)) * step, step), step)
            to_ref[one, where, :] = (
                to_ref[one, where, :].astype(jnp.float32)
                + from_ref[one, where, :].astype(jnp.float32)
            ).astype(jnp.bfloat16)

    for near, short, far, sign in shorts:
        for has, line, _, _ in order:
            @pl.when(near & has)
            def _():
                for k in range(count):
                    load(k, line, short).start()

    greet(shards, False)
    for near, short, far, sign in shorts:
        for has, line, _, _ in order:
            @pl.when(near & has)
            def _():
                for k in range(count):
                    to_core(k, line, short).start()

    for near, short, far, sign in shorts:
        for has, line, far_line, sign_line in order:
            @pl.when(near & has)
            def _():
                at = index(line, short)
                for k in range(count):
                    load(k, line, short).wait()
                    to_core(k, line, short).wait_recv()
                add(held.at[at], core_in.at[at])
                if far:
                    behind = at_short - sign

                    @pl.when((behind >= 0) & (behind < short_len))
                    def _():
                        along_short(line, short, sign).wait_recv()
                        add(held.at[at], short_in.at[(1 - sign) // 2, at])

                    along_short(line, short, sign).start()
                else:
                    for way in (-1, 1):
                        behind = at_short - way

                        @pl.when((behind >= 0) & (behind < short_len))
                        def _():
                            along_short(line, short, way).wait_recv()
                            add(held.at[at], short_in.at[(1 - way) // 2, at])

                    for way in (-1, 1) if not far_line else (sign_line,):
                        behind = at_long - way

                        @pl.when((behind >= 0) & (behind < long_len))
                        def _():
                            along_long(line, way).wait_recv()
                            add(held.at[at], long_in.at[(1 - way) // 2, line])

                    if far_line:
                        along_long(line, sign_line).start()

    results = [
        pltpu.make_async_copy(columns(held.at[index(at_long, at_short)], k), out[k], done_sem.at[k])
        for k in range(count)
    ]
    for each in results:
        each.start()
    for near, short, far, sign in shorts:
        for has, line, far_line, sign_line in order:
            @pl.when(near & has)
            def _():
                for k in range(count):
                    to_core(k, line, short).wait_send()
                if far:
                    along_short(line, short, sign).wait_send()
                elif far_line:
                    along_long(line, sign_line).wait_send()
    for each in results:
        each.wait()


def scatter_sum(shards, ident, *values):
    batch, _, rows, _ = values[0].shape
    widths = tuple(v.shape[3] for v in values)
    if shards > 16:
        return [
            sum_rows(v.reshape(batch, shards * rows, w)) for v, w in zip(values, widths)
        ]
    count = len(values)
    long_len, short_len = grid_of(shards)
    pairs = shards // 2
    block = (batch, rows, sum(widths))
    return pl.pallas_call(
        functools.partial(scatter_kernel, shards, widths),
        out_shape=[jax.ShapeDtypeStruct((batch, rows, w), jnp.bfloat16) for w in widths],
        in_specs=[pl.BlockSpec(memory_space=pl.ANY)] * count,
        out_specs=[pl.BlockSpec(memory_space=pl.ANY)] * count,
        scratch_shapes=[
            pltpu.VMEM((pairs,) + block, jnp.bfloat16),
            pltpu.VMEM((pairs,) + block, jnp.bfloat16),
            pltpu.VMEM((2, pairs) + block, jnp.bfloat16),
            pltpu.VMEM((2, long_len) + block, jnp.bfloat16),
            pltpu.SemaphoreType.DMA((count, pairs)),
            pltpu.SemaphoreType.DMA((2, count, pairs)),
            pltpu.SemaphoreType.DMA((3, pairs)),
            pltpu.SemaphoreType.DMA((3, long_len)),
            pltpu.SemaphoreType.DMA((count,)),
        ],
        compiler_params=pltpu.CompilerParams(
            collective_id=ident, has_side_effects=True, vmem_limit_bytes=60 << 20
        ),
        cost_estimate=wire_cost(1, values),
        name="scatter_%d" % ident,
    )(*values)


def product_kernel(shards, gate, up, weight, out, *scratch):
    planes, pair, core_in, short_in, long_in = scratch[:5]
    plane_sem, core_sem, short_sem, long_sem, done_sem = scratch[5:]
    long_len, _ = grid_of(shards)
    me, at_long, at_short, core = neighbours(shards)
    rows = pair.shape[3]
    load = pltpu.make_async_copy(weight.at[pl.ds(0, 2)], planes, plane_sem)
    load.start()

    lines = []
    first, last = me * 0, me * 0 + long_len - 1
    for _ in range(long_len - 1):
        up_side = (last - at_long >= at_long - first).astype(jnp.int32)
        lines.append((first + up_side * (last - first), 2 * up_side - 1))
        first, last = first + 1 - up_side, last - up_side
    lines.append((at_long, None))
    steps = [(line, sign, 1 - at_short) for line, sign in lines]
    steps += [(line, sign, at_short) for line, sign in lines]

    def held(at):
        return pair.at[at, :, core]

    def compute(at):
        where = pl.ds(pl.multiple_of(at * 2 * rows, 2 * rows), 2 * rows)
        left = gate[:, where, :].reshape(4 * rows, gate.shape[2])
        right = up[:, where, :].reshape(4 * rows, up.shape[2])

        @pl.loop(0, pair.shape[4] // 512)
        def _(tile):
            columns = pl.ds(pl.multiple_of(tile * 512, 512), 512)
            sums = jnp.dot(left, planes[0, :, columns], preferred_element_type=jnp.float32)
            sums += jnp.dot(right, planes[1, :, columns], preferred_element_type=jnp.float32)
            pair[at, :, :, :, columns] = sums.astype(jnp.bfloat16).reshape(2, 2, rows, 512)

    def to_core(at):
        return pltpu.make_async_remote_copy(
            src_ref=pair.at[at, :, 1 - core],
            dst_ref=core_in.at[at],
            send_sem=core_sem.at[0, at],
            recv_sem=core_sem.at[1, at],
            device_id={"fsdp": me + 1 - 2 * core},
        )

    def along_short(line, short):
        return pltpu.make_async_remote_copy(
            src_ref=held(line * 2 + short),
            dst_ref=short_in.at[line],
            send_sem=short_sem.at[0, line],
            recv_sem=short_sem.at[1, line],
            device_id={"fsdp": me + 2 - 4 * at_short},
        )

    def along_long(line, sign):
        return pltpu.make_async_remote_copy(
            src_ref=held(line * 2 + at_short),
            dst_ref=long_in.at[(1 - sign) // 2, line],
            send_sem=long_sem.at[0, line],
            recv_sem=long_sem.at[1 + (1 - sign) // 2, line],
            device_id={"fsdp": me + 4 * sign},
        )

    def add(at, other):
        @pl.loop(0, 2 * rows // 16)
        def _(group):
            one = group // (rows // 16)
            where = pl.ds(pl.multiple_of((group % (rows // 16)) * 16, 16), 16)
            pair[at, one, core, where, :] = (
                pair[at, one, core, where, :].astype(jnp.float32)
                + other[one, where, :].astype(jnp.float32)
            ).astype(jnp.bfloat16)

    def from_behind(at, line, sign):
        behind = at_long - sign

        @pl.when((behind >= 0) & (behind < long_len))
        def _():
            along_long(line, sign).wait_recv()
            add(at, long_in.at[(1 - sign) // 2, line])

    def settle(at_step):
        line, sign, short = steps[at_step]
        at = line * 2 + short
        to_core(at).wait_recv()
        add(at, core_in.at[at])
        if at_step < long_len:
            along_short(line, short).start()
            return
        along_short(line, short).wait_recv()
        add(at, short_in.at[line])
        if sign is None:
            from_behind(at, line, 1)
            from_behind(at, line, -1)
        else:
            from_behind(at, line, sign)
            along_long(line, sign).start()

    greet(shards, False)
    load.wait()
    for at_step, (line, _, short) in enumerate(steps):
        compute(line * 2 + short)
        to_core(line * 2 + short).start()
        if at_step:
            settle(at_step - 1)
    settle(len(steps) - 1)
    result = pltpu.make_async_copy(held(at_long * 2 + at_short), out, done_sem)
    result.start()
    for at_step, (line, sign, short) in enumerate(steps):
        to_core(line * 2 + short).wait_send()
        if at_step < long_len:
            along_short(line, short).wait_send()
        elif sign is not None:
            along_long(line, sign).wait_send()
    result.wait()


def product_sum(shards, ident, gate, up, weight):
    batch, every, units = gate.shape
    columns = weight.shape[2]
    rows = every // shards
    long_len, short_len = grid_of(shards)
    block = (batch, rows, columns)
    pairs = shards // 2
    return pl.pallas_call(
        functools.partial(product_kernel, shards),
        out_shape=jax.ShapeDtypeStruct(block, jnp.bfloat16),
        in_specs=[
            pl.BlockSpec(memory_space=pltpu.VMEM),
            pl.BlockSpec(memory_space=pltpu.VMEM),
            pl.BlockSpec(memory_space=pl.ANY),
        ],
        out_specs=pl.BlockSpec(memory_space=pl.ANY),
        scratch_shapes=[
            pltpu.VMEM((2, units, columns), jnp.bfloat16),
            pltpu.VMEM((pairs, batch, 2, rows, columns), jnp.bfloat16),
            pltpu.VMEM((pairs,) + block, jnp.bfloat16),
            pltpu.VMEM((long_len,) + block, jnp.bfloat16),
            pltpu.VMEM((2, long_len) + block, jnp.bfloat16),
            pltpu.SemaphoreType.DMA,
            pltpu.SemaphoreType.DMA((2, pairs)),
            pltpu.SemaphoreType.DMA((2, long_len)),
            pltpu.SemaphoreType.DMA((3, long_len)),
            pltpu.SemaphoreType.DMA,
        ],
        compiler_params=pltpu.CompilerParams(
            collective_id=ident, has_side_effects=True, vmem_limit_bytes=60 << 20
        ),
        cost_estimate=wire_cost(shards, [jax.ShapeDtypeStruct(block, jnp.bfloat16)]),
        name="product_%d" % ident,
    )(gate, up, weight)


def local(
    tokens, segment_ids, norm_gains, attn_weight, adapter, ffn_weight, ffn_adapter, cotangent
):
    micro, local_len, model_dim = tokens.shape
    shards = lax.axis_size("fsdp")
    me = lax.axis_index("fsdp")
    seq_len = local_len * shards
    offset = me * local_len
    count = micro * local_len
    every = micro * seq_len
    q_width = HEADS * HD
    kv_end = q_width + 2 * HD
    score_scale = HD ** (-0.5)
    hidden_cols = ffn_weight.shape[0]
    attn_rows = attn_weight.shape[0]

    seg_cols = count // attn_rows
    seg_block = low(segment_ids).reshape(attn_rows, seg_cols)
    spare = jnp.zeros((attn_rows, 128 - 2 - seg_cols), jnp.bfloat16)
    small = jnp.concatenate([norm_gains, seg_block, spare], axis=1)
    same = kv_end + 4 * RANK
    attn_all, adapter_all, small_all = gather_all(
        shards, 1, attn_weight[None], adapter[None], small[None], shared=same
    )
    cotangent_now, small_all = lax.optimization_barrier((cotangent, small_all))
    cot_all = gather_rows(cotangent_now).reshape(every, model_dim)
    attn_all = attn_all.reshape(model_dim, attn_weight.shape[1])
    adapter_all = adapter_all.reshape(model_dim, 3 * RANK)
    small_all = small_all.reshape(model_dim, 128)
    w_proj = attn_all[:, :kv_end]
    w_out = attn_all[:, kv_end:]
    a_q, bq_t, bd_t = (adapter_all[:, j * RANK : (j + 1) * RANK] for j in range(3))
    gain_two = small_all[:, :2].astype(jnp.float32)
    seg_all = small_all[:, 2 : 2 + seg_cols].reshape(shards, micro, local_len)
    seg_all = seg_all.transpose(1, 0, 2).reshape(micro, seq_len).astype(jnp.int32)

    hidden_in = tokens.reshape(count, model_dim).astype(jnp.float32)
    key_index = jnp.arange(seq_len, dtype=jnp.int32)
    query_index = offset + jnp.arange(local_len, dtype=jnp.int32)
    before = jnp.sum(
        (seg_all[:, None, :] < segment_ids[:, :, None]).astype(jnp.int32), axis=2
    )
    angles = angles_of(query_index[None, :] - before).reshape(count, HD // 2)
    normed, norm_back_one = jax.vjp(rms_scale, hidden_in, gain_two[:, 0])
    normed_low = low(normed)
    projected = contract(normed_low, w_proj, 1, 0)
    query_low = low(contract(normed_low, a_q, 1, 0))
    query_pre = projected[:, :q_width] + contract(query_low, bq_t, 1, 1)
    queries = low(rotate(query_pre.reshape(count, HEADS, HD), angles[:, None, :]))
    queries = queries.reshape(micro, local_len * HEADS, HD)
    keys_low = low(rotate(projected[:, q_width : q_width + HD], angles))
    values_low = low(projected[:, q_width + HD :])
    keys_all, values_all = (
        each.reshape(micro, seq_len, -1)
        for each in gather_all(
            shards,
            2,
            keys_low.reshape(micro, local_len, HD),
            values_low.reshape(micro, local_len, HD),
        )
    )
    allowed = (
        (segment_ids[:, :, None] == seg_all[:, None, :])
        & (key_index[None, None, :] <= query_index[None, :, None])
    )[:, :, None, :]
    scores = (batched(queries, keys_all, 2, 2) * score_scale).reshape(
        micro, local_len, HEADS, seq_len
    )
    scores = jnp.where(allowed, scores, -1e30)
    top_score = jnp.max(scores, axis=-1, keepdims=True)
    exp_scores = jnp.exp(scores - top_score)
    weights = exp_scores / jnp.sum(exp_scores, axis=-1, keepdims=True)
    weights_low = low(weights).reshape(micro, local_len * HEADS, seq_len)
    context = low(batched(weights_low, values_all, 2, 1)).reshape(count, q_width)
    mixed_sum = hidden_in + contract(context, w_out, 1, 1)
    normed_two, norm_back_two = jax.vjp(rms_scale, mixed_sum, gain_two[:, 1])
    (inputs_all,) = gather_all(shards, 3, low(normed_two).reshape(micro, local_len, model_dim))
    inputs_all = inputs_all.reshape(every, model_dim)
    kept, inputs_all = lax.optimization_barrier(
        (jnp.concatenate([context, query_low], axis=1), inputs_all)
    )
    kept_all = gather_rows(kept.reshape(micro, local_len, q_width + RANK))
    kept_all = kept_all.reshape(every, q_width + RANK)
    low_grad_all = low(contract(cot_all, bd_t, 1, 0))

    step = hidden_cols // CHUNKS
    hidden_parts, gate_parts, up_parts = [], [], []
    for at in range(CHUNKS):
        units = slice(at * step, (at + 1) * step)
        w_gate, w_up, w_down = (ffn_weight[units, j, :] for j in range(3))
        gate_pre = contract(inputs_all, w_gate, 1, 1)
        up_pre = contract(inputs_all, w_up, 1, 1)
        activated, gelu_back = jax.vjp(gelu_tanh, gate_pre)
        hidden_act = low(activated * up_pre)
        hidden_grad = contract(cot_all, w_down, 1, 1) + contract(
            low_grad_all, ffn_adapter[units], 1, 1
        )
        gate_grad = low(gelu_back(hidden_grad * up_pre)[0])
        up_grad = low(hidden_grad * activated)
        hidden_parts.append(hidden_act)
        gate_parts.append(gate_grad)
        up_parts.append(up_grad)

    gate_grad = jnp.concatenate(gate_parts, axis=1)
    up_grad = jnp.concatenate(up_parts, axis=1)
    hidden_act = jnp.concatenate(hidden_parts, axis=1)
    step = hidden_cols // PIECES

    def weight_grads(at, gate_now, up_now, hidden_now):
        units = slice(at * step, (at + 1) * step)
        made = []
        for left, right in (
            (gate_now, inputs_all),
            (up_now, inputs_all),
            (hidden_now, cot_all),
        ):
            mine = low(contract(left[:, units], right, 0, 0))
            made.append((mine, swap_rep(mine)))
        return made

    ffn_parts = weight_grads(0, gate_grad, up_grad, hidden_act)
    down_part = low(contract(hidden_act, ffn_weight[:, 2, :], 1, 0))
    low_part = low(contract(hidden_act, ffn_adapter, 1, 0))
    gate_grad, up_grad, kept_all, down_part, low_part, _ = lax.optimization_barrier(
        (gate_grad, up_grad, kept_all, down_part, low_part, [pair[0] for pair in ffn_parts])
    )
    if grid_of(shards)[1] == 2 and micro == 2:
        normed_two_grad = product_sum(
            shards,
            5,
            gate_grad.reshape(micro, seq_len, hidden_cols),
            up_grad.reshape(micro, seq_len, hidden_cols),
            ffn_weight.transpose(1, 0, 2),
        )
    else:
        (normed_two_grad,) = scatter_sum(
            shards,
            5,
            low(
                contract(gate_grad, ffn_weight[:, 0, :], 1, 0)
                + contract(up_grad, ffn_weight[:, 1, :], 1, 0)
            ).reshape(micro, shards, local_len, model_dim),
        )
    normed_two_grad, down_part, gate_grad, up_grad, hidden_act, _ = lax.optimization_barrier(
        (
            normed_two_grad,
            down_part,
            gate_grad,
            up_grad,
            hidden_act,
            [pair[1] for pair in ffn_parts[:2]],
        )
    )
    down_sum = sum_rows(down_part.reshape(micro, seq_len, model_dim))
    ffn_parts += weight_grads(1, gate_grad, up_grad, hidden_act)
    low_mine = low(contract(hidden_act, low_grad_all, 0, 0))
    low_other = swap_rep(low_mine)
    normed_two_grad, low_part, low_mine, _ = lax.optimization_barrier(
        (normed_two_grad, low_part, low_mine, [pair[0] for pair in ffn_parts])
    )
    normed_two_grad = normed_two_grad.reshape(count, model_dim).astype(jnp.float32)
    cot_full = cotangent.reshape(count, model_dim).astype(jnp.float32)
    mixed_part, gain_two_grad = norm_back_two(normed_two_grad)
    mixed_grad = cot_full + mixed_part
    out_grad_low = low(mixed_grad)
    context_grad = contract(out_grad_low, w_out, 1, 0)
    context_rows = low(context_grad).reshape(micro, local_len * HEADS, HD)
    prob_grad = batched(context_rows, values_all, 2, 2).reshape(micro, local_len, HEADS, seq_len)
    score_grad = weights * (prob_grad - jnp.sum(weights * prob_grad, axis=-1, keepdims=True))
    score_grad = low(score_grad).reshape(micro, local_len * HEADS, seq_len)
    query_grad = batched(score_grad, keys_all, 2, 1) * score_scale
    query_grad = query_grad.reshape(count, HEADS, HD)
    query_pre_grad = low(rotate(query_grad, -angles[:, None, :]).reshape(count, q_width))
    key_part = low(batched(score_grad, queries, 1, 1) * score_scale)
    value_part = low(batched(weights_low, context_rows, 1, 1))
    key_part, value_part, query_pre_grad, ffn_parts[2:3] = lax.optimization_barrier(
        (key_part, value_part, query_pre_grad, ffn_parts[2:3])
    )
    q_all = gather_rows(query_pre_grad.reshape(micro, local_len, q_width))
    q_all = q_all.reshape(every, q_width)
    key_sum, value_sum, down_low = (
        each.reshape(count, -1)
        for each in scatter_sum(
            shards,
            6,
            *(
                each.reshape(micro, shards, local_len, -1)
                for each in (key_part, value_part, low_part)
            ),
        )
    )
    result = (
        mixed_sum
        + down_sum.reshape(count, model_dim).astype(jnp.float32)
        + contract(down_low, bd_t, 1, 1)
    )
    key_grad = low(rotate(key_sum.astype(jnp.float32), -angles))
    value_grad = value_sum
    rank_grad = low(contract(query_pre_grad, bq_t, 1, 0))
    proj_grad = jnp.concatenate([query_pre_grad, key_grad, value_grad], axis=1)
    normed_grad = contract(proj_grad, w_proj, 1, 1) + contract(rank_grad, a_q, 1, 1)
    hidden_part, gain_one_grad = norm_back_one(normed_grad)
    input_grad = low(mixed_grad + hidden_part)

    narrow = jnp.concatenate([key_grad, value_grad, rank_grad, down_low], axis=1)
    narrow, ffn_parts[3:4] = lax.optimization_barrier((narrow, ffn_parts[3:4]))
    gain_parts = jnp.zeros((1, 16, model_dim), jnp.bfloat16)
    gain_parts = gain_parts.at[0, 0].set(low(gain_one_grad)).at[0, 1].set(low(gain_two_grad))
    narrow_all, normed_cols, out_cols, gain_cols = gather_all(
        shards,
        4,
        narrow.reshape(micro, local_len, 2 * HD + 2 * RANK),
        spread=(
            normed_low.reshape(micro, local_len, model_dim),
            out_grad_low.reshape(micro, local_len, model_dim),
            gain_parts,
        ),
    )
    narrow_all, ffn_parts[:3] = lax.optimization_barrier((narrow_all, ffn_parts[:3]))
    ffn_grad = place(None, 0, PIECES, ffn_parts[:3])
    narrow_all = narrow_all.reshape(every, 2 * HD + 2 * RANK)
    normed_cols = normed_cols.reshape(every, attn_rows)
    wout_grad = contract(out_cols.reshape(every, attn_rows), kept_all[:, :q_width], 0, 0)
    gain_now = jnp.sum(gain_cols[0, :, :2].astype(jnp.float32), axis=0)
    my_cols = me * attn_rows
    attn_q = low(contract(normed_cols, q_all, 0, 0))
    attn_rest = contract(normed_cols, narrow_all[:, : 2 * HD + RANK], 0, 0)
    bq_grad = contract(
        lax.dynamic_slice_in_dim(q_all, my_cols, attn_rows, 1), kept_all[:, q_width:], 0, 0
    )
    bd_grad = contract(
        lax.dynamic_slice_in_dim(cot_all, my_cols, attn_rows, 1),
        narrow_all[:, 2 * HD + RANK :],
        0,
        0,
    )
    tail = low(jnp.concatenate([attn_rest, bq_grad, bd_grad], axis=1))
    tail_out = low(wout_grad)
    tail_gain = low(gain_now)
    crossing = [swap_rep(each) for each in (tail_out, tail, attn_q)]
    attn_q, tail, tail_out, ffn_parts[3:], low_mine, low_other = lax.optimization_barrier(
        (attn_q, tail, tail_out, ffn_parts[3:], low_mine, low_other)
    )
    gains_grad = total(tail_gain, swap_rep(tail_gain)).transpose(1, 0)
    ffn_grad = place(ffn_grad, 1, PIECES, ffn_parts[3:])
    ffn_grad = ffn_grad.transpose(1, 0, 2)
    ffn_low_grad = total(low_mine, low_other)
    tail = total(tail, crossing[1])
    attn_grad = unwritten(attn_weight.shape, jnp.float32)
    for first, part in (
        (kv_end, total(tail_out, crossing[0])),
        (q_width, tail[:, : 2 * HD]),
        (0, total(attn_q, crossing[2])),
    ):
        attn_grad = lax.dynamic_update_slice(attn_grad, part, (0, first))
    adapter_grad = tail[:, 2 * HD :]
    return (
        low(result).reshape(micro, local_len, model_dim),
        input_grad.reshape(micro, local_len, model_dim),
        gains_grad,
        attn_grad,
        adapter_grad,
        ffn_grad,
        ffn_low_grad,
    )


def solution(mesh):
    placed = (
        P("rep", "fsdp", None),
        P("rep", "fsdp"),
        P("fsdp", None),
        P("fsdp", None),
        P("fsdp", None),
        P("fsdp", None, None),
        P("fsdp", None),
        P("rep", "fsdp", None),
    )
    return jax.shard_map(
        local,
        mesh=mesh,
        in_specs=placed,
        out_specs=(
            P("rep", "fsdp", None),
            P("rep", "fsdp", None),
            P("fsdp", None),
            P("fsdp", None),
            P("fsdp", None),
            P("fsdp", None, None),
            P("fsdp", None),
        ),
        check_vma=False,
    )
```

```python
import functools

import jax
import jax.numpy as jnp
from jax import lax
from jax.experimental import pallas as pl
from jax.experimental.pallas import tpu as pltpu
from jax.sharding import PartitionSpec as P

HEADS = 8
HD = 256
RANK = 256
CHUNKS = 1
PIECES = 2


epsilon = 1e-06


def rms_scale(values, gain_col):
    return (
        values * lax.rsqrt(jnp.mean(values * values, axis=-1, keepdims=True) + epsilon) * gain_col
    )


def angles_of(positions):
    inverse_freq = 10000.0 ** (-2.0 * jnp.arange(HD // 2, dtype=jnp.float32) / HD)
    return positions.astype(jnp.float32)[..., None] * inverse_freq


def rotate(field_in, angles):
    half_dim = field_in.shape[-1] // 2
    cosine = jnp.cos(angles)
    sine_part = jnp.sin(angles)
    lower_half = field_in[..., :half_dim]
    upper_half = field_in[..., half_dim:]
    return jnp.concatenate(
        [
            lower_half * cosine - upper_half * sine_part,
            upper_half * cosine + lower_half * sine_part,
        ],
        axis=-1,
    )


def gelu_tanh(values):
    return jax.nn.gelu(values, approximate=True)


def contract(left_op, right_op, left_dim, right_dim):
    return lax.dot_general(
        left_op,
        right_op,
        (((left_dim,), (right_dim,)), ((), ())),
        preferred_element_type=jnp.float32,
    )


def batched(left_op, right_op, left_dim, right_dim):
    return lax.dot_general(
        left_op,
        right_op,
        (((left_dim,), (right_dim,)), ((0,), (0,))),
        preferred_element_type=jnp.float32,
    )


def low(values):
    return values.astype(jnp.bfloat16)


def gather_rows(values):
    return lax.all_gather(values, "fsdp", axis=values.ndim - 2, tiled=True)


def sum_rows(values):
    return lax.psum_scatter(values, "fsdp", scatter_dimension=1, tiled=True)


def total(mine, other):
    return mine.astype(jnp.float32) + other.astype(jnp.float32)


def place_kernel(kinds, *refs):
    out = refs[-1]
    for kind in range(kinds):

        @pl.when(pl.program_id(0) == kind)
        def _():
            mine, other = refs[2 * kind], refs[2 * kind + 1]
            out[0] = total(mine[...], other[...])


def place(whole, group, groups, pairs):
    kinds = len(pairs)
    rows, columns = pairs[0][0].shape
    tile = min(rows, 256)
    tiles = rows // tile

    def part(kind):
        return pl.BlockSpec(
            (tile, columns),
            lambda k, j: (jnp.where(k == kind, j, jnp.where(k < kind, 0, tiles - 1)), 0),
        )

    in_specs = [part(kind) for kind in range(kinds) for _ in range(2)]
    operands = [each for pair in pairs for each in pair]
    aliases = {}
    if whole is not None:
        aliases = {len(operands): 0}
        in_specs.append(pl.BlockSpec(memory_space=pl.ANY))
        operands.append(whole)
    moved = kinds * rows * columns
    return pl.pallas_call(
        functools.partial(place_kernel, kinds),
        grid=(kinds, tiles),
        out_shape=jax.ShapeDtypeStruct((kinds, groups * rows, columns), jnp.float32),
        in_specs=in_specs,
        out_specs=pl.BlockSpec((1, tile, columns), lambda k, j: (k, group * tiles + j, 0)),
        input_output_aliases=aliases,
        cost_estimate=pl.CostEstimate(flops=moved, bytes_accessed=8 * moved, transcendentals=0),
        compiler_params=pltpu.CompilerParams(vmem_limit_bytes=24 << 20),
        name="place_%d" % group,
    )(*operands)


def swap_rep(values):
    return lax.ppermute(values, "rep", [(0, 1), (1, 0)])


def grid_of(shards):
    short = 2 if shards <= 16 else 4
    return shards // (2 * short), short


def wire_cost(times, values):
    moved = times * sum(v.size * v.dtype.itemsize for v in values)
    return pl.CostEstimate(flops=0, bytes_accessed=24 * moved + (40 << 20), transcendentals=0)


def unwritten(shape, dtype):
    return pl.pallas_call(
        lambda _: None,
        out_shape=jax.ShapeDtypeStruct(shape, dtype),
        out_specs=pl.BlockSpec(memory_space=pl.ANY),
        name="unwritten",
    )()


def neighbours(shards):
    long_len, short_len = grid_of(shards)
    me = lax.axis_index("fsdp")
    return me, me // (2 * short_len), (me // 2) % short_len, me % 2


def greet(shards, across, everyone=False):
    long_len, short_len = grid_of(shards)
    me, at_long, at_short, core = neighbours(shards)
    barrier = pltpu.get_barrier_semaphore()
    around = [
        (me >= 0, {"fsdp": me + 1 - 2 * core}),
        (at_long > 0, {"fsdp": me - 2 * short_len}),
        (at_long < long_len - 1, {"fsdp": me + 2 * short_len}),
        (at_short > 0, {"fsdp": me - 2}),
        (at_short < short_len - 1, {"fsdp": me + 2}),
    ]
    if everyone:
        around = [(me >= 0, {"fsdp": (me + far) % shards}) for far in range(1, shards)]
    if across:
        around.append((me >= 0, {"rep": 1 - lax.axis_index("rep")}))
    for has, peer in around:
        @pl.when(has)
        def _():
            pl.semaphore_signal(barrier, inc=1, device_id=peer)
    pl.semaphore_wait(barrier, sum(has.astype(jnp.int32) for has, _ in around))


def gather_kernel(shards, widths, shared, spread, *refs):
    long_len, short_len = grid_of(shards)
    count = len(widths)
    total = count + spread
    own = refs[:total]
    out = refs[total : 2 * total]
    send_sem, recv_sem, own_sem, spread_sem = refs[2 * total :]
    me, at_long, at_short, core = neighbours(shards)
    stride = 2 * short_len
    partner = {"fsdp": me + 1 - 2 * core}
    half = shared // 2
    parts = []
    if shared:
        rep = lax.axis_index("rep")
        peer_rep = {"rep": 1 - rep}
        parts.append((0, pl.multiple_of(rep * half, 128), half))
        parts.append((0, shared, widths[0] - shared))
        parts += [(k, 0, widths[k]) for k in range(1, count)]
        other = (0, pl.multiple_of((1 - rep) * half, 128), half)
    else:
        parts += [(k, 0, widths[k]) for k in range(count)]
        other = None
    lanes = list(range(len(parts)))
    away = len(parts)
    if shared:
        parts.append(other)

    def copy(lane, way, slot, peer, fresh):
        k, first, width = parts[lane]
        columns = pl.ds(first, width)
        there = out[k].at[:, slot, :, columns]
        return pltpu.make_async_remote_copy(
            src_ref=own[k].at[:, :, columns] if fresh else there,
            dst_ref=there,
            send_sem=send_sem.at[lane, way, slot],
            recv_sem=recv_sem.at[away if way == 5 else lane, slot],
            device_id=peer,
        )

    greet(shards, bool(shared), bool(spread))
    done = []

    def start(has, which, way, slot, peer, fresh=False):
        @pl.when(has)
        def _():
            for lane in which:
                copy(lane, way, slot, peer, fresh).start()

        done.append((has, which, way, slot, peer, fresh))

    def arrive(has, which, slot):
        @pl.when(has)
        def _():
            for lane in which:
                copy(lane, 0, slot, partner, False).wait_recv()

    late = []

    def got(has, slot):
        if shared:
            start(has, [0], 5, slot, peer_rep)
            late.append((has, slot))
        start(has, lanes, 4, slot, partner)

    def from_across():
        for has, slot in late:
            arrive(has, [away], slot)
            start(has, [away], 4, slot, partner)
        late.clear()

    def spread_short(has, slot, fresh=False):
        start(has & (at_short < short_len - 1), lanes, 2, slot, {"fsdp": me + 2}, fresh)
        start(has & (at_short > 0), lanes, 3, slot, {"fsdp": me - 2}, fresh)

    def short_arrivals(has, line):
        for far in range(1, short_len):
            for sign in (-1, 1):
                source = at_short + sign * far
                ok = has & (source >= 0) & (source < short_len)
                slot = me + 2 * sign * far + (line - at_long) * stride
                arrive(ok, lanes, slot)
                if far < short_len - 1:
                    onward = at_short - sign
                    start(
                        ok & (onward >= 0) & (onward < short_len),
                        lanes,
                        2 if sign < 0 else 3,
                        slot,
                        {"fsdp": me - 2 * sign},
                    )
                got(ok, slot)

    true = me >= 0
    start(at_long < long_len - 1, lanes, 0, me, {"fsdp": me + stride}, True)
    start(at_long > 0, lanes, 1, me, {"fsdp": me - stride}, True)
    spread_short(true, me, True)
    every = list(range(len(parts)))
    start(true, every, 4, me, partner, True)
    mine = [pltpu.make_async_copy(own[k], out[k].at[:, me], own_sem.at[k]) for k in range(count)]

    def share(k, peer, target):
        width = own[k].shape[2] // shards
        columns = pl.ds(pl.multiple_of(peer * width, 128), width)
        return own[k].at[:, :, columns], out[k].at[:, target]

    def dealt(k, far, back):
        peer = (me + far) % shards
        source, target = share(k, me if back else peer, peer if back else me)
        return pltpu.make_async_remote_copy(
            src_ref=source,
            dst_ref=target,
            send_sem=spread_sem.at[k - count, 0, peer],
            recv_sem=spread_sem.at[k - count, 1, peer if back else me],
            device_id={"fsdp": peer},
        )

    for k in range(count, total):
        mine.append(pltpu.make_async_copy(*share(k, me, me), own_sem.at[k]))
        for far in range(1, shards):
            dealt(k, far, False).start()
    for each in mine:
        each.start()
    for far in range(1, long_len):
        for sign in (-1, 1):
            source = at_long + sign * far
            ok = (source >= 0) & (source < long_len)
            slot = me + sign * far * stride
            arrive(ok, lanes, slot)
            onward = at_long - sign
            start(
                ok & (onward >= 0) & (onward < long_len),
                lanes,
                0 if sign < 0 else 1,
                slot,
                {"fsdp": me - sign * stride},
            )
            spread_short(ok, slot)
            got(ok, slot)
        if far == 1:
            short_arrivals(true, at_long)
        else:
            for sign in (-1, 1):
                source = at_long + sign * (far - 1)
                short_arrivals((source >= 0) & (source < long_len), source)
        if far > 1:
            from_across()
    for sign in (-1, 1):
        source = at_long + sign * (long_len - 1)
        short_arrivals((source >= 0) & (source < long_len), source)
    from_across()
    for line in range(long_len):
        for short in range(short_len):
            arrive(true, every, (line * short_len + short) * 2 + 1 - core)
    for has, which, way, slot, peer, fresh in done:
        @pl.when(has)
        def _():
            for lane in which:
                copy(lane, way, slot, peer, fresh).wait_send()
    for k in range(count, total):
        for far in range(1, shards):
            dealt(k, far, True).wait_recv()
            dealt(k, far, False).wait_send()
    for each in mine:
        each.wait()


def gather_all(shards, ident, *values, shared=0, spread=()):
    widths = tuple(v.shape[2] for v in values)
    count = len(values)
    lanes = count + (2 if shared else 0)
    shapes = [(v.shape[0], shards) + v.shape[1:] for v in values]
    dealt = []
    if spread and spread[0].shape[2] % (128 * shards):
        for v in spread:
            each = lax.all_to_all(v, "fsdp", 2, 1, tiled=True)
            dealt.append(each.reshape(v.shape[0], shards, v.shape[1], -1))
        spread = ()
    values = values + tuple(spread)
    shapes += [(v.shape[0], shards, v.shape[1], v.shape[2] // shards) for v in spread]
    results = pl.pallas_call(
        functools.partial(gather_kernel, shards, widths, shared, len(values) - count),
        out_shape=[jax.ShapeDtypeStruct(shape, v.dtype) for shape, v in zip(shapes, values)],
        in_specs=[pl.BlockSpec(memory_space=pltpu.VMEM)] * len(values),
        out_specs=[pl.BlockSpec(memory_space=pl.ANY)] * len(values),
        scratch_shapes=[
            pltpu.SemaphoreType.DMA((lanes, 6, shards)),
            pltpu.SemaphoreType.DMA((lanes, shards)),
            pltpu.SemaphoreType.DMA((len(values),)),
            pltpu.SemaphoreType.DMA((len(spread) + 1, 2, shards)),
        ],
        compiler_params=pltpu.CompilerParams(collective_id=ident, has_side_effects=True),
        cost_estimate=wire_cost(shards, values[:count]),
        name="gather_%d" % ident,
    )(*values)
    return list(results) + dealt


def scatter_kernel(shards, widths, *refs):
    long_len, short_len = grid_of(shards)
    count = len(widths)
    full = refs[:count]
    out = refs[count : 2 * count]
    held, core_in, short_in, long_in, load_sem, core_sem, short_sem, long_sem, done_sem = refs[
        2 * count :
    ]
    me, at_long, at_short, core = neighbours(shards)
    partner = {"fsdp": me + 1 - 2 * core}
    firsts = [sum(widths[:k]) for k in range(count)]

    def index(line, short):
        return line * short_len + short

    def block(k, line, short, side):
        return full[k].at[:, index(line, short) * 2 + side]

    def columns(ref, k):
        return ref.at[:, :, pl.ds(firsts[k], widths[k])]

    order = []
    for far in range(long_len - 1, 0, -1):
        for sign in (-1, 1):
            line = at_long + sign * far
            order.append(((line >= 0) & (line < long_len), line, far, sign))
    order.append((me >= 0, at_long, 0, 0))
    shorts = []
    for far in range(short_len - 1, 0, -1):
        for sign in (-1, 1):
            short = at_short + sign * far
            shorts.append(((short >= 0) & (short < short_len), short, far, sign))
    shorts.append((me >= 0, at_short, 0, 0))

    def to_core(k, line, short):
        return pltpu.make_async_remote_copy(
            src_ref=block(k, line, short, 1 - core),
            dst_ref=columns(core_in.at[index(line, short)], k),
            send_sem=core_sem.at[0, k, index(line, short)],
            recv_sem=core_sem.at[1, k, index(line, short)],
            device_id=partner,
        )

    def load(k, line, short):
        return pltpu.make_async_copy(
            block(k, line, short, core),
            columns(held.at[index(line, short)], k),
            load_sem.at[k, index(line, short)],
        )

    def along_short(line, short, sign):
        return pltpu.make_async_remote_copy(
            src_ref=held.at[index(line, short)],
            dst_ref=short_in.at[(1 - sign) // 2, index(line, short)],
            send_sem=short_sem.at[0, index(line, short)],
            recv_sem=short_sem.at[1 + (1 - sign) // 2, index(line, short)],
            device_id={"fsdp": me + 2 * sign},
        )

    def along_long(line, sign):
        return pltpu.make_async_remote_copy(
            src_ref=held.at[index(line, at_short)],
            dst_ref=long_in.at[(1 - sign) // 2, line],
            send_sem=long_sem.at[0, line],
            recv_sem=long_sem.at[1 + (1 - sign) // 2, line],
            device_id={"fsdp": me + 2 * short_len * sign},
        )

    def add(to_ref, from_ref):
        batch, rows, _ = to_ref.shape
        step = 16

        @pl.loop(0, batch * rows // step)
        def _(at):
            one = at // (rows // step)
            where = pl.ds(pl.multiple_of((at % (rows // step)) * step, step), step)
            to_ref[one, where, :] = (
                to_ref[one, where, :].astype(jnp.float32)
                + from_ref[one, where, :].astype(jnp.float32)
            ).astype(jnp.bfloat16)

    for near, short, far, sign in shorts:
        for has, line, _, _ in order:
            @pl.when(near & has)
            def _():
                for k in range(count):
                    load(k, line, short).start()

    greet(shards, False)
    for near, short, far, sign in shorts:
        for has, line, _, _ in order:
            @pl.when(near & has)
            def _():
                for k in range(count):
                    to_core(k, line, short).start()

    for near, short, far, sign in shorts:
        for has, line, far_line, sign_line in order:
            @pl.when(near & has)
            def _():
                at = index(line, short)
                for k in range(count):
                    load(k, line, short).wait()
                    to_core(k, line, short).wait_recv()
                add(held.at[at], core_in.at[at])
                if far:
                    behind = at_short - sign

                    @pl.when((behind >= 0) & (behind < short_len))
                    def _():
                        along_short(line, short, sign).wait_recv()
                        add(held.at[at], short_in.at[(1 - sign) // 2, at])

                    along_short(line, short, sign).start()
                else:
                    for way in (-1, 1):
                        behind = at_short - way

                        @pl.when((behind >= 0) & (behind < short_len))
                        def _():
                            along_short(line, short, way).wait_recv()
                            add(held.at[at], short_in.at[(1 - way) // 2, at])

                    for way in (-1, 1) if not far_line else (sign_line,):
                        behind = at_long - way

                        @pl.when((behind >= 0) & (behind < long_len))
                        def _():
                            along_long(line, way).wait_recv()
                            add(held.at[at], long_in.at[(1 - way) // 2, line])

                    if far_line:
                        along_long(line, sign_line).start()

    results = [
        pltpu.make_async_copy(columns(held.at[index(at_long, at_short)], k), out[k], done_sem.at[k])
        for k in range(count)
    ]
    for each in results:
        each.start()
    for near, short, far, sign in shorts:
        for has, line, far_line, sign_line in order:
            @pl.when(near & has)
            def _():
                for k in range(count):
                    to_core(k, line, short).wait_send()
                if far:
                    along_short(line, short, sign).wait_send()
                elif far_line:
                    along_long(line, sign_line).wait_send()
    for each in results:
        each.wait()


def scatter_sum(shards, ident, *values):
    batch, _, rows, _ = values[0].shape
    widths = tuple(v.shape[3] for v in values)
    if shards > 16:
        return [
            sum_rows(v.reshape(batch, shards * rows, w)) for v, w in zip(values, widths)
        ]
    count = len(values)
    long_len, short_len = grid_of(shards)
    pairs = shards // 2
    block = (batch, rows, sum(widths))
    return pl.pallas_call(
        functools.partial(scatter_kernel, shards, widths),
        out_shape=[jax.ShapeDtypeStruct((batch, rows, w), jnp.bfloat16) for w in widths],
        in_specs=[pl.BlockSpec(memory_space=pl.ANY)] * count,
        out_specs=[pl.BlockSpec(memory_space=pl.ANY)] * count,
        scratch_shapes=[
            pltpu.VMEM((pairs,) + block, jnp.bfloat16),
            pltpu.VMEM((pairs,) + block, jnp.bfloat16),
            pltpu.VMEM((2, pairs) + block, jnp.bfloat16),
            pltpu.VMEM((2, long_len) + block, jnp.bfloat16),
            pltpu.SemaphoreType.DMA((count, pairs)),
            pltpu.SemaphoreType.DMA((2, count, pairs)),
            pltpu.SemaphoreType.DMA((3, pairs)),
            pltpu.SemaphoreType.DMA((3, long_len)),
            pltpu.SemaphoreType.DMA((count,)),
        ],
        compiler_params=pltpu.CompilerParams(
            collective_id=ident, has_side_effects=True, vmem_limit_bytes=60 << 20
        ),
        cost_estimate=wire_cost(1, values),
        name="scatter_%d" % ident,
    )(*values)


def product_kernel(shards, gate, up, weight, out, *scratch):
    planes, pair, core_in, short_in, long_in = scratch[:5]
    plane_sem, core_sem, short_sem, long_sem, done_sem = scratch[5:]
    long_len, _ = grid_of(shards)
    me, at_long, at_short, core = neighbours(shards)
    rows = pair.shape[3]
    load = pltpu.make_async_copy(weight.at[pl.ds(0, 2)], planes, plane_sem)
    load.start()

    lines = []
    first, last = me * 0, me * 0 + long_len - 1
    for _ in range(long_len - 1):
        up_side = (last - at_long >= at_long - first).astype(jnp.int32)
        lines.append((first + up_side * (last - first), 2 * up_side - 1))
        first, last = first + 1 - up_side, last - up_side
    lines.append((at_long, None))
    steps = [(line, sign, 1 - at_short) for line, sign in lines]
    steps += [(line, sign, at_short) for line, sign in lines]

    def held(at):
        return pair.at[at, :, core]

    def compute(at):
        where = pl.ds(pl.multiple_of(at * 2 * rows, 2 * rows), 2 * rows)
        left = gate[:, where, :].reshape(4 * rows, gate.shape[2])
        right = up[:, where, :].reshape(4 * rows, up.shape[2])

        @pl.loop(0, pair.shape[4] // 512)
        def _(tile):
            columns = pl.ds(pl.multiple_of(tile * 512, 512), 512)
            sums = jnp.dot(left, planes[0, :, columns], preferred_element_type=jnp.float32)
            sums += jnp.dot(right, planes[1, :, columns], preferred_element_type=jnp.float32)
            pair[at, :, :, :, columns] = sums.astype(jnp.bfloat16).reshape(2, 2, rows, 512)

    def to_core(at):
        return pltpu.make_async_remote_copy(
            src_ref=pair.at[at, :, 1 - core],
            dst_ref=core_in.at[at],
            send_sem=core_sem.at[0, at],
            recv_sem=core_sem.at[1, at],
            device_id={"fsdp": me + 1 - 2 * core},
        )

    def along_short(line, short):
        return pltpu.make_async_remote_copy(
            src_ref=held(line * 2 + short),
            dst_ref=short_in.at[line],
            send_sem=short_sem.at[0, line],
            recv_sem=short_sem.at[1, line],
            device_id={"fsdp": me + 2 - 4 * at_short},
        )

    def along_long(line, sign):
        return pltpu.make_async_remote_copy(
            src_ref=held(line * 2 + at_short),
            dst_ref=long_in.at[(1 - sign) // 2, line],
            send_sem=long_sem.at[0, line],
            recv_sem=long_sem.at[1 + (1 - sign) // 2, line],
            device_id={"fsdp": me + 4 * sign},
        )

    def add(at, other):
        @pl.loop(0, 2 * rows // 16)
        def _(group):
            one = group // (rows // 16)
            where = pl.ds(pl.multiple_of((group % (rows // 16)) * 16, 16), 16)
            pair[at, one, core, where, :] = (
                pair[at, one, core, where, :].astype(jnp.float32)
                + other[one, where, :].astype(jnp.float32)
            ).astype(jnp.bfloat16)

    def from_behind(at, line, sign):
        behind = at_long - sign

        @pl.when((behind >= 0) & (behind < long_len))
        def _():
            along_long(line, sign).wait_recv()
            add(at, long_in.at[(1 - sign) // 2, line])

    def settle(at_step):
        line, sign, short = steps[at_step]
        at = line * 2 + short
        to_core(at).wait_recv()
        add(at, core_in.at[at])
        if at_step < long_len:
            along_short(line, short).start()
            return
        along_short(line, short).wait_recv()
        add(at, short_in.at[line])
        if sign is None:
            from_behind(at, line, 1)
            from_behind(at, line, -1)
        else:
            from_behind(at, line, sign)
            along_long(line, sign).start()

    greet(shards, False)
    load.wait()
    for at_step, (line, _, short) in enumerate(steps):
        compute(line * 2 + short)
        to_core(line * 2 + short).start()
        if at_step:
            settle(at_step - 1)
    settle(len(steps) - 1)
    result = pltpu.make_async_copy(held(at_long * 2 + at_short), out, done_sem)
    result.start()
    for at_step, (line, sign, short) in enumerate(steps):
        to_core(line * 2 + short).wait_send()
        if at_step < long_len:
            along_short(line, short).wait_send()
        elif sign is not None:
            along_long(line, sign).wait_send()
    result.wait()


def product_sum(shards, ident, gate, up, weight):
    batch, every, units = gate.shape
    columns = weight.shape[2]
    rows = every // shards
    long_len, short_len = grid_of(shards)
    block = (batch, rows, columns)
    pairs = shards // 2
    return pl.pallas_call(
        functools.partial(product_kernel, shards),
        out_shape=jax.ShapeDtypeStruct(block, jnp.bfloat16),
        in_specs=[
            pl.BlockSpec(memory_space=pltpu.VMEM),
            pl.BlockSpec(memory_space=pltpu.VMEM),
            pl.BlockSpec(memory_space=pl.ANY),
        ],
        out_specs=pl.BlockSpec(memory_space=pl.ANY),
        scratch_shapes=[
            pltpu.VMEM((2, units, columns), jnp.bfloat16),
            pltpu.VMEM((pairs, batch, 2, rows, columns), jnp.bfloat16),
            pltpu.VMEM((pairs,) + block, jnp.bfloat16),
            pltpu.VMEM((long_len,) + block, jnp.bfloat16),
            pltpu.VMEM((2, long_len) + block, jnp.bfloat16),
            pltpu.SemaphoreType.DMA,
            pltpu.SemaphoreType.DMA((2, pairs)),
            pltpu.SemaphoreType.DMA((2, long_len)),
            pltpu.SemaphoreType.DMA((3, long_len)),
            pltpu.SemaphoreType.DMA,
        ],
        compiler_params=pltpu.CompilerParams(
            collective_id=ident, has_side_effects=True, vmem_limit_bytes=60 << 20
        ),
        cost_estimate=wire_cost(shards, [jax.ShapeDtypeStruct(block, jnp.bfloat16)]),
        name="product_%d" % ident,
    )(gate, up, weight)


def local(
    tokens, segment_ids, norm_gains, attn_weight, adapter, ffn_weight, ffn_adapter, cotangent
):
    micro, local_len, model_dim = tokens.shape
    shards = lax.axis_size("fsdp")
    me = lax.axis_index("fsdp")
    seq_len = local_len * shards
    offset = me * local_len
    count = micro * local_len
    every = micro * seq_len
    q_width = HEADS * HD
    kv_end = q_width + 2 * HD
    score_scale = HD ** (-0.5)
    hidden_cols = ffn_weight.shape[0]
    attn_rows = attn_weight.shape[0]

    seg_cols = count // attn_rows
    seg_block = low(segment_ids).reshape(attn_rows, seg_cols)
    spare = jnp.zeros((attn_rows, 128 - 2 - seg_cols), jnp.bfloat16)
    small = jnp.concatenate([norm_gains, seg_block, spare], axis=1)
    same = kv_end + 4 * RANK
    attn_all, adapter_all, small_all = gather_all(
        shards, 1, attn_weight[None], adapter[None], small[None], shared=same
    )
    cotangent_now, small_all = lax.optimization_barrier((cotangent, small_all))
    cot_all = gather_rows(cotangent_now).reshape(every, model_dim)
    attn_all = attn_all.reshape(model_dim, attn_weight.shape[1])
    adapter_all = adapter_all.reshape(model_dim, 3 * RANK)
    small_all = small_all.reshape(model_dim, 128)
    w_proj = attn_all[:, :kv_end]
    w_out = attn_all[:, kv_end:]
    a_q, bq_t, bd_t = (adapter_all[:, j * RANK : (j + 1) * RANK] for j in range(3))
    gain_two = small_all[:, :2].astype(jnp.float32)
    seg_all = small_all[:, 2 : 2 + seg_cols].reshape(shards, micro, local_len)
    seg_all = seg_all.transpose(1, 0, 2).reshape(micro, seq_len).astype(jnp.int32)

    hidden_in = tokens.reshape(count, model_dim).astype(jnp.float32)
    key_index = jnp.arange(seq_len, dtype=jnp.int32)
    query_index = offset + jnp.arange(local_len, dtype=jnp.int32)
    before = jnp.sum(
        (seg_all[:, None, :] < segment_ids[:, :, None]).astype(jnp.int32), axis=2
    )
    angles = angles_of(query_index[None, :] - before).reshape(count, HD // 2)
    normed, norm_back_one = jax.vjp(rms_scale, hidden_in, gain_two[:, 0])
    normed_low = low(normed)
    projected = contract(normed_low, w_proj, 1, 0)
    query_low = low(contract(normed_low, a_q, 1, 0))
    query_pre = projected[:, :q_width] + contract(query_low, bq_t, 1, 1)
    queries = low(rotate(query_pre.reshape(count, HEADS, HD), angles[:, None, :]))
    queries = queries.reshape(micro, local_len * HEADS, HD)
    keys_low = low(rotate(projected[:, q_width : q_width + HD], angles))
    values_low = low(projected[:, q_width + HD :])
    keys_all, values_all = (
        each.reshape(micro, seq_len, -1)
        for each in gather_all(
            shards,
            2,
            keys_low.reshape(micro, local_len, HD),
            values_low.reshape(micro, local_len, HD),
        )
    )
    allowed = (
        (segment_ids[:, :, None] == seg_all[:, None, :])
        & (key_index[None, None, :] <= query_index[None, :, None])
    )[:, :, None, :]
    scores = (batched(queries, keys_all, 2, 2) * score_scale).reshape(
        micro, local_len, HEADS, seq_len
    )
    scores = jnp.where(allowed, scores, -1e30)
    top_score = jnp.max(scores, axis=-1, keepdims=True)
    exp_scores = jnp.exp(scores - top_score)
    weights = exp_scores / jnp.sum(exp_scores, axis=-1, keepdims=True)
    weights_low = low(weights).reshape(micro, local_len * HEADS, seq_len)
    context = low(batched(weights_low, values_all, 2, 1)).reshape(count, q_width)
    mixed_sum = hidden_in + contract(context, w_out, 1, 1)
    normed_two, norm_back_two = jax.vjp(rms_scale, mixed_sum, gain_two[:, 1])
    (inputs_all,) = gather_all(shards, 3, low(normed_two).reshape(micro, local_len, model_dim))
    inputs_all = inputs_all.reshape(every, model_dim)
    kept, inputs_all = lax.optimization_barrier(
        (jnp.concatenate([context, query_low], axis=1), inputs_all)
    )
    kept_all = gather_rows(kept.reshape(micro, local_len, q_width + RANK))
    kept_all = kept_all.reshape(every, q_width + RANK)
    low_grad_all = low(contract(cot_all, bd_t, 1, 0))

    step = hidden_cols // CHUNKS
    hidden_parts, gate_parts, up_parts = [], [], []
    for at in range(CHUNKS):
        units = slice(at * step, (at + 1) * step)
        w_gate, w_up, w_down = (ffn_weight[units, j, :] for j in range(3))
        gate_pre = contract(inputs_all, w_gate, 1, 1)
        up_pre = contract(inputs_all, w_up, 1, 1)
        activated, gelu_back = jax.vjp(gelu_tanh, gate_pre)
        hidden_act = low(activated * up_pre)
        hidden_grad = contract(cot_all, w_down, 1, 1) + contract(
            low_grad_all, ffn_adapter[units], 1, 1
        )
        gate_grad = low(gelu_back(hidden_grad * up_pre)[0])
        up_grad = low(hidden_grad * activated)
        hidden_parts.append(hidden_act)
        gate_parts.append(gate_grad)
        up_parts.append(up_grad)

    gate_grad = jnp.concatenate(gate_parts, axis=1)
    up_grad = jnp.concatenate(up_parts, axis=1)
    hidden_act = jnp.concatenate(hidden_parts, axis=1)
    step = hidden_cols // PIECES

    def weight_grads(at, gate_now, up_now, hidden_now):
        units = slice(at * step, (at + 1) * step)
        made = []
        for left, right in (
            (gate_now, inputs_all),
            (up_now, inputs_all),
            (hidden_now, cot_all),
        ):
            mine = low(contract(left[:, units], right, 0, 0))
            made.append((mine, swap_rep(mine)))
        return made

    ffn_parts = weight_grads(0, gate_grad, up_grad, hidden_act)
    down_part = low(contract(hidden_act, ffn_weight[:, 2, :], 1, 0))
    low_part = low(contract(hidden_act, ffn_adapter, 1, 0))
    gate_grad, up_grad, kept_all, down_part, low_part, _ = lax.optimization_barrier(
        (gate_grad, up_grad, kept_all, down_part, low_part, [pair[0] for pair in ffn_parts])
    )
    if grid_of(shards)[1] == 2 and micro == 2:
        normed_two_grad = product_sum(
            shards,
            5,
            gate_grad.reshape(micro, seq_len, hidden_cols),
            up_grad.reshape(micro, seq_len, hidden_cols),
            ffn_weight.transpose(1, 0, 2),
        )
    else:
        (normed_two_grad,) = scatter_sum(
            shards,
            5,
            low(
                contract(gate_grad, ffn_weight[:, 0, :], 1, 0)
                + contract(up_grad, ffn_weight[:, 1, :], 1, 0)
            ).reshape(micro, shards, local_len, model_dim),
        )
    normed_two_grad, down_part, gate_grad, up_grad, hidden_act, _ = lax.optimization_barrier(
        (
            normed_two_grad,
            down_part,
            gate_grad,
            up_grad,
            hidden_act,
            [pair[1] for pair in ffn_parts[:2]],
        )
    )
    down_sum = sum_rows(down_part.reshape(micro, seq_len, model_dim))
    ffn_parts += weight_grads(1, gate_grad, up_grad, hidden_act)
    low_mine = low(contract(hidden_act, low_grad_all, 0, 0))
    low_other = swap_rep(low_mine)
    normed_two_grad, low_part, low_mine, _ = lax.optimization_barrier(
        (normed_two_grad, low_part, low_mine, [pair[0] for pair in ffn_parts])
    )
    normed_two_grad = normed_two_grad.reshape(count, model_dim).astype(jnp.float32)
    cot_full = cotangent.reshape(count, model_dim).astype(jnp.float32)
    mixed_part, gain_two_grad = norm_back_two(normed_two_grad)
    mixed_grad = cot_full + mixed_part
    out_grad_low = low(mixed_grad)
    context_grad = contract(out_grad_low, w_out, 1, 0)
    context_rows = low(context_grad).reshape(micro, local_len * HEADS, HD)
    prob_grad = batched(context_rows, values_all, 2, 2).reshape(micro, local_len, HEADS, seq_len)
    score_grad = weights * (prob_grad - jnp.sum(weights * prob_grad, axis=-1, keepdims=True))
    score_grad = low(score_grad).reshape(micro, local_len * HEADS, seq_len)
    query_grad = batched(score_grad, keys_all, 2, 1) * score_scale
    query_grad = query_grad.reshape(count, HEADS, HD)
    query_pre_grad = low(rotate(query_grad, -angles[:, None, :]).reshape(count, q_width))
    key_part = low(batched(score_grad, queries, 1, 1) * score_scale)
    value_part = low(batched(weights_low, context_rows, 1, 1))
    key_part, value_part, query_pre_grad, ffn_parts[2:3] = lax.optimization_barrier(
        (key_part, value_part, query_pre_grad, ffn_parts[2:3])
    )
    q_all = gather_rows(query_pre_grad.reshape(micro, local_len, q_width))
    q_all = q_all.reshape(every, q_width)
    key_sum, value_sum, down_low = (
        each.reshape(count, -1)
        for each in scatter_sum(
            shards,
            6,
            *(
                each.reshape(micro, shards, local_len, -1)
                for each in (key_part, value_part, low_part)
            ),
        )
    )
    result = (
        mixed_sum
        + down_sum.reshape(count, model_dim).astype(jnp.float32)
        + contract(down_low, bd_t, 1, 1)
    )
    key_grad = low(rotate(key_sum.astype(jnp.float32), -angles))
    value_grad = value_sum
    rank_grad = low(contract(query_pre_grad, bq_t, 1, 0))
    proj_grad = jnp.concatenate([query_pre_grad, key_grad, value_grad], axis=1)
    normed_grad = contract(proj_grad, w_proj, 1, 1) + contract(rank_grad, a_q, 1, 1)
    hidden_part, gain_one_grad = norm_back_one(normed_grad)
    input_grad = low(mixed_grad + hidden_part)

    narrow = jnp.concatenate([key_grad, value_grad, rank_grad, down_low], axis=1)
    ffn_grad = place(None, 0, PIECES, ffn_parts[:3])
    narrow, ffn_grad, ffn_parts[3:4] = lax.optimization_barrier(
        (narrow, ffn_grad, ffn_parts[3:4])
    )
    gain_parts = jnp.zeros((1, 16, model_dim), jnp.bfloat16)
    gain_parts = gain_parts.at[0, 0].set(low(gain_one_grad)).at[0, 1].set(low(gain_two_grad))
    narrow_all, normed_cols, out_cols, gain_cols = gather_all(
        shards,
        4,
        narrow.reshape(micro, local_len, 2 * HD + 2 * RANK),
        spread=(
            normed_low.reshape(micro, local_len, model_dim),
            out_grad_low.reshape(micro, local_len, model_dim),
            gain_parts,
        ),
    )
    narrow_all = narrow_all.reshape(every, 2 * HD + 2 * RANK)
    normed_cols = normed_cols.reshape(every, attn_rows)
    wout_grad = contract(out_cols.reshape(every, attn_rows), kept_all[:, :q_width], 0, 0)
    gain_now = jnp.sum(gain_cols[0, :, :2].astype(jnp.float32), axis=0)
    my_cols = me * attn_rows
    attn_q = low(contract(normed_cols, q_all, 0, 0))
    attn_rest = contract(normed_cols, narrow_all[:, : 2 * HD + RANK], 0, 0)
    bq_grad = contract(
        lax.dynamic_slice_in_dim(q_all, my_cols, attn_rows, 1), kept_all[:, q_width:], 0, 0
    )
    bd_grad = contract(
        lax.dynamic_slice_in_dim(cot_all, my_cols, attn_rows, 1),
        narrow_all[:, 2 * HD + RANK :],
        0,
        0,
    )
    tail = low(jnp.concatenate([attn_rest, bq_grad, bd_grad], axis=1))
    tail_out = low(wout_grad)
    tail_gain = low(gain_now)
    crossing = [swap_rep(each) for each in (tail_out, tail, attn_q)]
    attn_q, tail, tail_out, ffn_parts[3:], low_mine, low_other = lax.optimization_barrier(
        (attn_q, tail, tail_out, ffn_parts[3:], low_mine, low_other)
    )
    gains_grad = total(tail_gain, swap_rep(tail_gain)).transpose(1, 0)
    ffn_grad = place(ffn_grad, 1, PIECES, ffn_parts[3:])
    ffn_grad = ffn_grad.transpose(1, 0, 2)
    ffn_low_grad = total(low_mine, low_other)
    tail = total(tail, crossing[1])
    attn_grad = unwritten(attn_weight.shape, jnp.float32)
    for first, part in (
        (kv_end, total(tail_out, crossing[0])),
        (q_width, tail[:, : 2 * HD]),
        (0, total(attn_q, crossing[2])),
    ):
        attn_grad = lax.dynamic_update_slice(attn_grad, part, (0, first))
    adapter_grad = tail[:, 2 * HD :]
    return (
        low(result).reshape(micro, local_len, model_dim),
        input_grad.reshape(micro, local_len, model_dim),
        gains_grad,
        attn_grad,
        adapter_grad,
        ffn_grad,
        ffn_low_grad,
    )


def solution(mesh):
    placed = (
        P("rep", "fsdp", None),
        P("rep", "fsdp"),
        P("fsdp", None),
        P("fsdp", None),
        P("fsdp", None),
        P("fsdp", None, None),
        P("fsdp", None),
        P("rep", "fsdp", None),
    )
    return jax.shard_map(
        local,
        mesh=mesh,
        in_specs=placed,
        out_specs=(
            P("rep", "fsdp", None),
            P("rep", "fsdp", None),
            P("fsdp", None),
            P("fsdp", None),
            P("fsdp", None),
            P("fsdp", None, None),
            P("fsdp", None),
        ),
        check_vma=False,
    )
```
